32 devices in a mesh: tok: 16 (over z, y, core), tp: 2 (over x).
Axes of the slice: x: 2, y: 2, z: 4, core: 2. Of those that a mesh axis runs over, the one named last changes fastest.
Arguments:
- hidden_in: bfloat16 [4096, 4096], P('tok', 'tp'), may hold values from -6 to 6
- norm_gain: float32 [4096], replicated, may hold values from 0.5 to 9, as said below
- w_query: bfloat16 [4096, 4096], P(None, 'tp'), may hold values from -0.09375 to 0.09375
- w_key: bfloat16 [4096, 1024], P(None, 'tp'), may hold values from -0.09375 to 0.09375
- w_value: bfloat16 [4096, 1024], P(None, 'tp'), may hold values from -0.09375 to 0.09375
- w_out: bfloat16 [4096, 4096], P('tp'), may hold values from -0.5 to 0.5
- doc_ids: int32 [4096], replicated, may hold values from 0 to 3, never falling along the last dimension, each value on 1 to 3072 neighbouring positions
Outputs:
- hidden_out: bfloat16 [4096, 4096], P('tok', 'tp')
- joint_cov: float32 [2, 4096, 2, 4096], P(None, 'tok', None, 'tp')
The draws below stay inside these ranges and needn't reach their ends.
Inputs may be any that keep to these rules, and one draw needn't show every extreme that they name: `norm_gain`: each channel's gain is positive. `doc_ids`: document numbers never fall along the tokens; a document holds 1 to 3072 tokens.
All inputs are finite; a program needn't handle non-finite values.
Results may differ from the reference program's by a relative error of at most 0.013.
The reference program's roundings to bfloat16 on the way count: a program that leaves them out, or rounds other values in their place, can miss the bound.
Values may be sent and summed in bfloat16 or wider, within the bound.
A program may use at most 192 MiB of HBM per device.

```python
import math
import jax
import jax.numpy as jnp
import numpy as np
from jax import lax

D = 4096
HEADS = 32
KV_HEADS = 8
HS = 128
TOKENS = 4096
SEQ = 4096


def draw_norm_gain(key, part):
    return jnp.exp(jax.random.uniform(key, (D,), jnp.float32, jnp.log(0.5), jnp.log(2.0)))


def levels(key, extent, pieces, least, top_value):
    gain, own = 1.0, jax.random.fold_in(key, 6)
    for dim, blocks in pieces:
        heights = jnp.exp(jax.random.uniform(jax.random.fold_in(own, dim), (blocks,), jnp.float32, least / len(pieces), top_value / len(pieces)))
        gain = gain * jnp.repeat(heights, extent[dim] // blocks).reshape([-1 if axis == dim else 1 for axis in range(len(extent))])
    return gain


def length_profile(count, total, limit, lean):
    portions = [(1 << 20) // math.isqrt(grade ** lean) + 1 for grade in range(2, count + 1)]
    spare, given = total - limit - (count - 1), [1] * (count - 1)
    while spare > 0:
        candidates = [i for i in range(count - 1) if given[i] < limit]
        mass, budget = sum([portions[i] for i in candidates]), spare
        for i in candidates:
            addition = min(limit - given[i], max(1, budget * portions[i] // mass), spare)
            given[i] = given[i] + addition
            spare = spare - addition
    return np.array([limit] + given)


def uneven_parts(rng, count, total, bound, skew):
    if count == 2:
        one = jax.random.randint(rng, (), max(1, total - bound), min(bound, total - 1) + 1)
        return jnp.stack([one, total - one])
    lengths = jnp.asarray(length_profile(count, total, bound, skew), jnp.int32)
    pairs = (count - 1) // 2
    source_of, taker = lengths[1:1 + 2 * pairs:2], lengths[2:2 + 2 * pairs:2]
    margin = jnp.minimum(source_of - 1, bound - taker)
    moved = jax.random.randint(jax.random.fold_in(rng, 1), (pairs,), 0, 1 << 20) % (margin + 1)
    lengths = lengths.at[1:1 + 2 * pairs:2].set(source_of - moved).at[2:2 + 2 * pairs:2].set(taker + moved)
    return lengths[jax.random.permutation(jax.random.fold_in(rng, 2), count)]


def scatter_about(rng, extent, width, bound, shards=(), held_as=jnp.bfloat16):
    array = width * jax.random.normal(rng, extent, jnp.float32)
    if shards:
        array = array * levels(rng, extent, shards, -0.22, 0.18)
    return jnp.clip(array, -bound, bound).astype(held_as)


def setup_inputs(seed: int = 0) -> dict:
    key_list = jax.random.split(jax.random.key(seed), 8)
    return {
        "hidden_in": scatter_about(key_list[0], (TOKENS, D), 1.0, 6.0, ((0, 16), (1, 2))),
        "norm_gain": draw_norm_gain(jax.random.fold_in(key_list[7], 71), 0),
        "w_query": scatter_about(key_list[2], (D, HEADS * HS), D ** -0.5, 0.09375, ((1, 2),)),
        "w_key": scatter_about(key_list[3], (D, KV_HEADS * HS), D ** -0.5, 0.09375, ((1, 2),)),
        "w_value": scatter_about(key_list[4], (D, KV_HEADS * HS), D ** -0.5, 0.09375, ((1, 2),)),
        "w_out": scatter_about(key_list[5], (HEADS * HS, D), HS ** -0.5, 0.5, ((0, 2),)),
        "doc_ids": jnp.searchsorted(jnp.cumsum(uneven_parts(key_list[6], 4, TOKENS, 3 * SEQ // 4, 2)), jnp.arange(TOKENS), side="right").astype(jnp.int32),
    }


epsilon = 1e-05
rope_base = 500000.0

def rotate(vectors, positions):
    half_dim = vectors.shape[-1] // 2
    inv_freq = rope_base ** (-(jnp.arange(half_dim, dtype=jnp.float32) * 2.0) / vectors.shape[-1])
    angles = positions.astype(jnp.float32)[:, None] * inv_freq[None, :]
    cosine = jnp.cos(angles)[:, None, :]
    sine_part = jnp.sin(angles)[:, None, :]
    first_half = vectors[..., :half_dim]
    second_half = vectors[..., half_dim:]
    return jnp.concatenate([first_half * cosine - second_half * sine_part, second_half * cosine + first_half * sine_part], axis=-1)

def reference(hidden_in, norm_gain, w_query, w_key, w_value, w_out, doc_ids):
    widened = hidden_in.astype(jnp.float32)
    factor = lax.rsqrt(lax.optimization_barrier(jnp.mean(widened * widened, axis=1, keepdims=True)) + epsilon)
    normed = (widened * factor * norm_gain[None, :]).astype(jnp.bfloat16)
    groups = HEADS // KV_HEADS
    positions = jnp.arange(TOKENS, dtype=jnp.int32)
    queries = rotate(jnp.dot(normed, w_query, preferred_element_type=jnp.float32).reshape(TOKENS, HEADS, HS), positions % SEQ)
    queries = queries.astype(jnp.bfloat16).reshape(TOKENS, KV_HEADS, groups, HS)
    key_rows = rotate(jnp.dot(normed, w_key, preferred_element_type=jnp.float32).reshape(TOKENS, KV_HEADS, HS), positions % SEQ).astype(jnp.bfloat16)
    value_rows = jnp.dot(normed, w_value, preferred_element_type=jnp.float32).astype(jnp.bfloat16).reshape(TOKENS, KV_HEADS, HS)
    block_size = SEQ // 16
    key_wide = key_rows.astype(jnp.float32)
    value_wide = value_rows.astype(jnp.float32)

    def attend(number):
        anchor = (number * block_size).astype(jnp.int32)
        seq_anchor = (anchor // SEQ * SEQ).astype(jnp.int32)
        query_part = lax.dynamic_slice_in_dim(queries, anchor, block_size, 0).astype(jnp.float32)
        query_pos = anchor + jnp.arange(block_size, dtype=jnp.int32)
        query_doc = lax.dynamic_slice_in_dim(doc_ids, anchor, block_size, 0)
        key_pos = seq_anchor + jnp.arange(SEQ, dtype=jnp.int32)
        key_doc = lax.dynamic_slice_in_dim(doc_ids, seq_anchor, SEQ, 0)
        key_part = lax.dynamic_slice_in_dim(key_wide, seq_anchor, SEQ, 0)
        value_part = lax.dynamic_slice_in_dim(value_wide, seq_anchor, SEQ, 0)
        allowed = (query_doc[:, None] == key_doc[None, :]) & (key_pos[None, :] <= query_pos[:, None])
        scores = jnp.einsum('qhgd,khd->hgqk', query_part, key_part) * HS ** (-0.5)
        scores = jnp.where(allowed[None, None], scores, -jnp.inf)
        row_max = lax.optimization_barrier(jnp.max(scores, axis=-1, keepdims=True))
        weights = jnp.exp(scores - row_max)
        weight_sum = lax.optimization_barrier(jnp.sum(weights, axis=-1, keepdims=True))
        rounded = lax.optimization_barrier(weights.astype(jnp.bfloat16)).astype(jnp.float32)
        blended = jnp.einsum('hgqk,khd->hgqd', rounded, value_part) / weight_sum
        return jnp.transpose(blended, (2, 0, 1, 3)).astype(jnp.bfloat16)
    attended = lax.map(attend, jnp.arange(TOKENS // block_size, dtype=jnp.int32)).reshape(TOKENS, HEADS * HS)
    layer_sum = jnp.dot(attended, w_out, preferred_element_type=jnp.float32)
    hidden_out = (widened + layer_sum).astype(jnp.bfloat16)
    joint_rows = jnp.stack([hidden_in, hidden_out], axis=1).reshape(TOKENS, 2 * D)
    gram_block = lax.dot_general(joint_rows, joint_rows, (((0,), (0,)), ((), ())), preferred_element_type=jnp.float32)
    means = lax.optimization_barrier(jnp.sum(joint_rows, axis=0, dtype=jnp.float32)) / TOKENS
    joint_cov = (gram_block / TOKENS - means[:, None] * means[None, :]).reshape(2, D, 2, D)
    return (hidden_out, joint_cov)
```

```python
import functools
import math

import jax
import jax.numpy as jnp
from jax import lax
from jax.experimental import pallas as pl
from jax.experimental.pallas import tpu as pltpu
from jax.sharding import PartitionSpec as P

HS = 128
epsilon = 1e-05
rope_base = 500000.0
VMEM_LIMIT = 60 * 1024 * 1024


def rotate(vectors, positions):
    half_dim = vectors.shape[-1] // 2
    inv_freq = rope_base ** (-(jnp.arange(half_dim, dtype=jnp.float32) * 2.0) / vectors.shape[-1])
    angles = positions.astype(jnp.float32)[:, None] * inv_freq[None, :]
    cosine = jnp.cos(angles)[:, None, :]
    sine_part = jnp.sin(angles)[:, None, :]
    first_half = vectors[..., :half_dim]
    second_half = vectors[..., half_dim:]
    return jnp.concatenate(
        [
            first_half * cosine - second_half * sine_part,
            second_half * cosine + first_half * sine_part,
        ],
        axis=-1,
    )


def attend_kernel(groups, block, bounds, q_ref, k_ref, v_ref, lo_ref, out_ref, s_ref, m_ref, l_ref, acc_ref):
    rows = q_ref.shape[0]
    first_row = bounds[0]
    scale = HS ** (-0.5) * math.log2(math.e)
    start = bounds[1] // block
    stop = (first_row + rows + block - 1) // block
    lanes = 128
    m_ref[...] = jnp.full_like(m_ref, -jnp.inf)
    l_ref[...] = jnp.zeros_like(l_ref)
    acc_ref[...] = jnp.zeros_like(acc_ref)

    @pl.loop(start, stop)
    def _(step):
        first_key = pl.multiple_of(step * block, block)
        keys = k_ref[pl.ds(first_key, block), :]
        key_pos = first_key + lax.broadcasted_iota(jnp.int32, (rows, block), 1)
        query_pos = first_row + lax.broadcasted_iota(jnp.int32, (rows, block), 0)
        allowed = (key_pos >= lo_ref[:, :1]) & (key_pos <= query_pos)
        for head in range(groups):
            part = pl.ds(head * rows, rows)
            s = lax.dot_general(
                q_ref[:, head * HS:(head + 1) * HS], keys,
                (((1,), (1,)), ((), ())), preferred_element_type=jnp.float32,
            ) * scale
            s = jnp.where(allowed, s, -jnp.inf)
            s_ref[step, part, :] = s
            top = m_ref[part, :]
            for piece in range(block // lanes):
                top = jnp.maximum(top, s[:, piece * lanes:(piece + 1) * lanes])
            m_ref[part, :] = top

    m_ref[...] = jnp.broadcast_to(jnp.max(m_ref[...], axis=-1, keepdims=True), m_ref.shape)

    @pl.loop(start, stop)
    def _(step):
        first_key = pl.multiple_of(step * block, block)
        values = v_ref[pl.ds(first_key, block), :]
        for head in range(groups):
            part = pl.ds(head * rows, rows)
            weights = jnp.exp2(s_ref[step, part, :] - m_ref[part, :1])
            total = l_ref[part, :]
            for piece in range(block // lanes):
                total = total + weights[:, piece * lanes:(piece + 1) * lanes]
            l_ref[part, :] = total
            acc_ref[part, :] += jnp.dot(
                weights.astype(jnp.bfloat16), values, preferred_element_type=jnp.float32
            )

    for head in range(groups):
        part = pl.ds(head * rows, rows)
        weight_sum = jnp.sum(l_ref[part, :], axis=-1, keepdims=True)
        out_ref[:, head * HS:(head + 1) * HS] = (acc_ref[part, :] / weight_sum).astype(out_ref.dtype)


def attend(queries, kv_rows, lo, bounds, kv_heads):
    rows, width = queries.shape
    all_rows = kv_rows.shape[1]
    groups = width // (kv_heads * HS)
    block = min(512, all_rows)
    wide = groups * HS
    return pl.pallas_call(
        functools.partial(attend_kernel, groups, block),
        out_shape=jax.ShapeDtypeStruct((rows, width), jnp.bfloat16),
        grid_spec=pltpu.PrefetchScalarGridSpec(
            num_scalar_prefetch=1,
            grid=(kv_heads,),
            in_specs=[
                pl.BlockSpec((rows, wide), lambda g, b: (0, g)),
                pl.BlockSpec((None, all_rows, HS), lambda g, b: (0, 0, g)),
                pl.BlockSpec((None, all_rows, HS), lambda g, b: (1, 0, g)),
                pl.BlockSpec((rows, 128), lambda g, b: (0, 0)),
            ],
            out_specs=pl.BlockSpec((rows, wide), lambda g, b: (0, g)),
            scratch_shapes=[
                pltpu.VMEM((all_rows // block, groups * rows, block), jnp.float32),
                pltpu.VMEM((groups * rows, 128), jnp.float32),
                pltpu.VMEM((groups * rows, 128), jnp.float32),
                pltpu.VMEM((groups * rows, HS), jnp.float32),
            ],
        ),
        compiler_params=pltpu.CompilerParams(
            dimension_semantics=("arbitrary",), vmem_limit_bytes=VMEM_LIMIT
        ),
        cost_estimate=pl.CostEstimate(
            flops=4 * rows * all_rows * width,
            bytes_accessed=2 * all_rows * kv_heads * HS * 2 + 4 * rows * width,
            transcendentals=rows * all_rows * width // HS,
        ),
        name="attend",
    )(bounds, queries, kv_rows, kv_rows, lo)


def gram_kernel(strips, rin_ref, rout_ref, low_ref, high_ref, cout_ref, out_ref, rt_ref, mean_ref):
    all_rows, row_width = rin_ref.shape

    @pl.when(pl.program_id(0) == 0)
    def _():
        ones = jnp.ones((all_rows, 128), jnp.bfloat16)
        for source, ref in enumerate((rin_ref, rout_ref)):
            part = pl.ds(source * row_width, row_width)
            rt_ref[part, :] = ref[...].T
            mean_ref[part, :] = (
                jnp.dot(rt_ref[part, :], ones, preferred_element_type=jnp.float32) / all_rows
            )

    ones = jnp.ones((8, all_rows), jnp.bfloat16)

    def block(source, ref):
        cols = ref[...]
        col_mean = jnp.dot(ones, cols, preferred_element_type=jnp.float32)[:1] / all_rows
        gram = jnp.dot(rt_ref[...], cols, preferred_element_type=jnp.float32)
        cov = gram / all_rows - mean_ref[:, :1] * col_mean
        for row_source in range(2):
            out_ref[row_source, :, source, :] = cov[row_source * row_width:(row_source + 1) * row_width]

    @pl.when(pl.program_id(0) < strips)
    def _():
        block(0, low_ref)

    @pl.when(pl.program_id(0) >= strips)
    def _():
        block(0, high_ref)

    block(1, cout_ref)


def joint_gram(rin, rout, cin, cout):
    all_rows, row_width = rin.shape
    half = cout.shape[2]
    col_width = 2 * half
    tile = min(256, half)
    strips = half // tile
    whole = pl.BlockSpec((all_rows, row_width), lambda j: (0, 0), pipeline_mode=pl.Buffered(1))
    strip = pl.BlockSpec((None, all_rows, tile), lambda j: (j // strips, 0, j % strips))
    low = pl.BlockSpec((all_rows, tile), lambda j: (0, jnp.minimum(j, strips - 1)))
    high = pl.BlockSpec((all_rows, tile), lambda j: (0, jnp.maximum(j - strips, 0)))
    return pl.pallas_call(
        functools.partial(gram_kernel, strips),
        out_shape=jax.ShapeDtypeStruct((2, row_width, 2, col_width), jnp.float32),
        grid=(col_width // tile,),
        in_specs=[whole, whole, low, high, strip],
        out_specs=pl.BlockSpec((2, row_width, 2, tile), lambda j: (0, 0, 0, j)),
        scratch_shapes=[
            pltpu.VMEM((2 * row_width, all_rows), jnp.bfloat16),
            pltpu.VMEM((2 * row_width, 128), jnp.float32),
        ],
        compiler_params=pltpu.CompilerParams(
            dimension_semantics=("arbitrary",), vmem_limit_bytes=VMEM_LIMIT
        ),
        cost_estimate=pl.CostEstimate(
            flops=8 * all_rows * row_width * col_width,
            bytes_accessed=4 * all_rows * (row_width + col_width) + 16 * row_width * col_width,
            transcendentals=0,
        ),
        name="joint_gram",
    )(rin, rout, *cin, cout)


def both_sides(block):
    if lax.axis_size("tp") != 2:
        return lax.all_gather(block, "tp", axis=1, tiled=True)
    other = lax.ppermute(block, "tp", ((0, 1), (1, 0)))
    first = lax.axis_index("tp") == 0
    return jnp.concatenate([jnp.where(first, block, other), jnp.where(first, other, block)], axis=1)


def ring_kernel(chips, share, x_ref, *refs):
    if share:
        out_ref, side_ref, send, recv, psend, precv, local, ssend, srecv = refs
    else:
        out_ref, send, recv, psend, precv, local = refs
    mesh_id = pl.DeviceIdType.MESH
    rows = x_ref.shape[1]
    me, tp = lax.axis_index("tok"), lax.axis_index("tp")
    count = 2 * chips
    core, chip = me % 2, me // 2
    depth = chips // 2
    spot = jnp.where(chip % 2 == 0, chip // 2, chips - 1 - chip // 2)

    def device(place):
        place = (place + 2 * chips) % chips
        return jnp.where(place < depth, place * 4, (chips - 1 - place) * 4 + 2) + core

    partner = me + 1 - 2 * core
    ways = (device(spot + 1), device(spot - 1))
    barrier = pltpu.get_barrier_semaphore()
    for peer in (*ways, partner):
        pl.semaphore_signal(barrier, inc=1, device_id={"tok": peer}, device_id_type=mesh_id)
    if share:
        pl.semaphore_signal(barrier, inc=1, device_id={"tp": 1 - tp}, device_id_type=mesh_id)
    pl.semaphore_wait(barrier, 4 if share else 3)

    def block(way, origin):
        return out_ref.at[way, pl.ds(pl.multiple_of(origin * rows, rows), rows), :]

    pending = []

    def step_copies(step, way):
        origin = device(spot - step if way == 0 else spot + step)
        source = x_ref.at[way] if step == 0 else block(way, origin)
        ring = None
        if step < chips - 1:
            ring = pltpu.make_async_remote_copy(
                src_ref=source, dst_ref=block(way, origin), send_sem=send.at[way, step],
                recv_sem=recv.at[way, step], device_id={"tok": ways[way]}, device_id_type=mesh_id,
            )
            ring.start()
        beside = pltpu.make_async_remote_copy(
            src_ref=source, dst_ref=block(way, origin), send_sem=psend.at[way, step],
            recv_sem=precv.at[way, step], device_id={"tok": partner}, device_id_type=mesh_id,
        )
        beside.start()
        pending.append((ring, beside))
        return ring

    rings = [step_copies(0, way) for way in range(2)]
    own = [pltpu.make_async_copy(x_ref.at[way], block(way, me), local.at[way]) for way in range(2)]
    for copy in own:
        copy.start()
    if share:
        width = side_ref.shape[1]
        half = x_ref.shape[2]
        owner = me // (count // 2)
        my_way = me * width % (2 * half) // half
        features = pl.ds(pl.multiple_of(me * width % half, width), width)

    def side_copy(step, way, kind):
        origin = device(spot - step if way == 0 else spot + step)
        origin = origin + kind * (1 - 2 * core)
        source = x_ref.at[way, :, features]
        if step > 0 or kind > 0:
            source = out_ref.at[way, pl.ds(pl.multiple_of(origin * rows, rows), rows), features]
        return pltpu.make_async_remote_copy(
            src_ref=source,
            dst_ref=side_ref.at[pl.ds(pl.multiple_of(origin * rows, rows), rows), :],
            send_sem=ssend.at[kind, step], recv_sem=srecv.at[kind, step],
            device_id={"tp": 1 - tp}, device_id_type=mesh_id,
        )

    def each_side(act, step, way, kind, holder):
        if share:
            @pl.when((my_way == way) & ((owner == tp) == holder))
            def _():
                act(side_copy(step, way, kind))

    def start(copy):
        copy.start()

    for way in range(2):
        each_side(start, 0, way, 0, True)
    for step in range(1, chips):
        for way in range(2):
            rings[way].wait_recv()
            rings[way] = step_copies(step, way)
            each_side(start, step, way, 0, True)
            pending[2 * (step - 1) + way][1].wait_recv()
            each_side(start, step - 1, way, 1, True)
    for way in range(2):
        pending[2 * (chips - 1) + way][1].wait_recv()
        each_side(start, chips - 1, way, 1, True)
    for ring, beside in pending:
        if ring is not None:
            ring.wait_send()
        beside.wait_send()
    for copy in own:
        copy.wait()
    for step in range(chips):
        for way in range(2):
            for kind in range(2):
                each_side(lambda copy: copy.wait_send(), step, way, kind, True)
                each_side(lambda copy: copy.wait_recv(), step, way, kind, False)


def ring_gather(halves, share, call_id):
    _, rows, width = halves.shape
    count = lax.axis_size("tok")
    chips = count // 2
    out_shape = [jax.ShapeDtypeStruct((2, rows * count, width), halves.dtype)]
    dma = pltpu.SemaphoreType.DMA
    scratch = [dma((2, chips))] * 4 + [dma((2,))]
    if share:
        out_shape.append(jax.ShapeDtypeStruct((rows * count, 4 * width // count), halves.dtype))
        scratch += [dma((2, chips))] * 2
    return pl.pallas_call(
        functools.partial(ring_kernel, chips, share),
        out_shape=out_shape,
        in_specs=[pl.BlockSpec(memory_space=pltpu.VMEM)],
        out_specs=[pl.BlockSpec(memory_space=pl.ANY)] * len(out_shape),
        scratch_shapes=scratch,
        compiler_params=pltpu.CompilerParams(
            collective_id=call_id, has_side_effects=True, vmem_limit_bytes=VMEM_LIMIT
        ),
        cost_estimate=pl.CostEstimate(
            flops=40_000_000_000, bytes_accessed=2 * halves.size * count * 2, transcendentals=0
        ),
        name="ring_share" if share else "ring",
    )(halves)


def row_features(columns, arrived):
    _, all_rows, half = columns.shape
    row_width = 2 * half * lax.axis_size("tp") // lax.axis_size("tok")
    first = lax.axis_index("tok") * row_width
    offset, owner = first % (2 * half), first // (2 * half)
    mine = lax.dynamic_slice(columns, (offset // half, 0, offset % half), (1, all_rows, row_width))[0]
    owned = lax.axis_index("tp") == owner
    if arrived is None:
        return lax.psum(jnp.where(owned, mine, jnp.zeros_like(mine)), "tp")
    return jnp.where(owned, mine, arrived)


SUBS = 2
MESH = pl.DeviceIdType.MESH


def ring_place(chips):
    me, tp = lax.axis_index("tok"), lax.axis_index("tp")
    core, chip = me % 2, me // 2
    spot = jnp.where(chip % 2 == 0, chip // 2, chips - 1 - chip // 2)

    def chip_at(place):
        place = (place + 2 * chips) % chips
        return jnp.where(place < chips // 2, place * 2, (chips - 1 - place) * 2 + 1)

    ahead = 1 - 2 * core
    return me, tp, core, spot, chip_at, ahead


def cov_kernel(chips, x_ref, rin_ref, *refs):
    parts = len(refs) - 17
    cin_refs, refs = refs[:parts], refs[parts:]
    acc_ref, rsum_ref, big, far, lt, cbuf = refs[:6]
    send, recv, psend, precv, ssend, srecv, tsend, trecv, own_sem, cin_sem = refs[6:16]
    (ones_r,) = refs[16:]
    me, tp, core, spot, chip_at, ahead = ring_place(chips)
    rows, width = x_ref.shape
    side = rin_ref.shape[1]
    sub_rows = rows // SUBS
    partner = me + 1 - 2 * core
    onward = chip_at(spot + ahead) * 2 + core
    back = chip_at(spot - ahead) * 2 + core
    owner = me * side // width == tp
    feature = pl.multiple_of(me * side % width, side)
    partner_feature = pl.multiple_of(partner * side % width, side)

    barrier = pltpu.get_barrier_semaphore()
    for peer in (onward, back, partner):
        pl.semaphore_signal(barrier, inc=1, device_id={"tok": peer}, device_id_type=MESH)
    for peer in (me, partner):
        pl.semaphore_signal(
            barrier, inc=1, device_id={"tok": peer, "tp": 1 - tp}, device_id_type=MESH
        )

    def block_row(step, mine):
        turn = ahead if mine else -ahead
        return pl.multiple_of(
            (chip_at(spot - turn * step) * 2 + (core if mine else 1 - core)) * rows, rows
        )

    def span(step, sub):
        return pl.ds(pl.multiple_of(block_row(step, True) + sub * sub_rows, sub_rows), sub_rows)

    def source(step, sub):
        return x_ref.at[pl.ds(sub * sub_rows, sub_rows)] if step == 0 else big.at[span(step, sub)]

    def ring_copy(step, sub):
        return pltpu.make_async_remote_copy(
            src_ref=source(step, sub), dst_ref=big.at[span(step, sub)],
            send_sem=send.at[step, sub], recv_sem=recv.at[step, sub],
            device_id={"tok": onward}, device_id_type=MESH,
        )

    def beside_copy(step, sub):
        return pltpu.make_async_remote_copy(
            src_ref=source(step, sub), dst_ref=big.at[span(step, sub)],
            send_sem=psend.at[step, sub], recv_sem=precv.at[step, sub],
            device_id={"tok": partner}, device_id_type=MESH,
        )

    def side_copy(step, sub, same):
        wanted, target = (feature, me) if same else (partner_feature, partner)
        out_sem, in_sem = (ssend, srecv) if same else (tsend, trecv)
        return pltpu.make_async_remote_copy(
            src_ref=source(step, sub).at[:, pl.ds(wanted, side)], dst_ref=far.at[span(step, sub), :],
            send_sem=out_sem.at[step, sub], recv_sem=in_sem.at[step, sub],
            device_id={"tok": target, "tp": 1 - tp}, device_id_type=MESH,
        )

    def launch(step, sub):
        if step < chips - 1:
            ring_copy(step, sub).start()
        beside_copy(step, sub).start()

        @pl.when(owner)
        def _():
            for same in (True, False):
                side_copy(step, sub, same).start()

    def fetch(step, mine):
        slot = step % 2 * 2 + (0 if mine else 1)
        piece = width // parts
        return [
            pltpu.make_async_copy(
                ref.at[pl.ds(block_row(step, mine), rows), :],
                cbuf.at[slot, :, pl.ds(i * piece, piece)], cin_sem.at[slot, i],
            )
            for i, ref in enumerate(cin_refs)
        ]

    tile = min(512, width)

    def compute(step, mine):
        slot = step % 2 * 2 + (0 if mine else 1)
        place = pl.ds(block_row(step, mine), rows)
        lt[0:side, :] = rin_ref[place, :].T

        @pl.when(owner)
        def _():
            lt[side:2 * side, :] = big[place, pl.ds(feature, side)].T

        @pl.when(jnp.logical_not(owner))
        def _():
            lt[side:2 * side, :] = far[place, :].T

        for copy in fetch(step, mine):
            copy.wait()
        rsum_ref[...] += jnp.dot(lt[0:2 * side, :], ones_r[...], preferred_element_type=jnp.float32)

        @pl.loop(0, width // tile)
        def _(i):
            here = pl.ds(pl.multiple_of(i * tile, tile), tile)
            acc_ref[:, here] += jnp.dot(
                lt[...], cbuf[slot, :, here], preferred_element_type=jnp.float32
            )
            there = pl.ds(pl.multiple_of(width + i * tile, tile), tile)
            acc_ref[:, there] += jnp.dot(
                lt[...], big[place, here], preferred_element_type=jnp.float32
            )

    def arrive(step, mine):
        if not mine:
            for sub in range(SUBS):
                beside_copy(step, sub).wait_recv()

        @pl.when(jnp.logical_not(owner))
        def _():
            for sub in range(SUBS):
                side_copy(step, sub, mine).wait_recv()

    pl.semaphore_wait(barrier, 5)
    for sub in range(SUBS):
        launch(0, sub)
    own = pltpu.make_async_copy(x_ref, big.at[pl.ds(pl.multiple_of(me * rows, rows), rows)], own_sem.at[0])
    own.start()
    for step in range(2):
        for mine in (True, False):
            for copy in fetch(step, mine):
                copy.start()
    ones_r[...] = jnp.ones_like(ones_r)
    lt[2 * side:, :] = jnp.ones((lt.shape[0] - 2 * side, rows), lt.dtype)
    acc_ref[...] = jnp.zeros_like(acc_ref)
    rsum_ref[...] = jnp.zeros_like(rsum_ref)
    own.wait()

    def work(step, mine):
        arrive(step, mine)
        compute(step, mine)
        if step + 2 < chips:
            for copy in fetch(step + 2, mine):
                copy.start()

    for step in range(1, chips):
        for sub in range(SUBS):
            ring_copy(step - 1, sub).wait_recv()
            launch(step, sub)
            if sub == 0:
                work(step - 1, True)
            if sub == SUBS - 1:
                work(step - 1, False)
    work(chips - 1, True)
    work(chips - 1, False)
    for step in range(chips):
        for sub in range(SUBS):
            if step < chips - 1:
                ring_copy(step, sub).wait_send()
            beside_copy(step, sub).wait_send()

            @pl.when(owner)
            def _():
                for same in (True, False):
                    side_copy(step, sub, same).wait_send()


def finish_kernel(all_rows, *refs):
    rsum_ref, out_ref = refs[4:]
    side = out_ref.shape[1]
    for source in range(2):
        acc_ref, csum_ref = refs[2 * source:2 * source + 2]
        mean_col = csum_ref[0:1, :] / all_rows
        for row_source in range(2):
            part = slice(row_source * side, (row_source + 1) * side)
            cov = acc_ref[part, :] / all_rows - (rsum_ref[part, :1] / all_rows) * mean_col
            out_ref[row_source, :, source, :] = cov


def joint_cov(hidden_out, rows_in, cols_in, call_id):
    rows, width = hidden_out.shape
    all_rows, side = rows_in.shape
    chips = all_rows // rows // 2
    parts = len(cols_in)
    dma = pltpu.SemaphoreType.DMA
    tall = 2 * side + 16
    acc, rsum = pl.pallas_call(
        functools.partial(cov_kernel, chips),
        out_shape=[
            jax.ShapeDtypeStruct((tall, 2 * width), jnp.float32),
            jax.ShapeDtypeStruct((2 * side, 128), jnp.float32),
        ],
        in_specs=[pl.BlockSpec(memory_space=pltpu.VMEM)] * 2
        + [pl.BlockSpec(memory_space=pl.ANY)] * parts,
        out_specs=[pl.BlockSpec(memory_space=pltpu.VMEM)] * 2,
        scratch_shapes=[
            pltpu.VMEM((all_rows, width), jnp.bfloat16),
            pltpu.VMEM((all_rows, side), jnp.bfloat16),
            pltpu.VMEM((tall, rows), jnp.bfloat16),
            pltpu.VMEM((4, rows, width), jnp.bfloat16),
        ]
        + [dma((chips, SUBS))] * 8
        + [dma((1,)), dma((4, parts))]
        + [pltpu.VMEM((rows, 128), jnp.bfloat16)],
        compiler_params=pltpu.CompilerParams(
            collective_id=call_id, has_side_effects=True, vmem_limit_bytes=VMEM_LIMIT
        ),
        cost_estimate=pl.CostEstimate(
            flops=8 * all_rows * side * width * 4,
            bytes_accessed=4 * all_rows * (side + width) + 16 * side * width,
            transcendentals=0,
        ),
        name="cov_ring",
    )(hidden_out, rows_in, *cols_in)
    return finish(acc, rsum, all_rows, side, width)


def finish(acc, rsum, all_rows, side, width):
    tile = min(256, width)
    strips = width // tile
    specs = []
    for source in range(2):
        specs.append(pl.BlockSpec((2 * side, tile), lambda j, source=source: (0, source * strips + j)))
        specs.append(
            pl.BlockSpec((8, tile), lambda j, source=source: (2 * side // 8, source * strips + j))
        )
    return pl.pallas_call(
        functools.partial(finish_kernel, all_rows),
        out_shape=jax.ShapeDtypeStruct((2, side, 2, width), jnp.float32),
        grid=(strips,),
        in_specs=specs + [pl.BlockSpec((2 * side, 128), lambda j: (0, 0))],
        out_specs=pl.BlockSpec((2, side, 2, tile), lambda j: (0, 0, 0, j)),
        compiler_params=pltpu.CompilerParams(
            dimension_semantics=("arbitrary",), vmem_limit_bytes=VMEM_LIMIT
        ),
        name="finish",
    )(acc, acc, acc, acc, rsum)


def on_device(hidden_in, norm_gain, w_query, w_key, w_value, w_out, doc_ids):
    tok_rows, col_width = hidden_in.shape
    tok_count = lax.axis_size("tok")
    tp_count = lax.axis_size("tp")
    tok_index = lax.axis_index("tok")
    all_rows = tok_rows * tok_count
    full_in = both_sides(hidden_in)
    widened = full_in.astype(jnp.float32)
    factor = lax.rsqrt(jnp.mean(widened * widened, axis=1, keepdims=True) + epsilon)
    normed = (widened * factor * norm_gain[None, :]).astype(jnp.bfloat16)
    kv_heads = w_key.shape[1] // HS
    groups = w_query.shape[1] // w_key.shape[1]
    first_row = tok_index * tok_rows
    positions = first_row + jnp.arange(tok_rows, dtype=jnp.int32)
    key_local = rotate(
        jnp.dot(normed, w_key, preferred_element_type=jnp.float32).reshape(tok_rows, kv_heads, HS),
        positions % all_rows,
    )
    key_local = key_local.astype(jnp.bfloat16).reshape(tok_rows, kv_heads * HS)
    value_local = jnp.dot(normed, w_value, preferred_element_type=jnp.float32).astype(jnp.bfloat16)
    (kv_rows,) = ring_gather(jnp.stack([key_local, value_local]), False, 0)
    early, late = hidden_in[:, : col_width // 2], hidden_in[:, col_width // 2 :]
    late, kv_rows = lax.optimization_barrier((late, kv_rows))
    cols_in = [lax.all_gather(part, "tok", axis=0, tiled=True) for part in (early, late)]
    rows_in = lax.all_to_all(full_in, "tok", 1, 0, tiled=True)
    queries = rotate(
        jnp.dot(normed, w_query, preferred_element_type=jnp.float32).reshape(
            tok_rows, kv_heads * groups, HS
        ),
        positions % all_rows,
    )
    queries = queries.astype(jnp.bfloat16).reshape(tok_rows, kv_heads * groups * HS)
    query_doc = lax.dynamic_slice_in_dim(doc_ids, first_row, tok_rows, 0)
    lo = jnp.sum((doc_ids[None, :] < query_doc[:, None]).astype(jnp.int32), axis=1)
    bounds = jnp.stack([first_row.astype(jnp.int32), lo[0]])
    attended = attend(queries, kv_rows, jnp.broadcast_to(lo[:, None], (tok_rows, 128)), bounds, kv_heads)
    partial_out = jnp.dot(attended, w_out, preferred_element_type=jnp.float32)
    if tp_count == 2:
        first = lax.axis_index("tp") == 0
        low, high = partial_out[:, :col_width], partial_out[:, col_width:]
        sent = jnp.where(first, high, low).astype(jnp.bfloat16)
        arrived = lax.ppermute(sent, "tp", ((0, 1), (1, 0)))
        summed = jnp.where(first, low, high) + arrived.astype(jnp.float32)
    else:
        summed = lax.psum_scatter(partial_out, "tp", scatter_dimension=1, tiled=True)
    hidden_out = (hidden_in.astype(jnp.float32) + summed).astype(jnp.bfloat16)
    if tp_count == 2:
        return (hidden_out, joint_cov(hidden_out, rows_in, cols_in, 1))
    halves = jnp.stack([hidden_out[:, : col_width // 2], hidden_out[:, col_width // 2 :]])
    (cols_out,) = ring_gather(halves, False, 1)
    rows_out = row_features(cols_out, None)
    return (hidden_out, joint_gram(rows_in, rows_out, cols_in, cols_out))


def solution(mesh):
    return jax.shard_map(
        on_device,
        mesh=mesh,
        in_specs=(
            P("tok", "tp"),
            P(),
            P(None, "tp"),
            P(None, "tp"),
            P(None, "tp"),
            P("tp", None),
            P(),
        ),
        out_specs=(P("tok", "tp"), P(None, "tok", None, "tp")),
        check_vma=False,
    )
```

```python
import functools
import math

import jax
import jax.numpy as jnp
from jax import lax
from jax.experimental import pallas as pl
from jax.experimental.pallas import tpu as pltpu
from jax.sharding import PartitionSpec as P

HS = 128
epsilon = 1e-05
rope_base = 500000.0
VMEM_LIMIT = 60 * 1024 * 1024


def rotate(vectors, positions):
    half_dim = vectors.shape[-1] // 2
    inv_freq = rope_base ** (-(jnp.arange(half_dim, dtype=jnp.float32) * 2.0) / vectors.shape[-1])
    angles = positions.astype(jnp.float32)[:, None] * inv_freq[None, :]
    cosine = jnp.cos(angles)[:, None, :]
    sine_part = jnp.sin(angles)[:, None, :]
    first_half = vectors[..., :half_dim]
    second_half = vectors[..., half_dim:]
    return jnp.concatenate(
        [
            first_half * cosine - second_half * sine_part,
            second_half * cosine + first_half * sine_part,
        ],
        axis=-1,
    )


def attend_kernel(groups, block, bounds, q_ref, k_ref, v_ref, lo_ref, out_ref, s_ref, m_ref, l_ref, acc_ref):
    rows = q_ref.shape[0]
    first_row = bounds[0]
    scale = HS ** (-0.5) * math.log2(math.e)
    start = bounds[1] // block
    stop = (first_row + rows + block - 1) // block
    lanes = 128
    m_ref[...] = jnp.full_like(m_ref, -jnp.inf)
    l_ref[...] = jnp.zeros_like(l_ref)
    acc_ref[...] = jnp.zeros_like(acc_ref)

    @pl.loop(start, stop)
    def _(step):
        first_key = pl.multiple_of(step * block, block)
        keys = k_ref[pl.ds(first_key, block), :]
        key_pos = first_key + lax.broadcasted_iota(jnp.int32, (rows, block), 1)
        query_pos = first_row + lax.broadcasted_iota(jnp.int32, (rows, block), 0)
        allowed = (key_pos >= lo_ref[:, :1]) & (key_pos <= query_pos)
        for head in range(groups):
            part = pl.ds(head * rows, rows)
            s = lax.dot_general(
                q_ref[:, head * HS:(head + 1) * HS], keys,
                (((1,), (1,)), ((), ())), preferred_element_type=jnp.float32,
            ) * scale
            s = jnp.where(allowed, s, -jnp.inf)
            s_ref[step, part, :] = s
            top = m_ref[part, :]
            for piece in range(block // lanes):
                top = jnp.maximum(top, s[:, piece * lanes:(piece + 1) * lanes])
            m_ref[part, :] = top

    m_ref[...] = jnp.broadcast_to(jnp.max(m_ref[...], axis=-1, keepdims=True), m_ref.shape)

    @pl.loop(start, stop)
    def _(step):
        first_key = pl.multiple_of(step * block, block)
        values = v_ref[pl.ds(first_key, block), :]
        for head in range(groups):
            part = pl.ds(head * rows, rows)
            weights = jnp.exp2(s_ref[step, part, :] - m_ref[part, :1])
            total = l_ref[part, :]
            for piece in range(block // lanes):
                total = total + weights[:, piece * lanes:(piece + 1) * lanes]
            l_ref[part, :] = total
            acc_ref[part, :] += jnp.dot(
                weights.astype(jnp.bfloat16), values, preferred_element_type=jnp.float32
            )

    for head in range(groups):
        part = pl.ds(head * rows, rows)
        weight_sum = jnp.sum(l_ref[part, :], axis=-1, keepdims=True)
        out_ref[:, head * HS:(head + 1) * HS] = (acc_ref[part, :] / weight_sum).astype(out_ref.dtype)


def attend(queries, kv_rows, lo, bounds, kv_heads):
    rows, width = queries.shape
    all_rows = kv_rows.shape[1]
    groups = width // (kv_heads * HS)
    block = min(512, all_rows)
    wide = groups * HS
    return pl.pallas_call(
        functools.partial(attend_kernel, groups, block),
        out_shape=jax.ShapeDtypeStruct((rows, width), jnp.bfloat16),
        grid_spec=pltpu.PrefetchScalarGridSpec(
            num_scalar_prefetch=1,
            grid=(kv_heads,),
            in_specs=[
                pl.BlockSpec((rows, wide), lambda g, b: (0, g)),
                pl.BlockSpec((None, all_rows, HS), lambda g, b: (0, 0, g)),
                pl.BlockSpec((None, all_rows, HS), lambda g, b: (1, 0, g)),
                pl.BlockSpec((rows, 128), lambda g, b: (0, 0)),
            ],
            out_specs=pl.BlockSpec((rows, wide), lambda g, b: (0, g)),
            scratch_shapes=[
                pltpu.VMEM((all_rows // block, groups * rows, block), jnp.float32),
                pltpu.VMEM((groups * rows, 128), jnp.float32),
                pltpu.VMEM((groups * rows, 128), jnp.float32),
                pltpu.VMEM((groups * rows, HS), jnp.float32),
            ],
        ),
        compiler_params=pltpu.CompilerParams(
            dimension_semantics=("arbitrary",), vmem_limit_bytes=VMEM_LIMIT
        ),
        cost_estimate=pl.CostEstimate(
            flops=4 * rows * all_rows * width,
            bytes_accessed=2 * all_rows * kv_heads * HS * 2 + 4 * rows * width,
            transcendentals=rows * all_rows * width // HS,
        ),
        name="attend",
    )(bounds, queries, kv_rows, kv_rows, lo)


def gram_kernel(strips, rin_ref, rout_ref, low_ref, high_ref, cout_ref, out_ref, rt_ref, mean_ref):
    all_rows, row_width = rin_ref.shape

    @pl.when(pl.program_id(0) == 0)
    def _():
        ones = jnp.ones((all_rows, 128), jnp.bfloat16)
        for source, ref in enumerate((rin_ref, rout_ref)):
            part = pl.ds(source * row_width, row_width)
            rt_ref[part, :] = ref[...].T
            mean_ref[part, :] = (
                jnp.dot(rt_ref[part, :], ones, preferred_element_type=jnp.float32) / all_rows
            )

    ones = jnp.ones((8, all_rows), jnp.bfloat16)

    def block(source, ref):
        cols = ref[...]
        col_mean = jnp.dot(ones, cols, preferred_element_type=jnp.float32)[:1] / all_rows
        gram = jnp.dot(rt_ref[...], cols, preferred_element_type=jnp.float32)
        cov = gram / all_rows - mean_ref[:, :1] * col_mean
        for row_source in range(2):
            out_ref[row_source, :, source, :] = cov[row_source * row_width:(row_source + 1) * row_width]

    @pl.when(pl.program_id(0) < strips)
    def _():
        block(0, low_ref)

    @pl.when(pl.program_id(0) >= strips)
    def _():
        block(0, high_ref)

    block(1, cout_ref)


def joint_gram(rin, rout, cin, cout):
    all_rows, row_width = rin.shape
    half = cout.shape[2]
    col_width = 2 * half
    tile = min(256, half)
    strips = half // tile
    whole = pl.BlockSpec((all_rows, row_width), lambda j: (0, 0), pipeline_mode=pl.Buffered(1))
    strip = pl.BlockSpec((None, all_rows, tile), lambda j: (j // strips, 0, j % strips))
    low = pl.BlockSpec((all_rows, tile), lambda j: (0, jnp.minimum(j, strips - 1)))
    high = pl.BlockSpec((all_rows, tile), lambda j: (0, jnp.maximum(j - strips, 0)))
    return pl.pallas_call(
        functools.partial(gram_kernel, strips),
        out_shape=jax.ShapeDtypeStruct((2, row_width, 2, col_width), jnp.float32),
        grid=(col_width // tile,),
        in_specs=[whole, whole, low, high, strip],
        out_specs=pl.BlockSpec((2, row_width, 2, tile), lambda j: (0, 0, 0, j)),
        scratch_shapes=[
            pltpu.VMEM((2 * row_width, all_rows), jnp.bfloat16),
            pltpu.VMEM((2 * row_width, 128), jnp.float32),
        ],
        compiler_params=pltpu.CompilerParams(
            dimension_semantics=("arbitrary",), vmem_limit_bytes=VMEM_LIMIT
        ),
        cost_estimate=pl.CostEstimate(
            flops=8 * all_rows * row_width * col_width,
            bytes_accessed=4 * all_rows * (row_width + col_width) + 16 * row_width * col_width,
            transcendentals=0,
        ),
        name="joint_gram",
    )(rin, rout, *cin, cout)


def both_sides(block):
    if lax.axis_size("tp") != 2:
        return lax.all_gather(block, "tp", axis=1, tiled=True)
    other = lax.ppermute(block, "tp", ((0, 1), (1, 0)))
    first = lax.axis_index("tp") == 0
    return jnp.concatenate([jnp.where(first, block, other), jnp.where(first, other, block)], axis=1)


def ring_kernel(chips, share, x_ref, *refs):
    if share:
        out_ref, side_ref, send, recv, psend, precv, local, ssend, srecv = refs
    else:
        out_ref, send, recv, psend, precv, local = refs
    mesh_id = pl.DeviceIdType.MESH
    rows = x_ref.shape[1]
    me, tp = lax.axis_index("tok"), lax.axis_index("tp")
    count = 2 * chips
    core, chip = me % 2, me // 2
    depth = chips // 2
    spot = jnp.where(chip % 2 == 0, chip // 2, chips - 1 - chip // 2)

    def device(place):
        place = (place + 2 * chips) % chips
        return jnp.where(place < depth, place * 4, (chips - 1 - place) * 4 + 2) + core

    partner = me + 1 - 2 * core
    ways = (device(spot + 1), device(spot - 1))
    barrier = pltpu.get_barrier_semaphore()
    for peer in (*ways, partner):
        pl.semaphore_signal(barrier, inc=1, device_id={"tok": peer}, device_id_type=mesh_id)
    if share:
        pl.semaphore_signal(barrier, inc=1, device_id={"tp": 1 - tp}, device_id_type=mesh_id)
    pl.semaphore_wait(barrier, 4 if share else 3)

    def block(way, origin):
        return out_ref.at[way, pl.ds(pl.multiple_of(origin * rows, rows), rows), :]

    pending = []

    def step_copies(step, way):
        origin = device(spot - step if way == 0 else spot + step)
        source = x_ref.at[way] if step == 0 else block(way, origin)
        ring = None
        if step < chips - 1:
            ring = pltpu.make_async_remote_copy(
                src_ref=source, dst_ref=block(way, origin), send_sem=send.at[way, step],
                recv_sem=recv.at[way, step], device_id={"tok": ways[way]}, device_id_type=mesh_id,
            )
            ring.start()
        beside = pltpu.make_async_remote_copy(
            src_ref=source, dst_ref=block(way, origin), send_sem=psend.at[way, step],
            recv_sem=precv.at[way, step], device_id={"tok": partner}, device_id_type=mesh_id,
        )
        beside.start()
        pending.append((ring, beside))
        return ring

    rings = [step_copies(0, way) for way in range(2)]
    own = [pltpu.make_async_copy(x_ref.at[way], block(way, me), local.at[way]) for way in range(2)]
    for copy in own:
        copy.start()
    if share:
        width = side_ref.shape[1]
        half = x_ref.shape[2]
        owner = me // (count // 2)
        my_way = me * width % (2 * half) // half
        features = pl.ds(pl.multiple_of(me * width % half, width), width)

    def side_copy(step, way, kind):
        origin = device(spot - step if way == 0 else spot + step)
        origin = origin + kind * (1 - 2 * core)
        source = x_ref.at[way, :, features]
        if step > 0 or kind > 0:
            source = out_ref.at[way, pl.ds(pl.multiple_of(origin * rows, rows), rows), features]
        return pltpu.make_async_remote_copy(
            src_ref=source,
            dst_ref=side_ref.at[pl.ds(pl.multiple_of(origin * rows, rows), rows), :],
            send_sem=ssend.at[kind, step], recv_sem=srecv.at[kind, step],
            device_id={"tp": 1 - tp}, device_id_type=mesh_id,
        )

    def each_side(act, step, way, kind, holder):
        if share:
            @pl.when((my_way == way) & ((owner == tp) == holder))
            def _():
                act(side_copy(step, way, kind))

    def start(copy):
        copy.start()

    for way in range(2):
        each_side(start, 0, way, 0, True)
    for step in range(1, chips):
        for way in range(2):
            rings[way].wait_recv()
            rings[way] = step_copies(step, way)
            each_side(start, step, way, 0, True)
            pending[2 * (step - 1) + way][1].wait_recv()
            each_side(start, step - 1, way, 1, True)
    for way in range(2):
        pending[2 * (chips - 1) + way][1].wait_recv()
        each_side(start, chips - 1, way, 1, True)
    for ring, beside in pending:
        if ring is not None:
            ring.wait_send()
        beside.wait_send()
    for copy in own:
        copy.wait()
    for step in range(chips):
        for way in range(2):
            for kind in range(2):
                each_side(lambda copy: copy.wait_send(), step, way, kind, True)
                each_side(lambda copy: copy.wait_recv(), step, way, kind, False)


def ring_gather(halves, share, call_id):
    _, rows, width = halves.shape
    count = lax.axis_size("tok")
    chips = count // 2
    out_shape = [jax.ShapeDtypeStruct((2, rows * count, width), halves.dtype)]
    dma = pltpu.SemaphoreType.DMA
    scratch = [dma((2, chips))] * 4 + [dma((2,))]
    if share:
        out_shape.append(jax.ShapeDtypeStruct((rows * count, 4 * width // count), halves.dtype))
        scratch += [dma((2, chips))] * 2
    return pl.pallas_call(
        functools.partial(ring_kernel, chips, share),
        out_shape=out_shape,
        in_specs=[pl.BlockSpec(memory_space=pltpu.VMEM)],
        out_specs=[pl.BlockSpec(memory_space=pl.ANY)] * len(out_shape),
        scratch_shapes=scratch,
        compiler_params=pltpu.CompilerParams(
            collective_id=call_id, has_side_effects=True, vmem_limit_bytes=VMEM_LIMIT
        ),
        cost_estimate=pl.CostEstimate(
            flops=40_000_000_000, bytes_accessed=2 * halves.size * count * 2, transcendentals=0
        ),
        name="ring_share" if share else "ring",
    )(halves)


def row_features(columns, arrived):
    _, all_rows, half = columns.shape
    row_width = 2 * half * lax.axis_size("tp") // lax.axis_size("tok")
    first = lax.axis_index("tok") * row_width
    offset, owner = first % (2 * half), first // (2 * half)
    mine = lax.dynamic_slice(columns, (offset // half, 0, offset % half), (1, all_rows, row_width))[0]
    owned = lax.axis_index("tp") == owner
    if arrived is None:
        return lax.psum(jnp.where(owned, mine, jnp.zeros_like(mine)), "tp")
    return jnp.where(owned, mine, arrived)


SUBS = 2
MESH = pl.DeviceIdType.MESH


def ring_place(chips):
    me, tp = lax.axis_index("tok"), lax.axis_index("tp")
    core, chip = me % 2, me // 2
    spot = jnp.where(chip % 2 == 0, chip // 2, chips - 1 - chip // 2)

    def chip_at(place):
        place = (place + 2 * chips) % chips
        return jnp.where(place < chips // 2, place * 2, (chips - 1 - place) * 2 + 1)

    ahead = 1 - 2 * core
    return me, tp, core, spot, chip_at, ahead, chips


class Ring:
    def __init__(self, place, big, own, subs, sems, far=None, side=None, side_sems=None):
        self.me, self.tp, self.core, self.spot, self.chip_at, self.ahead, self.chips = place
        self.big, self.own, self.subs = big, own, subs
        self.rows = big.shape[0] // (2 * self.chips)
        self.part = self.rows // subs
        self.send, self.recv, self.psend, self.precv = sems
        self.far, self.side = far, side
        self.partner = self.me + 1 - 2 * self.core
        self.onward = self.chip_at(self.spot + self.ahead) * 2 + self.core
        self.back = self.chip_at(self.spot - self.ahead) * 2 + self.core
        if far is not None:
            self.ssend, self.srecv, self.tsend, self.trecv = side_sems
            width = big.shape[1]
            self.owner = self.me * side // width == self.tp
            self.feature = pl.multiple_of(self.me * side % width, side)
            self.partner_feature = pl.multiple_of(self.partner * side % width, side)

    def block(self, step, mine):
        turn = self.ahead if mine else -self.ahead
        return self.chip_at(self.spot - turn * step) * 2 + (self.core if mine else 1 - self.core)

    def block_row(self, step, mine):
        return pl.multiple_of(self.block(step, mine) * self.rows, self.rows)

    def span(self, step, sub):
        return pl.ds(pl.multiple_of(self.block_row(step, True) + sub * self.part, self.part), self.part)

    def source(self, step, sub):
        if self.own is not None and isinstance(step, int) and step == 0:
            return self.own.at[pl.ds(sub * self.part, self.part)]
        return self.big.at[self.span(step, sub)]

    def ring_copy(self, step, sub):
        return pltpu.make_async_remote_copy(
            src_ref=self.source(step, sub), dst_ref=self.big.at[self.span(step, sub)],
            send_sem=self.send.at[step, sub], recv_sem=self.recv.at[step, sub],
            device_id={"tok": self.onward}, device_id_type=MESH,
        )

    def beside_copy(self, step, sub):
        return pltpu.make_async_remote_copy(
            src_ref=self.source(step, sub), dst_ref=self.big.at[self.span(step, sub)],
            send_sem=self.psend.at[step, sub], recv_sem=self.precv.at[step, sub],
            device_id={"tok": self.partner}, device_id_type=MESH,
        )

    def side_copy(self, step, sub, same):
        wanted, target = (self.feature, self.me) if same else (self.partner_feature, self.partner)
        out_sem, in_sem = (self.ssend, self.srecv) if same else (self.tsend, self.trecv)
        return pltpu.make_async_remote_copy(
            src_ref=self.source(step, sub).at[:, pl.ds(wanted, self.side)],
            dst_ref=self.far.at[self.span(step, sub), :],
            send_sem=out_sem.at[step, sub], recv_sem=in_sem.at[step, sub],
            device_id={"tok": target, "tp": 1 - self.tp}, device_id_type=MESH,
        )

    def launch(self, step, sub):
        if isinstance(step, int):
            if step < self.chips - 1:
                self.ring_copy(step, sub).start()
        else:
            @pl.when(step < self.chips - 1)
            def _():
                self.ring_copy(step, sub).start()
        self.beside_copy(step, sub).start()

    def launch_side(self, step, sub):
        @pl.when(self.owner)
        def _():
            for same in (True, False):
                self.side_copy(step, sub, same).start()

    def event(self, step, sub):
        self.ring_copy(step - 1, sub).wait_recv()
        self.launch(step, sub)

    def beside_arrived(self, step):
        for sub in range(self.subs):
            self.beside_copy(step, sub).wait_recv()

    def side_arrived(self, step, mine):
        @pl.when(jnp.logical_not(self.owner))
        def _():
            for sub in range(self.subs):
                self.side_copy(step, sub, mine).wait_recv()

    def drain(self):
        for step in range(self.chips):
            for sub in range(self.subs):
                if step < self.chips - 1:
                    self.ring_copy(step, sub).wait_send()
                self.beside_copy(step, sub).wait_send()
                if self.far is not None:
                    @pl.when(self.owner)
                    def _():
                        for same in (True, False):
                            self.side_copy(step, sub, same).wait_send()


def greet(ring):
    barrier = pltpu.get_barrier_semaphore()
    for peer in (ring.onward, ring.back, ring.partner):
        pl.semaphore_signal(barrier, inc=1, device_id={"tok": peer}, device_id_type=MESH)
    for peer in (ring.me, ring.partner):
        pl.semaphore_signal(
            barrier, inc=1, device_id={"tok": peer, "tp": 1 - ring.tp}, device_id_type=MESH
        )
    pl.semaphore_wait(barrier, 5)


def cov_kernel(chips, x_ref, cin_ref, rin_ref, *refs):
    acc_ref, rsum_ref, big, far, lt, cbuf, rbuf = refs[:7]
    sems, side_sems, own_sem, cin_sem, rin_sem, ones_r = refs[7:11], refs[11:15], *refs[15:]
    ring = Ring(ring_place(chips), big, x_ref, SUBS, sems, far, rin_ref.shape[1], side_sems)
    rows, width = x_ref.shape
    side = ring.side
    owner = ring.owner
    greet(ring)
    for sub in range(SUBS):
        ring.launch(0, sub)
        ring.launch_side(0, sub)
    own = pltpu.make_async_copy(x_ref, big.at[pl.ds(pl.multiple_of(ring.me * rows, rows), rows)], own_sem.at[0])
    own.start()

    def slot_of(step, mine):
        return step % 2 * 2 + (0 if mine else 1)

    def fetch(step, mine):
        slot = slot_of(step, mine)
        place = pl.ds(ring.block_row(step, mine), rows)
        return (
            pltpu.make_async_copy(cin_ref.at[place, :], cbuf.at[slot], cin_sem.at[slot]),
            pltpu.make_async_copy(rin_ref.at[place, :], rbuf.at[slot], rin_sem.at[slot]),
        )

    def start_fetch(step, mine):
        cols, strip = fetch(step, mine)
        cols.start()

        @pl.when(jnp.logical_not(owner))
        def _():
            strip.start()

    for step in range(2):
        for mine in (True, False):
            start_fetch(step, mine)
    ones_r[...] = jnp.ones_like(ones_r)
    lt[2 * side:, :] = jnp.ones((lt.shape[0] - 2 * side, rows), lt.dtype)
    acc_ref[...] = jnp.zeros_like(acc_ref)
    rsum_ref[...] = jnp.zeros_like(rsum_ref)
    own.wait()
    tile = min(512, width)

    def work(step, mine):
        if not mine:
            ring.beside_arrived(step)
        ring.side_arrived(step, mine)
        slot = slot_of(step, mine)
        place = pl.ds(ring.block_row(step, mine), rows)
        cols, strip = fetch(step, mine)
        cols.wait()

        @pl.when(owner)
        def _():
            lt[0:side, :] = cbuf[slot, :, pl.ds(ring.feature, side)].T
            lt[side:2 * side, :] = big[place, pl.ds(ring.feature, side)].T

        @pl.when(jnp.logical_not(owner))
        def _():
            strip.wait()
            lt[0:side, :] = rbuf[slot].T
            lt[side:2 * side, :] = far[place, :].T

        rsum_ref[...] += jnp.dot(lt[0:2 * side, :], ones_r[...], preferred_element_type=jnp.float32)

        @pl.loop(0, width // tile)
        def _(i):
            here = pl.ds(pl.multiple_of(i * tile, tile), tile)
            acc_ref[:, here] += jnp.dot(
                lt[...], cbuf[slot, :, here], preferred_element_type=jnp.float32
            )
            there = pl.ds(pl.multiple_of(width + i * tile, tile), tile)
            acc_ref[:, there] += jnp.dot(
                lt[...], big[place, here], preferred_element_type=jnp.float32
            )

        if step + 2 < chips:
            start_fetch(step + 2, mine)

    for step in range(1, chips):
        for sub in range(SUBS):
            ring.event(step, sub)
            ring.launch_side(step, sub)
            if sub == 0:
                work(step - 1, True)
            if sub == SUBS - 1:
                work(step - 1, False)
    work(chips - 1, True)
    work(chips - 1, False)
    ring.drain()


def finish_kernel(all_rows, *refs):
    rsum_ref, out_ref = refs[4:]
    side = out_ref.shape[1]
    for source in range(2):
        acc_ref, csum_ref = refs[2 * source:2 * source + 2]
        mean_col = csum_ref[0:1, :] / all_rows
        for row_source in range(2):
            part = slice(row_source * side, (row_source + 1) * side)
            cov = acc_ref[part, :] / all_rows - (rsum_ref[part, :1] / all_rows) * mean_col
            out_ref[row_source, :, source, :] = cov


def joint_cov(hidden_out, rows_in, cols_in, call_id):
    rows, width = hidden_out.shape
    all_rows, side = rows_in.shape
    chips = all_rows // rows // 2
    dma = pltpu.SemaphoreType.DMA
    tall = 2 * side + 16
    acc, rsum = pl.pallas_call(
        functools.partial(cov_kernel, chips),
        out_shape=[
            jax.ShapeDtypeStruct((tall, 2 * width), jnp.float32),
            jax.ShapeDtypeStruct((2 * side, 128), jnp.float32),
        ],
        in_specs=[pl.BlockSpec(memory_space=pltpu.VMEM)]
        + [pl.BlockSpec(memory_space=pl.ANY)] * 2,
        out_specs=[pl.BlockSpec(memory_space=pltpu.VMEM)] * 2,
        scratch_shapes=[
            pltpu.VMEM((all_rows, width), jnp.bfloat16),
            pltpu.VMEM((all_rows, side), jnp.bfloat16),
            pltpu.VMEM((tall, rows), jnp.bfloat16),
            pltpu.VMEM((4, rows, width), jnp.bfloat16),
            pltpu.VMEM((4, rows, side), jnp.bfloat16),
        ]
        + [dma((chips, SUBS))] * 8
        + [dma((1,)), dma((4,)), dma((4,))]
        + [pltpu.VMEM((rows, 128), jnp.bfloat16)],
        compiler_params=pltpu.CompilerParams(
            collective_id=call_id, has_side_effects=True, vmem_limit_bytes=VMEM_LIMIT
        ),
        cost_estimate=pl.CostEstimate(
            flops=8 * all_rows * side * width * 4,
            bytes_accessed=4 * all_rows * (side + width) + 16 * side * width,
            transcendentals=0,
        ),
        name="cov_ring",
    )(hidden_out, cols_in, rows_in)
    return finish(acc, rsum, all_rows, side, width)


def finish(acc, rsum, all_rows, side, width):
    tile = min(256, width)
    strips = width // tile
    specs = []
    for source in range(2):
        specs.append(pl.BlockSpec((2 * side, tile), lambda j, source=source: (0, source * strips + j)))
        specs.append(
            pl.BlockSpec((8, tile), lambda j, source=source: (2 * side // 8, source * strips + j))
        )
    return pl.pallas_call(
        functools.partial(finish_kernel, all_rows),
        out_shape=jax.ShapeDtypeStruct((2, side, 2, width), jnp.float32),
        grid=(strips,),
        in_specs=specs + [pl.BlockSpec((2 * side, 128), lambda j: (0, 0))],
        out_specs=pl.BlockSpec((2, side, 2, tile), lambda j: (0, 0, 0, j)),
        compiler_params=pltpu.CompilerParams(
            dimension_semantics=("arbitrary",), vmem_limit_bytes=VMEM_LIMIT
        ),
        name="finish",
    )(acc, acc, acc, acc, rsum)


NEG = -1e30


def front_kernel(
    chips, kv_heads, groups, x_ref, gain_ref, cos_ref, sin_ref, kdoc_ref, qdoc_ref,
    wq_ref, wk_ref, wv_ref, wo_ref, out_ref, cin, far, other, normed, wkv, wq, wo, kv, q_ref,
    m_ref, l_ref, acc_ref, att, mine_sum, sent, arrived, bias, *sems
):
    place = ring_place(chips)
    hid_sems, side_sems, kv_sems = sems[0:4], sems[4:8], sems[8:12]
    xsend, xrecv, osend, orecv, own_sem, wkv_sem, wq_sem, wo_sem = sems[12:]
    rows, width = x_ref.shape
    side = far.shape[1]
    hid = Ring(place, cin, x_ref, SUBS, hid_sems, far, side, side_sems)
    ring = Ring(place, kv, None, SUBS, kv_sems)
    me, tp = hid.me, hid.tp
    half = rows // SUBS
    kv_width = kv_heads * HS
    scale = HS ** (-0.5) * math.log2(math.e)
    head_pair = 2 * HS
    q_tiles = kv_heads * groups // 2
    out_tile = width // 4

    def swap(sub):
        part = pl.ds(sub * half, half)
        return pltpu.make_async_remote_copy(
            src_ref=x_ref.at[part], dst_ref=other.at[part], send_sem=xsend.at[sub],
            recv_sem=xrecv.at[sub], device_id={"tp": 1 - tp}, device_id_type=MESH,
        )

    def fetch_q(t):
        col = pl.ds(pl.multiple_of(t * head_pair, head_pair), head_pair)
        return pltpu.make_async_copy(wq_ref.at[:, col], wq.at[t % 4], wq_sem.at[t % 4])

    def fetch_out(side_tp, i):
        col = pl.ds(pl.multiple_of(side_tp * width + i * out_tile, out_tile), out_tile)
        return pltpu.make_async_copy(wo_ref.at[:, col], wo.at[i], wo_sem.at[i])

    def out_part(i):
        return pl.ds(pl.multiple_of(i * out_tile, out_tile), out_tile)

    def give(i):
        return pltpu.make_async_remote_copy(
            src_ref=sent.at[:, out_part(i)], dst_ref=arrived.at[:, out_part(i)],
            send_sem=osend.at[i], recv_sem=orecv.at[i],
            device_id={"tp": 1 - tp}, device_id_type=MESH,
        )

    keys = [
        pltpu.make_async_copy(ref, wkv.at[:, pl.ds(i * kv_width, kv_width)], wkv_sem.at[i])
        for i, ref in enumerate((wk_ref, wv_ref))
    ]
    for copy in keys:
        copy.start()
    greet(hid)
    for sub in range(SUBS):
        swap(sub).start()
        hid.launch(0, sub)
    own = pltpu.make_async_copy(x_ref, cin.at[pl.ds(pl.multiple_of(me * rows, rows), rows)], own_sem.at[0])
    own.start()
    for t in range(4):
        fetch_q(t).start()
    for i in range(4):
        fetch_out(1 - tp, i).start()

    @pl.loop(0, kv_heads)
    def _(g):
        m_ref[g] = jnp.full(m_ref.shape[1:], NEG, jnp.float32)
        l_ref[g] = jnp.zeros(l_ref.shape[1:], jnp.float32)
        acc_ref[g] = jnp.zeros(acc_ref.shape[1:], jnp.float32)

    my_cols = pl.ds(pl.multiple_of(tp * width, width), width)
    other_cols = pl.ds(pl.multiple_of((1 - tp) * width, width), width)

    def normalise(sub):
        @pl.loop(0, half // 32)
        def _(r):
            part = pl.ds(pl.multiple_of(sub * half + r * 32, 32), 32)
            near = x_ref[part, :].astype(jnp.float32)
            away = other[part, :].astype(jnp.float32)
            total = jnp.sum(near * near, axis=1, keepdims=True) + jnp.sum(away * away, axis=1, keepdims=True)
            factor = lax.rsqrt(total / (2 * width) + epsilon)
            normed[part, my_cols] = (near * factor * gain_ref[:, my_cols]).astype(jnp.bfloat16)
            normed[part, other_cols] = (away * factor * gain_ref[:, other_cols]).astype(jnp.bfloat16)

    def turned(vectors):
        return vectors * cos_ref[...] + pltpu.roll(vectors, HS // 2, 1) * sin_ref[...]

    hid.event(1, 0)
    hid.event(1, 1)
    swap(0).wait_recv()
    normalise(0)
    hid.event(2, 0)
    hid.event(2, 1)
    swap(1).wait_recv()
    normalise(1)
    for copy in keys:
        copy.wait()
    my_rows = pl.ds(pl.multiple_of(me * rows, rows), rows)

    @pl.loop(0, kv_width // head_pair)
    def _(t):
        col = pl.multiple_of(t * head_pair, head_pair)
        found = jnp.dot(normed[...], wkv[:, pl.ds(col, head_pair)], preferred_element_type=jnp.float32)
        for j in range(2):
            piece = turned(found[:, j * HS:(j + 1) * HS]).astype(jnp.bfloat16)
            kv[my_rows, pl.ds(pl.multiple_of(col + j * HS, HS), HS)] = piece

    @pl.loop(0, kv_width // head_pair)
    def _(t):
        col = pl.ds(pl.multiple_of(kv_width + t * head_pair, head_pair), head_pair)
        found = jnp.dot(normed[...], wkv[:, col], preferred_element_type=jnp.float32)
        kv[my_rows, col] = found.astype(jnp.bfloat16)

    for sub in range(SUBS):
        ring.launch(0, sub)
    for step in range(3):
        for sub in range(SUBS):
            hid.launch_side(step, sub)

    @pl.loop(0, q_tiles)
    def _(t):
        fetch_q(t).wait()
        found = jnp.dot(normed[...], wq[t % 4], preferred_element_type=jnp.float32)
        for j in range(2):
            head = t * 2 + j
            row = pl.multiple_of(head % groups * rows, rows)
            q_ref[head // groups, pl.ds(row, rows), :] = turned(found[:, j * HS:(j + 1) * HS]).astype(jnp.bfloat16)

        @pl.when(t + 4 < q_tiles)
        def _():
            fetch_q(t + 4).start()

        @pl.when(t == q_tiles // 2)
        def _():
            ring.event(1, 0)

    ring.event(1, 1)

    def block_attention(row):
        key_pos = row + lax.broadcasted_iota(jnp.int32, (rows, rows), 1)
        query_pos = me * rows + lax.broadcasted_iota(jnp.int32, (rows, rows), 0)
        allowed = (kdoc_ref[:, pl.ds(row, rows)] == qdoc_ref[:, :1]) & (key_pos <= query_pos)
        bias[...] = jnp.where(allowed, 0.0, NEG)

        @pl.loop(0, kv_heads)
        def _(g):
            k = kv[pl.ds(row, rows), pl.ds(pl.multiple_of(g * HS, HS), HS)]
            v = kv[pl.ds(row, rows), pl.ds(pl.multiple_of(kv_width + g * HS, HS), HS)]
            for head in range(groups):
                part = pl.ds(head * rows, rows)
                s = lax.dot_general(
                    q_ref[g, part, :], k, (((1,), (1,)), ((), ())), preferred_element_type=jnp.float32
                ) * scale + bias[...]
                old = m_ref[g, part, :]
                top = jnp.maximum(old, jnp.max(s, axis=-1, keepdims=True))
                fade = jnp.exp2(old - top)
                weights = [jnp.exp2(s[:, i:i + 128] - top) for i in range(0, rows, 128)]
                total = l_ref[g, part, :] * fade
                for piece in weights:
                    total = total + piece
                l_ref[g, part, :] = total
                m_ref[g, part, :] = top
                acc_ref[g, part, :] = acc_ref[g, part, :] * fade + jnp.dot(
                    jnp.concatenate(weights, axis=1).astype(jnp.bfloat16), v,
                    preferred_element_type=jnp.float32,
                )

    @pl.loop(0, 2 * chips)
    def _(u):
        step, which = u // 2, u % 2
        later = u + 4
        @pl.when(later < 2 * chips)
        def _():
            ring.event(later // 2, later % 2)

        @pl.when(later == 2 * chips - 2)
        def _():
            for sub in range(SUBS):
                hid.event(3, sub)
                hid.launch_side(3, sub)

        @pl.when(which == 1)
        def _():
            ring.beside_arrived(step)

        block = jnp.where(which == 0, ring.block(step, True), ring.block(step, False))

        @pl.when(block <= me)
        def _():
            block_attention(pl.multiple_of(block * rows, rows))

    hid.event(4, 0)
    hid.event(4, 1)

    @pl.loop(0, kv_heads)
    def _(g):
        for head in range(groups):
            part = pl.ds(head * rows, rows)
            weight_sum = jnp.sum(l_ref[g, part, :], axis=-1, keepdims=True)
            col = pl.ds(pl.multiple_of((g * groups + head) * HS, HS), HS)
            att[:, col] = (acc_ref[g, part, :] / weight_sum).astype(jnp.bfloat16)

    @pl.loop(0, 4)
    def _(i):
        fetch_out(1 - tp, i).wait()
        found = jnp.dot(att[...], wo[i], preferred_element_type=jnp.float32)
        sent[:, out_part(i)] = found.astype(jnp.bfloat16)

        @pl.when(i > 0)
        def _():
            give(i - 1).start()

        fetch_out(tp, i).start()

    for sub in range(SUBS):
        hid.launch_side(4, sub)
    hid.event(5, 0)
    give(3).start()

    @pl.loop(0, 4)
    def _(i):
        fetch_out(tp, i).wait()
        mine_sum[:, out_part(i)] = jnp.dot(att[...], wo[i], preferred_element_type=jnp.float32)

    hid.event(5, 1)
    for sub in range(SUBS):
        hid.launch_side(5, sub)

    def settle(i):
        give(i).wait_recv()
        summed = mine_sum[:, out_part(i)] + arrived[:, out_part(i)].astype(jnp.float32)
        out_ref[:, out_part(i)] = (x_ref[:, out_part(i)].astype(jnp.float32) + summed).astype(jnp.bfloat16)

    pl.loop(0, 2)(settle)
    for step in range(6, chips):
        for sub in range(SUBS):
            hid.event(step, sub)
            hid.launch_side(step, sub)
    pl.loop(2, 4)(settle)
    own.wait()
    for step in range(chips):
        hid.beside_arrived(step)
        for mine in (True, False):
            hid.side_arrived(step, mine)
    hid.drain()
    ring.drain()
    for sub in range(SUBS):
        swap(sub).wait_send()
    for i in range(4):
        give(i).wait_send()


def front(hidden_in, norm_gain, cosine, sine, doc_ids, query_doc, w_query, w_key, w_value, w_out, call_id):
    rows, width = hidden_in.shape
    all_rows = doc_ids.shape[1]
    chips = all_rows // rows // 2
    side = width * 2 // (2 * chips)
    kv_heads = w_key.shape[1] // HS
    groups = w_query.shape[1] // w_key.shape[1]
    dma = pltpu.SemaphoreType.DMA
    bf16, f32 = jnp.bfloat16, jnp.float32
    stacked = (kv_heads, groups * rows, HS)
    return pl.pallas_call(
        functools.partial(front_kernel, chips, kv_heads, groups),
        out_shape=[
            jax.ShapeDtypeStruct((rows, width), bf16),
            jax.ShapeDtypeStruct((all_rows, width), bf16),
            jax.ShapeDtypeStruct((all_rows, side), bf16),
        ],
        in_specs=[pl.BlockSpec(memory_space=pltpu.VMEM)] * 6 + [pl.BlockSpec(memory_space=pl.ANY)] * 4,
        out_specs=[pl.BlockSpec(memory_space=pltpu.VMEM)] + [pl.BlockSpec(memory_space=pl.ANY)] * 2,
        scratch_shapes=[
            pltpu.VMEM((rows, width), bf16),
            pltpu.VMEM((rows, 2 * width), bf16),
            pltpu.VMEM((2 * width, 2 * w_key.shape[1]), bf16),
            pltpu.VMEM((4, 2 * width, 2 * HS), bf16),
            pltpu.VMEM((4, w_out.shape[0], width // 4), bf16),
            pltpu.VMEM((all_rows, 2 * w_key.shape[1]), bf16),
            pltpu.VMEM(stacked, bf16),
            pltpu.VMEM(stacked, f32),
            pltpu.VMEM(stacked, f32),
            pltpu.VMEM(stacked, f32),
            pltpu.VMEM((rows, w_out.shape[0]), bf16),
            pltpu.VMEM((rows, width), f32),
            pltpu.VMEM((rows, width), bf16),
            pltpu.VMEM((rows, width), bf16),
            pltpu.VMEM((rows, rows), f32),
        ]
        + [dma((chips, SUBS))] * 12
        + [dma((SUBS,))] * 2
        + [dma((4,))] * 2
        + [dma((1,)), dma((2,)), dma((4,)), dma((4,))],
        compiler_params=pltpu.CompilerParams(
            collective_id=call_id, has_side_effects=True, vmem_limit_bytes=VMEM_LIMIT
        ),
        name="front",
    )(hidden_in, norm_gain, cosine, sine, doc_ids, query_doc, w_query, w_key, w_value, w_out)


def on_pairs(hidden_in, norm_gain, w_query, w_key, w_value, w_out, doc_ids):
    rows = hidden_in.shape[0]
    first_row = lax.axis_index("tok") * rows
    positions = (first_row + jnp.arange(rows, dtype=jnp.int32)) % doc_ids.shape[0]
    lane = jnp.arange(HS, dtype=jnp.int32)
    pair = (lane % (HS // 2)).astype(jnp.float32)
    inv_freq = rope_base ** (-(pair * 2.0) / HS)
    angles = positions.astype(jnp.float32)[:, None] * inv_freq[None, :]
    sine = jnp.sin(angles) * jnp.where(lane < HS // 2, -1.0, 1.0)[None, :]
    query_doc = lax.dynamic_slice_in_dim(doc_ids, first_row, rows, 0)
    hidden_out, cols_in, rows_in = front(
        hidden_in, norm_gain[None, :], jnp.cos(angles), sine, doc_ids[None, :],
        jnp.broadcast_to(query_doc[:, None], (rows, 128)), w_query, w_key, w_value, w_out, 0,
    )
    return (hidden_out, joint_cov(hidden_out, rows_in, cols_in, 1))


def on_device(hidden_in, norm_gain, w_query, w_key, w_value, w_out, doc_ids):
    tok_rows, col_width = hidden_in.shape
    tok_count = lax.axis_size("tok")
    tp_count = lax.axis_size("tp")
    if tp_count == 2:
        return on_pairs(hidden_in, norm_gain, w_query, w_key, w_value, w_out, doc_ids)
    tok_index = lax.axis_index("tok")
    all_rows = tok_rows * tok_count
    full_in = both_sides(hidden_in)
    widened = full_in.astype(jnp.float32)
    factor = lax.rsqrt(jnp.mean(widened * widened, axis=1, keepdims=True) + epsilon)
    normed = (widened * factor * norm_gain[None, :]).astype(jnp.bfloat16)
    kv_heads = w_key.shape[1] // HS
    groups = w_query.shape[1] // w_key.shape[1]
    first_row = tok_index * tok_rows
    positions = first_row + jnp.arange(tok_rows, dtype=jnp.int32)
    key_local = rotate(
        jnp.dot(normed, w_key, preferred_element_type=jnp.float32).reshape(tok_rows, kv_heads, HS),
        positions % all_rows,
    )
    key_local = key_local.astype(jnp.bfloat16).reshape(tok_rows, kv_heads * HS)
    value_local = jnp.dot(normed, w_value, preferred_element_type=jnp.float32).astype(jnp.bfloat16)
    (kv_rows,) = ring_gather(jnp.stack([key_local, value_local]), False, 0)
    early, late = hidden_in[:, : col_width // 2], hidden_in[:, col_width // 2 :]
    late, kv_rows = lax.optimization_barrier((late, kv_rows))
    cols_in = [lax.all_gather(part, "tok", axis=0, tiled=True) for part in (early, late)]
    rows_in = lax.all_to_all(full_in, "tok", 1, 0, tiled=True)
    queries = rotate(
        jnp.dot(normed, w_query, preferred_element_type=jnp.float32).reshape(
            tok_rows, kv_heads * groups, HS
        ),
        positions % all_rows,
    )
    queries = queries.astype(jnp.bfloat16).reshape(tok_rows, kv_heads * groups * HS)
    query_doc = lax.dynamic_slice_in_dim(doc_ids, first_row, tok_rows, 0)
    lo = jnp.sum((doc_ids[None, :] < query_doc[:, None]).astype(jnp.int32), axis=1)
    bounds = jnp.stack([first_row.astype(jnp.int32), lo[0]])
    attended = attend(queries, kv_rows, jnp.broadcast_to(lo[:, None], (tok_rows, 128)), bounds, kv_heads)
    partial_out = jnp.dot(attended, w_out, preferred_element_type=jnp.float32)
    summed = lax.psum_scatter(partial_out, "tp", scatter_dimension=1, tiled=True)
    hidden_out = (hidden_in.astype(jnp.float32) + summed).astype(jnp.bfloat16)
    halves = jnp.stack([hidden_out[:, : col_width // 2], hidden_out[:, col_width // 2 :]])
    (cols_out,) = ring_gather(halves, False, 1)
    rows_out = row_features(cols_out, None)
    return (hidden_out, joint_gram(rows_in, rows_out, cols_in, cols_out))


def solution(mesh):
    return jax.shard_map(
        on_device,
        mesh=mesh,
        in_specs=(
            P("tok", "tp"),
            P(),
            P(None, "tp"),
            P(None, "tp"),
            P(None, "tp"),
            P("tp", None),
            P(),
        ),
        out_specs=(P("tok", "tp"), P(None, "tok", None, "tp")),
        check_vma=False,
    )
```

```python
import functools
import math

import jax
import jax.numpy as jnp
from jax import lax
from jax.experimental import pallas as pl
from jax.experimental.pallas import tpu as pltpu
from jax.sharding import PartitionSpec as P

HS = 128
epsilon = 1e-05
rope_base = 500000.0
VMEM_LIMIT = 60 * 1024 * 1024


def rotate(vectors, positions):
    half_dim = vectors.shape[-1] // 2
    inv_freq = rope_base ** (-(jnp.arange(half_dim, dtype=jnp.float32) * 2.0) / vectors.shape[-1])
    angles = positions.astype(jnp.float32)[:, None] * inv_freq[None, :]
    cosine = jnp.cos(angles)[:, None, :]
    sine_part = jnp.sin(angles)[:, None, :]
    first_half = vectors[..., :half_dim]
    second_half = vectors[..., half_dim:]
    return jnp.concatenate(
        [
            first_half * cosine - second_half * sine_part,
            second_half * cosine + first_half * sine_part,
        ],
        axis=-1,
    )


def attend_kernel(groups, block, bounds, q_ref, k_ref, v_ref, lo_ref, out_ref, s_ref, m_ref, l_ref, acc_ref):
    rows = q_ref.shape[0]
    first_row = bounds[0]
    scale = HS ** (-0.5) * math.log2(math.e)
    start = bounds[1] // block
    stop = (first_row + rows + block - 1) // block
    lanes = 128
    m_ref[...] = jnp.full_like(m_ref, -jnp.inf)
    l_ref[...] = jnp.zeros_like(l_ref)
    acc_ref[...] = jnp.zeros_like(acc_ref)

    @pl.loop(start, stop)
    def _(step):
        first_key = pl.multiple_of(step * block, block)
        keys = k_ref[pl.ds(first_key, block), :]
        key_pos = first_key + lax.broadcasted_iota(jnp.int32, (rows, block), 1)
        query_pos = first_row + lax.broadcasted_iota(jnp.int32, (rows, block), 0)
        allowed = (key_pos >= lo_ref[:, :1]) & (key_pos <= query_pos)
        for head in range(groups):
            part = pl.ds(head * rows, rows)
            s = lax.dot_general(
                q_ref[:, head * HS:(head + 1) * HS], keys,
                (((1,), (1,)), ((), ())), preferred_element_type=jnp.float32,
            ) * scale
            s = jnp.where(allowed, s, -jnp.inf)
            s_ref[step, part, :] = s
            top = m_ref[part, :]
            for piece in range(block // lanes):
                top = jnp.maximum(top, s[:, piece * lanes:(piece + 1) * lanes])
            m_ref[part, :] = top

    m_ref[...] = jnp.broadcast_to(jnp.max(m_ref[...], axis=-1, keepdims=True), m_ref.shape)

    @pl.loop(start, stop)
    def _(step):
        first_key = pl.multiple_of(step * block, block)
        values = v_ref[pl.ds(first_key, block), :]
        for head in range(groups):
            part = pl.ds(head * rows, rows)
            weights = jnp.exp2(s_ref[step, part, :] - m_ref[part, :1])
            total = l_ref[part, :]
            for piece in range(block // lanes):
                total = total + weights[:, piece * lanes:(piece + 1) * lanes]
            l_ref[part, :] = total
            acc_ref[part, :] += jnp.dot(
                weights.astype(jnp.bfloat16), values, preferred_element_type=jnp.float32
            )

    for head in range(groups):
        part = pl.ds(head * rows, rows)
        weight_sum = jnp.sum(l_ref[part, :], axis=-1, keepdims=True)
        out_ref[:, head * HS:(head + 1) * HS] = (acc_ref[part, :] / weight_sum).astype(out_ref.dtype)


def attend(queries, kv_rows, lo, bounds, kv_heads):
    rows, width = queries.shape
    all_rows = kv_rows.shape[1]
    groups = width // (kv_heads * HS)
    block = min(512, all_rows)
    wide = groups * HS
    return pl.pallas_call(
        functools.partial(attend_kernel, groups, block),
        out_shape=jax.ShapeDtypeStruct((rows, width), jnp.bfloat16),
        grid_spec=pltpu.PrefetchScalarGridSpec(
            num_scalar_prefetch=1,
            grid=(kv_heads,),
            in_specs=[
                pl.BlockSpec((rows, wide), lambda g, b: (0, g)),
                pl.BlockSpec((None, all_rows, HS), lambda g, b: (0, 0, g)),
                pl.BlockSpec((None, all_rows, HS), lambda g, b: (1, 0, g)),
                pl.BlockSpec((rows, 128), lambda g, b: (0, 0)),
            ],
            out_specs=pl.BlockSpec((rows, wide), lambda g, b: (0, g)),
            scratch_shapes=[
                pltpu.VMEM((all_rows // block, groups * rows, block), jnp.float32),
                pltpu.VMEM((groups * rows, 128), jnp.float32),
                pltpu.VMEM((groups * rows, 128), jnp.float32),
                pltpu.VMEM((groups * rows, HS), jnp.float32),
            ],
        ),
        compiler_params=pltpu.CompilerParams(
            dimension_semantics=("arbitrary",), vmem_limit_bytes=VMEM_LIMIT
        ),
        cost_estimate=pl.CostEstimate(
            flops=4 * rows * all_rows * width,
            bytes_accessed=2 * all_rows * kv_heads * HS * 2 + 4 * rows * width,
            transcendentals=rows * all_rows * width // HS,
        ),
        name="attend",
    )(bounds, queries, kv_rows, kv_rows, lo)


def gram_kernel(strips, rin_ref, rout_ref, low_ref, high_ref, cout_ref, out_ref, rt_ref, mean_ref):
    all_rows, row_width = rin_ref.shape

    @pl.when(pl.program_id(0) == 0)
    def _():
        ones = jnp.ones((all_rows, 128), jnp.bfloat16)
        for source, ref in enumerate((rin_ref, rout_ref)):
            part = pl.ds(source * row_width, row_width)
            rt_ref[part, :] = ref[...].T
            mean_ref[part, :] = (
                jnp.dot(rt_ref[part, :], ones, preferred_element_type=jnp.float32) / all_rows
            )

    ones = jnp.ones((8, all_rows), jnp.bfloat16)

    def block(source, ref):
        cols = ref[...]
        col_mean = jnp.dot(ones, cols, preferred_element_type=jnp.float32)[:1] / all_rows
        gram = jnp.dot(rt_ref[...], cols, preferred_element_type=jnp.float32)
        cov = gram / all_rows - mean_ref[:, :1] * col_mean
        for row_source in range(2):
            out_ref[row_source, :, source, :] = cov[row_source * row_width:(row_source + 1) * row_width]

    @pl.when(pl.program_id(0) < strips)
    def _():
        block(0, low_ref)

    @pl.when(pl.program_id(0) >= strips)
    def _():
        block(0, high_ref)

    block(1, cout_ref)


def joint_gram(rin, rout, cin, cout):
    all_rows, row_width = rin.shape
    half = cout.shape[2]
    col_width = 2 * half
    tile = min(256, half)
    strips = half // tile
    whole = pl.BlockSpec((all_rows, row_width), lambda j: (0, 0), pipeline_mode=pl.Buffered(1))
    strip = pl.BlockSpec((None, all_rows, tile), lambda j: (j // strips, 0, j % strips))
    low = pl.BlockSpec((all_rows, tile), lambda j: (0, jnp.minimum(j, strips - 1)))
    high = pl.BlockSpec((all_rows, tile), lambda j: (0, jnp.maximum(j - strips, 0)))
    return pl.pallas_call(
        functools.partial(gram_kernel, strips),
        out_shape=jax.ShapeDtypeStruct((2, row_width, 2, col_width), jnp.float32),
        grid=(col_width // tile,),
        in_specs=[whole, whole, low, high, strip],
        out_specs=pl.BlockSpec((2, row_width, 2, tile), lambda j: (0, 0, 0, j)),
        scratch_shapes=[
            pltpu.VMEM((2 * row_width, all_rows), jnp.bfloat16),
            pltpu.VMEM((2 * row_width, 128), jnp.float32),
        ],
        compiler_params=pltpu.CompilerParams(
            dimension_semantics=("arbitrary",), vmem_limit_bytes=VMEM_LIMIT
        ),
        cost_estimate=pl.CostEstimate(
            flops=8 * all_rows * row_width * col_width,
            bytes_accessed=4 * all_rows * (row_width + col_width) + 16 * row_width * col_width,
            transcendentals=0,
        ),
        name="joint_gram",
    )(rin, rout, *cin, cout)


def both_sides(block):
    if lax.axis_size("tp") != 2:
        return lax.all_gather(block, "tp", axis=1, tiled=True)
    other = lax.ppermute(block, "tp", ((0, 1), (1, 0)))
    first = lax.axis_index("tp") == 0
    return jnp.concatenate([jnp.where(first, block, other), jnp.where(first, other, block)], axis=1)


def ring_kernel(chips, share, x_ref, *refs):
    if share:
        out_ref, side_ref, send, recv, psend, precv, local, ssend, srecv = refs
    else:
        out_ref, send, recv, psend, precv, local = refs
    mesh_id = pl.DeviceIdType.MESH
    rows = x_ref.shape[1]
    me, tp = lax.axis_index("tok"), lax.axis_index("tp")
    count = 2 * chips
    core, chip = me % 2, me // 2
    depth = chips // 2
    spot = jnp.where(chip % 2 == 0, chip // 2, chips - 1 - chip // 2)

    def device(place):
        place = (place + 2 * chips) % chips
        return jnp.where(place < depth, place * 4, (chips - 1 - place) * 4 + 2) + core

    partner = me + 1 - 2 * core
    ways = (device(spot + 1), device(spot - 1))
    barrier = pltpu.get_barrier_semaphore()
    for peer in (*ways, partner):
        pl.semaphore_signal(barrier, inc=1, device_id={"tok": peer}, device_id_type=mesh_id)
    if share:
        pl.semaphore_signal(barrier, inc=1, device_id={"tp": 1 - tp}, device_id_type=mesh_id)
    pl.semaphore_wait(barrier, 4 if share else 3)

    def block(way, origin):
        return out_ref.at[way, pl.ds(pl.multiple_of(origin * rows, rows), rows), :]

    pending = []

    def step_copies(step, way):
        origin = device(spot - step if way == 0 else spot + step)
        source = x_ref.at[way] if step == 0 else block(way, origin)
        ring = None
        if step < chips - 1:
            ring = pltpu.make_async_remote_copy(
                src_ref=source, dst_ref=block(way, origin), send_sem=send.at[way, step],
                recv_sem=recv.at[way, step], device_id={"tok": ways[way]}, device_id_type=mesh_id,
            )
            ring.start()
        beside = pltpu.make_async_remote_copy(
            src_ref=source, dst_ref=block(way, origin), send_sem=psend.at[way, step],
            recv_sem=precv.at[way, step], device_id={"tok": partner}, device_id_type=mesh_id,
        )
        beside.start()
        pending.append((ring, beside))
        return ring

    rings = [step_copies(0, way) for way in range(2)]
    own = [pltpu.make_async_copy(x_ref.at[way], block(way, me), local.at[way]) for way in range(2)]
    for copy in own:
        copy.start()
    if share:
        width = side_ref.shape[1]
        half = x_ref.shape[2]
        owner = me // (count // 2)
        my_way = me * width % (2 * half) // half
        features = pl.ds(pl.multiple_of(me * width % half, width), width)

    def side_copy(step, way, kind):
        origin = device(spot - step if way == 0 else spot + step)
        origin = origin + kind * (1 - 2 * core)
        source = x_ref.at[way, :, features]
        if step > 0 or kind > 0:
            source = out_ref.at[way, pl.ds(pl.multiple_of(origin * rows, rows), rows), features]
        return pltpu.make_async_remote_copy(
            src_ref=source,
            dst_ref=side_ref.at[pl.ds(pl.multiple_of(origin * rows, rows), rows), :],
            send_sem=ssend.at[kind, step], recv_sem=srecv.at[kind, step],
            device_id={"tp": 1 - tp}, device_id_type=mesh_id,
        )

    def each_side(act, step, way, kind, holder):
        if share:
            @pl.when((my_way == way) & ((owner == tp) == holder))
            def _():
                act(side_copy(step, way, kind))

    def start(copy):
        copy.start()

    for way in range(2):
        each_side(start, 0, way, 0, True)
    for step in range(1, chips):
        for way in range(2):
            rings[way].wait_recv()
            rings[way] = step_copies(step, way)
            each_side(start, step, way, 0, True)
            pending[2 * (step - 1) + way][1].wait_recv()
            each_side(start, step - 1, way, 1, True)
    for way in range(2):
        pending[2 * (chips - 1) + way][1].wait_recv()
        each_side(start, chips - 1, way, 1, True)
    for ring, beside in pending:
        if ring is not None:
            ring.wait_send()
        beside.wait_send()
    for copy in own:
        copy.wait()
    for step in range(chips):
        for way in range(2):
            for kind in range(2):
                each_side(lambda copy: copy.wait_send(), step, way, kind, True)
                each_side(lambda copy: copy.wait_recv(), step, way, kind, False)


def ring_gather(halves, share, call_id):
    _, rows, width = halves.shape
    count = lax.axis_size("tok")
    chips = count // 2
    out_shape = [jax.ShapeDtypeStruct((2, rows * count, width), halves.dtype)]
    dma = pltpu.SemaphoreType.DMA
    scratch = [dma((2, chips))] * 4 + [dma((2,))]
    if share:
        out_shape.append(jax.ShapeDtypeStruct((rows * count, 4 * width // count), halves.dtype))
        scratch += [dma((2, chips))] * 2
    return pl.pallas_call(
        functools.partial(ring_kernel, chips, share),
        out_shape=out_shape,
        in_specs=[pl.BlockSpec(memory_space=pltpu.VMEM)],
        out_specs=[pl.BlockSpec(memory_space=pl.ANY)] * len(out_shape),
        scratch_shapes=scratch,
        compiler_params=pltpu.CompilerParams(
            collective_id=call_id, has_side_effects=True, vmem_limit_bytes=VMEM_LIMIT
        ),
        cost_estimate=pl.CostEstimate(
            flops=40_000_000_000, bytes_accessed=2 * halves.size * count * 2, transcendentals=0
        ),
        name="ring_share" if share else "ring",
    )(halves)


def row_features(columns, arrived):
    _, all_rows, half = columns.shape
    row_width = 2 * half * lax.axis_size("tp") // lax.axis_size("tok")
    first = lax.axis_index("tok") * row_width
    offset, owner = first % (2 * half), first // (2 * half)
    mine = lax.dynamic_slice(columns, (offset // half, 0, offset % half), (1, all_rows, row_width))[0]
    owned = lax.axis_index("tp") == owner
    if arrived is None:
        return lax.psum(jnp.where(owned, mine, jnp.zeros_like(mine)), "tp")
    return jnp.where(owned, mine, arrived)


SUBS = 2
SIDE_STEPS = 6
COV_SUBS = 2
MESH = pl.DeviceIdType.MESH


def ring_place(chips):
    me, tp = lax.axis_index("tok"), lax.axis_index("tp")
    core, chip = me % 2, me // 2
    spot = jnp.where(chip % 2 == 0, chip // 2, chips - 1 - chip // 2)

    def chip_at(place):
        place = (place + 2 * chips) % chips
        return jnp.where(place < chips // 2, place * 2, (chips - 1 - place) * 2 + 1)

    ahead = 1 - 2 * core
    return me, tp, core, spot, chip_at, ahead, chips


class Ring:
    def __init__(self, place, big, own, subs, sems, far=None, side=None, side_sems=None):
        self.me, self.tp, self.core, self.spot, self.chip_at, self.ahead, self.chips = place
        self.big, self.own, self.subs = big, own, subs
        self.rows = big.shape[0] // (2 * self.chips)
        self.part = self.rows // subs
        self.send, self.recv, self.psend, self.precv = sems
        self.far, self.side = far, side
        self.partner = self.me + 1 - 2 * self.core
        self.onward = self.chip_at(self.spot + self.ahead) * 2 + self.core
        self.back = self.chip_at(self.spot - self.ahead) * 2 + self.core
        if far is not None:
            self.ssend, self.srecv, self.tsend, self.trecv = side_sems
            width = big.shape[1]
            self.owner = self.me * side // width == self.tp
            self.feature = pl.multiple_of(self.me * side % width, side)
            self.partner_feature = pl.multiple_of(self.partner * side % width, side)

    def block(self, step, mine):
        turn = self.ahead if mine else -self.ahead
        return self.chip_at(self.spot - turn * step) * 2 + (self.core if mine else 1 - self.core)

    def block_row(self, step, mine):
        return pl.multiple_of(self.block(step, mine) * self.rows, self.rows)

    def span(self, step, sub):
        return pl.ds(pl.multiple_of(self.block_row(step, True) + sub * self.part, self.part), self.part)

    def source(self, step, sub):
        if self.own is not None and isinstance(step, int) and step == 0:
            return self.own.at[pl.ds(sub * self.part, self.part)]
        return self.big.at[self.span(step, sub)]

    def ring_copy(self, step, sub):
        return pltpu.make_async_remote_copy(
            src_ref=self.source(step, sub), dst_ref=self.big.at[self.span(step, sub)],
            send_sem=self.send.at[step, sub], recv_sem=self.recv.at[step, sub],
            device_id={"tok": self.onward}, device_id_type=MESH,
        )

    def beside_copy(self, step, sub):
        return pltpu.make_async_remote_copy(
            src_ref=self.source(step, sub), dst_ref=self.big.at[self.span(step, sub)],
            send_sem=self.psend.at[step, sub], recv_sem=self.precv.at[step, sub],
            device_id={"tok": self.partner}, device_id_type=MESH,
        )

    def side_copy(self, step, sub, same):
        wanted, target = (self.feature, self.me) if same else (self.partner_feature, self.partner)
        out_sem, in_sem = (self.ssend, self.srecv) if same else (self.tsend, self.trecv)
        return pltpu.make_async_remote_copy(
            src_ref=self.source(step, sub).at[:, pl.ds(wanted, self.side)],
            dst_ref=self.far.at[self.span(step, sub), :],
            send_sem=out_sem.at[step, sub], recv_sem=in_sem.at[step, sub],
            device_id={"tok": target, "tp": 1 - self.tp}, device_id_type=MESH,
        )

    def launch(self, step, sub):
        if isinstance(step, int):
            if step < self.chips - 1:
                self.ring_copy(step, sub).start()
        else:
            @pl.when(step < self.chips - 1)
            def _():
                self.ring_copy(step, sub).start()
        self.beside_copy(step, sub).start()

    def launch_side(self, step, sub):
        @pl.when(self.owner)
        def _():
            for same in (True, False):
                self.side_copy(step, sub, same).start()

    def event(self, step, sub):
        self.ring_copy(step - 1, sub).wait_recv()
        self.launch(step, sub)

    def beside_arrived(self, step):
        for sub in range(self.subs):
            self.beside_copy(step, sub).wait_recv()

    def side_arrived(self, step, mine):
        @pl.when(jnp.logical_not(self.owner))
        def _():
            for sub in range(self.subs):
                self.side_copy(step, sub, mine).wait_recv()

    def drain(self, side_steps=0):
        for step in range(self.chips):
            for sub in range(self.subs):
                if step < self.chips - 1:
                    self.ring_copy(step, sub).wait_send()
                self.beside_copy(step, sub).wait_send()
                if step < side_steps:
                    @pl.when(self.owner)
                    def _():
                        for same in (True, False):
                            self.side_copy(step, sub, same).wait_send()


def greet(ring):
    barrier = pltpu.get_barrier_semaphore()
    for peer in (ring.onward, ring.back, ring.partner):
        pl.semaphore_signal(barrier, inc=1, device_id={"tok": peer}, device_id_type=MESH)
    for peer in (ring.me, ring.partner):
        pl.semaphore_signal(
            barrier, inc=1, device_id={"tok": peer, "tp": 1 - ring.tp}, device_id_type=MESH
        )
    pl.semaphore_wait(barrier, 5)


def cov_kernel(chips, x_ref, cin_ref, rin_ref, *refs):
    acc_ref, rsum_ref, big, far, lt, cbuf, rbuf, late = refs[:8]
    sems, side_sems = refs[8:12], refs[12:16]
    own_sem, cin_sem, rin_sem, lsend, lrecv, ones_r = refs[16:]
    ring = Ring(ring_place(chips), big, x_ref, COV_SUBS, sems, far, rin_ref.shape[1], side_sems)
    rows, width = x_ref.shape
    side = ring.side
    owner = ring.owner
    greet(ring)
    for sub in range(COV_SUBS):
        ring.launch(0, sub)
        ring.launch_side(0, sub)
    own = pltpu.make_async_copy(x_ref, big.at[pl.ds(pl.multiple_of(ring.me * rows, rows), rows)], own_sem.at[0])
    own.start()

    def slot_of(step, mine):
        return step % 2 * 2 + (0 if mine else 1)

    def fetch_cols(step, mine):
        slot = slot_of(step, mine)
        place = pl.ds(ring.block_row(step, mine), rows)
        return pltpu.make_async_copy(cin_ref.at[place, :], cbuf.at[slot], cin_sem.at[slot])

    def fetch_strip(step, mine):
        slot = slot_of(step, mine)
        place = pl.ds(ring.block_row(step, mine), rows)
        return pltpu.make_async_copy(rin_ref.at[place, :], rbuf.at[slot], rin_sem.at[slot])

    def late_copy(step, same):
        wanted, target = (ring.feature, ring.me) if same else (ring.partner_feature, ring.partner)
        slot = (step - SIDE_STEPS) * 2 + (0 if same else 1)
        return pltpu.make_async_remote_copy(
            src_ref=cin_ref.at[pl.ds(ring.block_row(step, True), rows), pl.ds(wanted, side)],
            dst_ref=late.at[slot], send_sem=lsend.at[slot], recv_sem=lrecv.at[slot],
            device_id={"tok": target, "tp": 1 - ring.tp}, device_id_type=MESH,
        )

    def start_fetch(step, mine):
        fetch_cols(step, mine).start()
        if step < SIDE_STEPS:
            @pl.when(jnp.logical_not(owner))
            def _():
                fetch_strip(step, mine).start()

    for step in range(2):
        for mine in (True, False):
            start_fetch(step, mine)

    ones_r[...] = jnp.ones_like(ones_r)
    lt[2 * side:, :] = jnp.ones((lt.shape[0] - 2 * side, rows), lt.dtype)
    acc_ref[...] = jnp.zeros_like(acc_ref)
    rsum_ref[...] = jnp.zeros_like(rsum_ref)
    own.wait()
    tile = min(512, width)

    def work(step, mine):
        if not mine:
            ring.beside_arrived(step)
        ring.side_arrived(step, mine)
        slot = slot_of(step, mine)
        place = pl.ds(ring.block_row(step, mine), rows)
        fetch_cols(step, mine).wait()

        @pl.when(owner)
        def _():
            lt[0:side, :] = cbuf[slot, :, pl.ds(ring.feature, side)].T
            lt[side:2 * side, :] = big[place, pl.ds(ring.feature, side)].T

        @pl.when(jnp.logical_not(owner))
        def _():
            if step < SIDE_STEPS:
                fetch_strip(step, mine).wait()
                lt[0:side, :] = rbuf[slot].T
            else:
                late_copy(step, mine).wait_recv()
                lt[0:side, :] = late[(step - SIDE_STEPS) * 2 + (0 if mine else 1)].T
            lt[side:2 * side, :] = far[place, :].T

        rsum_ref[...] += jnp.dot(lt[0:2 * side, :], ones_r[...], preferred_element_type=jnp.float32)

        @pl.loop(0, width // tile)
        def _(i):
            here = pl.ds(pl.multiple_of(i * tile, tile), tile)
            acc_ref[:, here] += jnp.dot(
                lt[...], cbuf[slot, :, here], preferred_element_type=jnp.float32
            )
            there = pl.ds(pl.multiple_of(width + i * tile, tile), tile)
            acc_ref[:, there] += jnp.dot(
                lt[...], big[place, here], preferred_element_type=jnp.float32
            )

        if step + 2 < chips:
            start_fetch(step + 2, mine)

    for step in range(1, chips):
        for sub in range(COV_SUBS):
            ring.event(step, sub)
            ring.launch_side(step, sub)
            if sub == 0 and 1 <= step <= chips - SIDE_STEPS:
                @pl.when(owner)
                def _():
                    for same in (True, False):
                        late_copy(SIDE_STEPS + step - 1, same).start()
            if sub == COV_SUBS // 2 - 1:
                work(step - 1, True)
            if sub == COV_SUBS - 1:
                work(step - 1, False)
    work(chips - 1, True)
    work(chips - 1, False)
    ring.drain(chips)

    @pl.when(owner)
    def _():
        for step in range(SIDE_STEPS, chips):
            for same in (True, False):
                late_copy(step, same).wait_send()


def finish_kernel(all_rows, width, upper_ref, lower_ref, csum_ref, rtop_ref, rlow_ref, x_ref, out_ref, y_ref):
    tall = upper_ref.shape[0]
    groups = 2 * width // 128
    part_of = 1.0 / all_rows
    y_ref[...] = x_ref[...]
    for row_source, (acc_ref, rsum_ref) in enumerate(((upper_ref, rtop_ref), (lower_ref, rlow_ref))):
        mean_row = rsum_ref[...] * part_of
        for source in range(2):
            for j in range(width // 128):
                part = slice(source * width + j * 128, source * width + (j + 1) * 128)
                mean_col = csum_ref[0:1, part] * part_of
                out_ref[row_source, pl.ds(2 * j + source, tall, stride=groups), :] = (
                    acc_ref[:, part] * part_of - mean_row * mean_col
                )


def joint_cov(hidden_out, rows_in, cols_in, call_id):
    rows, width = hidden_out.shape
    all_rows, side = rows_in.shape
    chips = all_rows // rows // 2
    dma = pltpu.SemaphoreType.DMA
    tall = 2 * side + 16
    acc, rsum = pl.pallas_call(
        functools.partial(cov_kernel, chips),
        out_shape=[
            jax.ShapeDtypeStruct((tall, 2 * width), jnp.float32),
            jax.ShapeDtypeStruct((2 * side, 128), jnp.float32),
        ],
        in_specs=[pl.BlockSpec(memory_space=pltpu.VMEM)]
        + [pl.BlockSpec(memory_space=pl.ANY)] * 2,
        out_specs=[pl.BlockSpec(memory_space=pltpu.VMEM)] * 2,
        scratch_shapes=[
            pltpu.VMEM((all_rows, width), jnp.bfloat16),
            pltpu.VMEM((all_rows, side), jnp.bfloat16),
            pltpu.VMEM((tall, rows), jnp.bfloat16),
            pltpu.VMEM((4, rows, width), jnp.bfloat16),
            pltpu.VMEM((4, rows, side), jnp.bfloat16),
            pltpu.VMEM((2 * (chips - SIDE_STEPS), rows, side), jnp.bfloat16),
        ]
        + [dma((chips, COV_SUBS))] * 8
        + [dma((1,)), dma((4,)), dma((4,))]
        + [dma((2 * (chips - SIDE_STEPS),))] * 2
        + [pltpu.VMEM((rows, 128), jnp.bfloat16)],
        compiler_params=pltpu.CompilerParams(
            collective_id=call_id, has_side_effects=True, vmem_limit_bytes=38 * 1024 * 1024
        ),
        cost_estimate=pl.CostEstimate(
            flops=8 * all_rows * side * width * 4,
            bytes_accessed=4 * all_rows * (side + width) + 16 * side * width,
            transcendentals=0,
        ),
        name="cov_ring",
    )(hidden_out, cols_in, rows_in)
    cov, settled = finish(acc, rsum, hidden_out, side)
    return settled, cov


def finish(acc, rsum, hidden_out, side):
    rows, width = hidden_out.shape
    all_rows = rows * lax.axis_size("tok")
    strips = 8
    tall = side // strips
    groups = 2 * width // 128
    cov, settled = pl.pallas_call(
        functools.partial(finish_kernel, all_rows, width),
        out_shape=[
            jax.ShapeDtypeStruct((2, side * groups, 128), jnp.float32),
            jax.ShapeDtypeStruct(hidden_out.shape, hidden_out.dtype),
        ],
        grid=(strips,),
        in_specs=[
            pl.BlockSpec((tall, 2 * width), lambda i: (i, 0)),
            pl.BlockSpec((tall, 2 * width), lambda i: (strips + i, 0)),
            pl.BlockSpec((8, 2 * width), lambda i: (2 * side // 8, 0)),
            pl.BlockSpec((tall, 128), lambda i: (i, 0)),
            pl.BlockSpec((tall, 128), lambda i: (strips + i, 0)),
            pl.BlockSpec((rows // strips, width), lambda i: (i, 0)),
        ],
        out_specs=[
            pl.BlockSpec((2, tall * groups, 128), lambda i: (0, i, 0)),
            pl.BlockSpec((rows // strips, width), lambda i: (i, 0)),
        ],
        compiler_params=pltpu.CompilerParams(
            dimension_semantics=("arbitrary",), vmem_limit_bytes=8 * 1024 * 1024
        ),
        name="finish",
    )(acc, acc, acc, rsum, rsum, hidden_out)
    cov = cov.reshape(2, side, width // 128, 2, 128).transpose(0, 1, 3, 2, 4)
    return cov.reshape(2, side, 2, width), settled


NEG = -1e30


def front_kernel(
    chips, kv_heads, groups, x_ref, gain_ref, cos_ref, sin_ref, kdoc_ref,
    wq_ref, wk_ref, wv_ref, wo_ref, out_ref, cin, far, other, normed, wkv, wq, wo, kv, q_ref,
    m_ref, l_ref, acc_ref, att, mine_sum, sent, arrived, bias, qdoc_ref, *sems
):
    place = ring_place(chips)
    hid_sems, side_sems, kv_sems = sems[0:4], sems[4:8], sems[8:12]
    xsend, xrecv, osend, orecv, own_sem, wkv_sem, wq_sem, wo_sem = sems[12:]
    rows, width = x_ref.shape
    side = far.shape[1]
    hid = Ring(place, cin, x_ref, SUBS, hid_sems, far, side, side_sems)
    ring = Ring(place, kv, None, SUBS, kv_sems)
    me, tp = hid.me, hid.tp
    half = rows // SUBS
    kv_width = kv_heads * HS
    scale = HS ** (-0.5) * math.log2(math.e)
    head_pair = 2 * HS
    q_tiles = kv_heads * groups // 2
    out_tile = width // 4

    def swap(sub):
        part = pl.ds(sub * half, half)
        return pltpu.make_async_remote_copy(
            src_ref=x_ref.at[part], dst_ref=other.at[part], send_sem=xsend.at[sub],
            recv_sem=xrecv.at[sub], device_id={"tp": 1 - tp}, device_id_type=MESH,
        )

    def fetch_q(t):
        col = pl.ds(pl.multiple_of(t * head_pair, head_pair), head_pair)
        return pltpu.make_async_copy(wq_ref.at[:, col], wq.at[t % 4], wq_sem.at[t % 4])

    def fetch_out(side_tp, i):
        col = pl.ds(pl.multiple_of(side_tp * width + i * out_tile, out_tile), out_tile)
        return pltpu.make_async_copy(wo_ref.at[:, col], wo.at[i], wo_sem.at[i])

    def out_part(i):
        return pl.ds(pl.multiple_of(i * out_tile, out_tile), out_tile)

    def give(i):
        return pltpu.make_async_remote_copy(
            src_ref=sent.at[:, out_part(i)], dst_ref=arrived.at[:, out_part(i)],
            send_sem=osend.at[i], recv_sem=orecv.at[i],
            device_id={"tp": 1 - tp}, device_id_type=MESH,
        )

    keys = [
        pltpu.make_async_copy(ref, wkv.at[:, pl.ds(i * kv_width, kv_width)], wkv_sem.at[i])
        for i, ref in enumerate((wk_ref, wv_ref))
    ]
    for copy in keys:
        copy.start()
    greet(hid)
    for sub in range(SUBS):
        swap(sub).start()
        hid.launch(0, sub)
    own = pltpu.make_async_copy(x_ref, cin.at[pl.ds(pl.multiple_of(me * rows, rows), rows)], own_sem.at[0])
    own.start()
    for t in range(4):
        fetch_q(t).start()
    for i in range(4):
        fetch_out(1 - tp, i).start()

    @pl.loop(0, kv_heads)
    def _(g):
        m_ref[g] = jnp.full(m_ref.shape[1:], NEG, jnp.float32)
        l_ref[g] = jnp.zeros(l_ref.shape[1:], jnp.float32)
        acc_ref[g] = jnp.zeros(acc_ref.shape[1:], jnp.float32)

    my_doc = kdoc_ref[:, pl.ds(pl.multiple_of(me * rows, rows), rows)]
    qdoc_ref[...] = jnp.broadcast_to(my_doc, (128, rows)).T
    my_cols = pl.ds(pl.multiple_of(tp * width, width), width)
    other_cols = pl.ds(pl.multiple_of((1 - tp) * width, width), width)

    def normalise(sub):
        @pl.loop(0, half // 32)
        def _(r):
            part = pl.ds(pl.multiple_of(sub * half + r * 32, 32), 32)
            near = x_ref[part, :].astype(jnp.float32)
            away = other[part, :].astype(jnp.float32)
            total = jnp.sum(near * near, axis=1, keepdims=True) + jnp.sum(away * away, axis=1, keepdims=True)
            factor = lax.rsqrt(total / (2 * width) + epsilon)
            normed[part, my_cols] = (near * factor * gain_ref[:, my_cols]).astype(jnp.bfloat16)
            normed[part, other_cols] = (away * factor * gain_ref[:, other_cols]).astype(jnp.bfloat16)

    def turned(vectors):
        return vectors * cos_ref[...] + pltpu.roll(vectors, HS // 2, 1) * sin_ref[...]

    hid.event(1, 0)
    hid.event(1, 1)
    swap(0).wait_recv()
    normalise(0)
    hid.event(2, 0)
    hid.event(2, 1)
    swap(1).wait_recv()
    normalise(1)
    for copy in keys:
        copy.wait()
    my_base = pl.multiple_of(me * 2 * kv_width, 2 * kv_width)

    @pl.loop(0, kv_width // head_pair)
    def _(t):
        col = pl.multiple_of(t * head_pair, head_pair)
        found = jnp.dot(normed[...], wkv[:, pl.ds(col, head_pair)], preferred_element_type=jnp.float32)
        for j in range(2):
            piece = turned(found[:, j * HS:(j + 1) * HS])
            kv[pl.ds(pl.multiple_of(my_base + col + j * HS, HS), HS), :] = piece.T.astype(jnp.bfloat16)


    @pl.loop(0, kv_width // head_pair)
    def _(t):
        col = pl.multiple_of(kv_width + t * head_pair, head_pair)
        found = jnp.dot(normed[...], wkv[:, pl.ds(col, head_pair)], preferred_element_type=jnp.float32)
        kv[pl.ds(pl.multiple_of(my_base + col, head_pair), rows), :] = found.astype(jnp.bfloat16)

    for sub in range(SUBS):
        ring.launch(0, sub)
    for step in range(3):
        for sub in range(SUBS):
            hid.launch_side(step, sub)

    @pl.loop(0, q_tiles)
    def _(t):
        fetch_q(t).wait()
        found = jnp.dot(normed[...], wq[t % 4], preferred_element_type=jnp.float32)
        for j in range(2):
            head = t * 2 + j
            row = pl.multiple_of(head % groups * rows, rows)
            q_ref[head // groups, pl.ds(row, rows), :] = turned(found[:, j * HS:(j + 1) * HS]).astype(jnp.bfloat16)

        @pl.when(t + 4 < q_tiles)
        def _():
            fetch_q(t + 4).start()

        @pl.when(t == q_tiles // 2)
        def _():
            ring.event(1, 0)

    ring.event(1, 1)

    def make_bias(blocks):
        for i, block in enumerate(blocks):
            row = pl.multiple_of(block * rows, rows)
            key_pos = row + lax.broadcasted_iota(jnp.int32, (rows, rows), 1)
            query_pos = me * rows + lax.broadcasted_iota(jnp.int32, (rows, rows), 0)
            allowed = (kdoc_ref[:, pl.ds(row, rows)] == qdoc_ref[:, :1]) & (key_pos <= query_pos)
            bias[:, i * rows:(i + 1) * rows] = jnp.where(allowed, 0.0, NEG)

    def pair_attention(blocks, heads):
        @pl.loop(*heads)
        def _(g):
            k_row, v_row = g * HS, kv_width + g // 2 * rows
            v_col = pl.ds(pl.multiple_of(g % 2 * HS, HS), HS)
            k = jnp.concatenate(
                [kv[pl.ds(pl.multiple_of(b * 2 * kv_width + k_row, HS), HS), :] for b in blocks], axis=1
            )
            v = jnp.concatenate(
                [kv[pl.ds(pl.multiple_of(b * 2 * kv_width + v_row, rows), rows), v_col] for b in blocks],
                axis=0,
            )
            for head in range(groups):
                part = pl.ds(head * rows, rows)
                s = jnp.dot(q_ref[g, part, :], k, preferred_element_type=jnp.float32) * scale + bias[...]
                old = m_ref[g, part, :]
                pieces = [s[:, i:i + 128] for i in range(0, 2 * rows, 128)]
                peak = functools.reduce(jnp.maximum, pieces)
                top = jnp.maximum(old, jnp.max(peak, axis=-1, keepdims=True))
                fade = jnp.exp2(old - top)
                weights = [jnp.exp2(piece - top) for piece in pieces]
                l_ref[g, part, :] = l_ref[g, part, :] * fade + functools.reduce(jnp.add, weights)
                m_ref[g, part, :] = top
                acc_ref[g, part, :] = acc_ref[g, part, :] * fade + jnp.dot(
                    jnp.concatenate(weights, axis=1).astype(jnp.bfloat16), v,
                    preferred_element_type=jnp.float32,
                )

    @pl.loop(0, chips * SUBS)
    def _(turn):
        step, sub = turn // SUBS, turn % SUBS

        @pl.when(step + 2 < chips)
        def _():
            ring.event(step + 2, sub)


        @pl.when(step + 2 == chips - 1)
        def _():
            hid.event(3, sub)
            hid.launch_side(3, sub)

        @pl.when(step + 2 == chips + 1)
        def _():
            hid.event(4, sub)
            hid.launch_side(4, sub)

        blocks = (ring.block(step, True), ring.block(step, False))
        needed = (blocks[0] <= me) | (blocks[1] <= me)

        @pl.when(sub == 0)
        def _():
            ring.beside_arrived(step)

        @pl.when((sub == 0) & needed)
        def _():
            make_bias(blocks)

        @pl.when(needed)
        def _():
            pair_attention(blocks, (sub * (kv_heads // SUBS), (sub + 1) * (kv_heads // SUBS)))

    @pl.loop(0, kv_heads)
    def _(g):
        for head in range(groups):
            part = pl.ds(head * rows, rows)
            weight_sum = jnp.sum(l_ref[g, part, :], axis=-1, keepdims=True)
            col = pl.ds(pl.multiple_of((g * groups + head) * HS, HS), HS)
            att[:, col] = (acc_ref[g, part, :] / weight_sum).astype(jnp.bfloat16)

    @pl.loop(0, 4)
    def _(i):
        fetch_out(1 - tp, i).wait()
        found = jnp.dot(att[...], wo[i], preferred_element_type=jnp.float32)
        sent[:, out_part(i)] = found.astype(jnp.bfloat16)

        @pl.when(i > 0)
        def _():
            give(i - 1).start()

        fetch_out(tp, i).start()

    give(3).start()
    for i in range(2):
        hid.event(5, i)
        hid.launch_side(5, i)
    hid.event(6, 0)

    @pl.loop(0, 4)
    def _(i):
        fetch_out(tp, i).wait()
        mine_sum[:, out_part(i)] = jnp.dot(att[...], wo[i], preferred_element_type=jnp.float32)

    hid.event(6, 1)

    def settle(i):
        give(i).wait_recv()
        summed = mine_sum[:, out_part(i)] + arrived[:, out_part(i)].astype(jnp.float32)
        out_ref[:, out_part(i)] = (x_ref[:, out_part(i)].astype(jnp.float32) + summed).astype(jnp.bfloat16)

    pl.loop(0, 4)(settle)
    for sub in range(SUBS):
        hid.event(7, sub)
    own.wait()
    for step in range(chips):
        hid.beside_arrived(step)
        if step < SIDE_STEPS:
            for mine in (True, False):
                hid.side_arrived(step, mine)
    hid.drain(SIDE_STEPS)
    ring.drain()
    for sub in range(SUBS):
        swap(sub).wait_send()
    for i in range(4):
        give(i).wait_send()


def front(hidden_in, norm_gain, cosine, sine, doc_ids, w_query, w_key, w_value, w_out, call_id):
    rows, width = hidden_in.shape
    all_rows = doc_ids.shape[1]
    chips = all_rows // rows // 2
    side = width * 2 // (2 * chips)
    kv_heads = w_key.shape[1] // HS
    groups = w_query.shape[1] // w_key.shape[1]
    dma = pltpu.SemaphoreType.DMA
    bf16, f32 = jnp.bfloat16, jnp.float32
    stacked = (kv_heads, groups * rows, HS)
    return pl.pallas_call(
        functools.partial(front_kernel, chips, kv_heads, groups),
        out_shape=[
            jax.ShapeDtypeStruct((rows, width), bf16),
            jax.ShapeDtypeStruct((all_rows, width), bf16),
            jax.ShapeDtypeStruct((all_rows, side), bf16),
        ],
        in_specs=[pl.BlockSpec(memory_space=pltpu.VMEM)] * 5 + [pl.BlockSpec(memory_space=pl.ANY)] * 4,
        out_specs=[pl.BlockSpec(memory_space=pltpu.VMEM)] + [pl.BlockSpec(memory_space=pl.ANY)] * 2,
        scratch_shapes=[
            pltpu.VMEM((rows, width), bf16),
            pltpu.VMEM((rows, 2 * width), bf16),
            pltpu.VMEM((2 * width, 2 * w_key.shape[1]), bf16),
            pltpu.VMEM((4, 2 * width, 2 * HS), bf16),
            pltpu.VMEM((4, w_out.shape[0], width // 4), bf16),
            pltpu.VMEM((all_rows // rows * 2 * w_key.shape[1], rows), bf16),
            pltpu.VMEM(stacked, bf16),
            pltpu.VMEM(stacked, f32),
            pltpu.VMEM(stacked, f32),
            pltpu.VMEM(stacked, f32),
            pltpu.VMEM((rows, w_out.shape[0]), bf16),
            pltpu.VMEM((rows, width), f32),
            pltpu.VMEM((rows, width), bf16),
            pltpu.VMEM((rows, width), bf16),
            pltpu.VMEM((rows, 2 * rows), f32),
            pltpu.VMEM((rows, 128), jnp.int32),
        ]
        + [dma((chips, SUBS))] * 12
        + [dma((SUBS,))] * 2
        + [dma((4,))] * 2
        + [dma((1,)), dma((2,)), dma((4,)), dma((4,))],
        compiler_params=pltpu.CompilerParams(
            collective_id=call_id, has_side_effects=True, vmem_limit_bytes=VMEM_LIMIT
        ),
        name="front",
    )(hidden_in, norm_gain, cosine, sine, doc_ids, w_query, w_key, w_value, w_out)


def on_pairs(hidden_in, norm_gain, w_query, w_key, w_value, w_out, doc_ids):
    rows = hidden_in.shape[0]
    first_row = lax.axis_index("tok") * rows
    positions = (first_row + jnp.arange(rows, dtype=jnp.int32)) % doc_ids.shape[0]
    lane = jnp.arange(HS, dtype=jnp.int32)
    pair = (lane % (HS // 2)).astype(jnp.float32)
    inv_freq = rope_base ** (-(pair * 2.0) / HS)
    angles = positions.astype(jnp.float32)[:, None] * inv_freq[None, :]
    sine = jnp.sin(angles) * jnp.where(lane < HS // 2, -1.0, 1.0)[None, :]
    hidden_out, cols_in, rows_in = front(
        hidden_in, norm_gain[None, :], jnp.cos(angles), sine, doc_ids[None, :],
        w_query, w_key, w_value, w_out, 0,
    )
    return joint_cov(hidden_out, rows_in, cols_in, 1)


def on_device(hidden_in, norm_gain, w_query, w_key, w_value, w_out, doc_ids):
    tok_rows, col_width = hidden_in.shape
    tok_count = lax.axis_size("tok")
    tp_count = lax.axis_size("tp")
    if tp_count == 2 and tok_rows == 2 * HS and w_key.shape[1] % (2 * HS) == 0:
        return on_pairs(hidden_in, norm_gain, w_query, w_key, w_value, w_out, doc_ids)
    tok_index = lax.axis_index("tok")
    all_rows = tok_rows * tok_count
    full_in = both_sides(hidden_in)
    widened = full_in.astype(jnp.float32)
    factor = lax.rsqrt(jnp.mean(widened * widened, axis=1, keepdims=True) + epsilon)
    normed = (widened * factor * norm_gain[None, :]).astype(jnp.bfloat16)
    kv_heads = w_key.shape[1] // HS
    groups = w_query.shape[1] // w_key.shape[1]
    first_row = tok_index * tok_rows
    positions = first_row + jnp.arange(tok_rows, dtype=jnp.int32)
    key_local = rotate(
        jnp.dot(normed, w_key, preferred_element_type=jnp.float32).reshape(tok_rows, kv_heads, HS),
        positions % all_rows,
    )
    key_local = key_local.astype(jnp.bfloat16).reshape(tok_rows, kv_heads * HS)
    value_local = jnp.dot(normed, w_value, preferred_element_type=jnp.float32).astype(jnp.bfloat16)
    (kv_rows,) = ring_gather(jnp.stack([key_local, value_local]), False, 0)
    early, late = hidden_in[:, : col_width // 2], hidden_in[:, col_width // 2 :]
    late, kv_rows = lax.optimization_barrier((late, kv_rows))
    cols_in = [lax.all_gather(part, "tok", axis=0, tiled=True) for part in (early, late)]
    rows_in = lax.all_to_all(full_in, "tok", 1, 0, tiled=True)
    queries = rotate(
        jnp.dot(normed, w_query, preferred_element_type=jnp.float32).reshape(
            tok_rows, kv_heads * groups, HS
        ),
        positions % all_rows,
    )
    queries = queries.astype(jnp.bfloat16).reshape(tok_rows, kv_heads * groups * HS)
    query_doc = lax.dynamic_slice_in_dim(doc_ids, first_row, tok_rows, 0)
    lo = jnp.sum((doc_ids[None, :] < query_doc[:, None]).astype(jnp.int32), axis=1)
    bounds = jnp.stack([first_row.astype(jnp.int32), lo[0]])
    attended = attend(queries, kv_rows, jnp.broadcast_to(lo[:, None], (tok_rows, 128)), bounds, kv_heads)
    partial_out = jnp.dot(attended, w_out, preferred_element_type=jnp.float32)
    summed = lax.psum_scatter(partial_out, "tp", scatter_dimension=1, tiled=True)
    hidden_out = (hidden_in.astype(jnp.float32) + summed).astype(jnp.bfloat16)
    halves = jnp.stack([hidden_out[:, : col_width // 2], hidden_out[:, col_width // 2 :]])
    (cols_out,) = ring_gather(halves, False, 1)
    rows_out = row_features(cols_out, None)
    return (hidden_out, joint_gram(rows_in, rows_out, cols_in, cols_out))


def solution(mesh):
    return jax.shard_map(
        on_device,
        mesh=mesh,
        in_specs=(
            P("tok", "tp"),
            P(),
            P(None, "tp"),
            P(None, "tp"),
            P(None, "tp"),
            P("tp", None),
            P(),
        ),
        out_specs=(P("tok", "tp"), P(None, "tok", None, "tp")),
        check_vma=False,
    )
```

```python
import functools
import math

import jax
import jax.numpy as jnp
from jax import lax
from jax.experimental import pallas as pl
from jax.experimental.pallas import tpu as pltpu
from jax.sharding import PartitionSpec as P

HS = 128
epsilon = 1e-05
rope_base = 500000.0
VMEM_LIMIT = 60 * 1024 * 1024


def rotate(vectors, positions):
    half_dim = vectors.shape[-1] // 2
    inv_freq = rope_base ** (-(jnp.arange(half_dim, dtype=jnp.float32) * 2.0) / vectors.shape[-1])
    angles = positions.astype(jnp.float32)[:, None] * inv_freq[None, :]
    cosine = jnp.cos(angles)[:, None, :]
    sine_part = jnp.sin(angles)[:, None, :]
    first_half = vectors[..., :half_dim]
    second_half = vectors[..., half_dim:]
    return jnp.concatenate(
        [
            first_half * cosine - second_half * sine_part,
            second_half * cosine + first_half * sine_part,
        ],
        axis=-1,
    )


def attend_kernel(groups, block, bounds, q_ref, k_ref, v_ref, lo_ref, out_ref, s_ref, m_ref, l_ref, acc_ref):
    rows = q_ref.shape[0]
    first_row = bounds[0]
    scale = HS ** (-0.5) * math.log2(math.e)
    start = bounds[1] // block
    stop = (first_row + rows + block - 1) // block
    lanes = 128
    m_ref[...] = jnp.full_like(m_ref, -jnp.inf)
    l_ref[...] = jnp.zeros_like(l_ref)
    acc_ref[...] = jnp.zeros_like(acc_ref)

    @pl.loop(start, stop)
    def _(step):
        first_key = pl.multiple_of(step * block, block)
        keys = k_ref[pl.ds(first_key, block), :]
        key_pos = first_key + lax.broadcasted_iota(jnp.int32, (rows, block), 1)
        query_pos = first_row + lax.broadcasted_iota(jnp.int32, (rows, block), 0)
        allowed = (key_pos >= lo_ref[:, :1]) & (key_pos <= query_pos)
        for head in range(groups):
            part = pl.ds(head * rows, rows)
            s = lax.dot_general(
                q_ref[:, head * HS:(head + 1) * HS], keys,
                (((1,), (1,)), ((), ())), preferred_element_type=jnp.float32,
            ) * scale
            s = jnp.where(allowed, s, -jnp.inf)
            s_ref[step, part, :] = s
            top = m_ref[part, :]
            for piece in range(block // lanes):
                top = jnp.maximum(top, s[:, piece * lanes:(piece + 1) * lanes])
            m_ref[part, :] = top

    m_ref[...] = jnp.broadcast_to(jnp.max(m_ref[...], axis=-1, keepdims=True), m_ref.shape)

    @pl.loop(start, stop)
    def _(step):
        first_key = pl.multiple_of(step * block, block)
        values = v_ref[pl.ds(first_key, block), :]
        for head in range(groups):
            part = pl.ds(head * rows, rows)
            weights = jnp.exp2(s_ref[step, part, :] - m_ref[part, :1])
            total = l_ref[part, :]
            for piece in range(block // lanes):
                total = total + weights[:, piece * lanes:(piece + 1) * lanes]
            l_ref[part, :] = total
            acc_ref[part, :] += jnp.dot(
                weights.astype(jnp.bfloat16), values, preferred_element_type=jnp.float32
            )

    for head in range(groups):
        part = pl.ds(head * rows, rows)
        weight_sum = jnp.sum(l_ref[part, :], axis=-1, keepdims=True)
        out_ref[:, head * HS:(head + 1) * HS] = (acc_ref[part, :] / weight_sum).astype(out_ref.dtype)


def attend(queries, kv_rows, lo, bounds, kv_heads):
    rows, width = queries.shape
    all_rows = kv_rows.shape[1]
    groups = width // (kv_heads * HS)
    block = min(512, all_rows)
    wide = groups * HS
    return pl.pallas_call(
        functools.partial(attend_kernel, groups, block),
        out_shape=jax.ShapeDtypeStruct((rows, width), jnp.bfloat16),
        grid_spec=pltpu.PrefetchScalarGridSpec(
            num_scalar_prefetch=1,
            grid=(kv_heads,),
            in_specs=[
                pl.BlockSpec((rows, wide), lambda g, b: (0, g)),
                pl.BlockSpec((None, all_rows, HS), lambda g, b: (0, 0, g)),
                pl.BlockSpec((None, all_rows, HS), lambda g, b: (1, 0, g)),
                pl.BlockSpec((rows, 128), lambda g, b: (0, 0)),
            ],
            out_specs=pl.BlockSpec((rows, wide), lambda g, b: (0, g)),
            scratch_shapes=[
                pltpu.VMEM((all_rows // block, groups * rows, block), jnp.float32),
                pltpu.VMEM((groups * rows, 128), jnp.float32),
                pltpu.VMEM((groups * rows, 128), jnp.float32),
                pltpu.VMEM((groups * rows, HS), jnp.float32),
            ],
        ),
        compiler_params=pltpu.CompilerParams(
            dimension_semantics=("arbitrary",), vmem_limit_bytes=VMEM_LIMIT
        ),
        cost_estimate=pl.CostEstimate(
            flops=4 * rows * all_rows * width,
            bytes_accessed=2 * all_rows * kv_heads * HS * 2 + 4 * rows * width,
            transcendentals=rows * all_rows * width // HS,
        ),
        name="attend",
    )(bounds, queries, kv_rows, kv_rows, lo)


def gram_kernel(strips, rin_ref, rout_ref, low_ref, high_ref, cout_ref, out_ref, rt_ref, mean_ref):
    all_rows, row_width = rin_ref.shape

    @pl.when(pl.program_id(0) == 0)
    def _():
        ones = jnp.ones((all_rows, 128), jnp.bfloat16)
        for source, ref in enumerate((rin_ref, rout_ref)):
            part = pl.ds(source * row_width, row_width)
            rt_ref[part, :] = ref[...].T
            mean_ref[part, :] = (
                jnp.dot(rt_ref[part, :], ones, preferred_element_type=jnp.float32) / all_rows
            )

    ones = jnp.ones((8, all_rows), jnp.bfloat16)

    def block(source, ref):
        cols = ref[...]
        col_mean = jnp.dot(ones, cols, preferred_element_type=jnp.float32)[:1] / all_rows
        gram = jnp.dot(rt_ref[...], cols, preferred_element_type=jnp.float32)
        cov = gram / all_rows - mean_ref[:, :1] * col_mean
        for row_source in range(2):
            out_ref[row_source, :, source, :] = cov[row_source * row_width:(row_source + 1) * row_width]

    @pl.when(pl.program_id(0) < strips)
    def _():
        block(0, low_ref)

    @pl.when(pl.program_id(0) >= strips)
    def _():
        block(0, high_ref)

    block(1, cout_ref)


def joint_gram(rin, rout, cin, cout):
    all_rows, row_width = rin.shape
    half = cout.shape[2]
    col_width = 2 * half
    tile = min(256, half)
    strips = half // tile
    whole = pl.BlockSpec((all_rows, row_width), lambda j: (0, 0), pipeline_mode=pl.Buffered(1))
    strip = pl.BlockSpec((None, all_rows, tile), lambda j: (j // strips, 0, j % strips))
    low = pl.BlockSpec((all_rows, tile), lambda j: (0, jnp.minimum(j, strips - 1)))
    high = pl.BlockSpec((all_rows, tile), lambda j: (0, jnp.maximum(j - strips, 0)))
    return pl.pallas_call(
        functools.partial(gram_kernel, strips),
        out_shape=jax.ShapeDtypeStruct((2, row_width, 2, col_width), jnp.float32),
        grid=(col_width // tile,),
        in_specs=[whole, whole, low, high, strip],
        out_specs=pl.BlockSpec((2, row_width, 2, tile), lambda j: (0, 0, 0, j)),
        scratch_shapes=[
            pltpu.VMEM((2 * row_width, all_rows), jnp.bfloat16),
            pltpu.VMEM((2 * row_width, 128), jnp.float32),
        ],
        compiler_params=pltpu.CompilerParams(
            dimension_semantics=("arbitrary",), vmem_limit_bytes=VMEM_LIMIT
        ),
        cost_estimate=pl.CostEstimate(
            flops=8 * all_rows * row_width * col_width,
            bytes_accessed=4 * all_rows * (row_width + col_width) + 16 * row_width * col_width,
            transcendentals=0,
        ),
        name="joint_gram",
    )(rin, rout, *cin, cout)


def both_sides(block):
    if lax.axis_size("tp") != 2:
        return lax.all_gather(block, "tp", axis=1, tiled=True)
    other = lax.ppermute(block, "tp", ((0, 1), (1, 0)))
    first = lax.axis_index("tp") == 0
    return jnp.concatenate([jnp.where(first, block, other), jnp.where(first, other, block)], axis=1)


def ring_kernel(chips, share, x_ref, *refs):
    if share:
        out_ref, side_ref, send, recv, psend, precv, local, ssend, srecv = refs
    else:
        out_ref, send, recv, psend, precv, local = refs
    mesh_id = pl.DeviceIdType.MESH
    rows = x_ref.shape[1]
    me, tp = lax.axis_index("tok"), lax.axis_index("tp")
    count = 2 * chips
    core, chip = me % 2, me // 2
    depth = chips // 2
    spot = jnp.where(chip % 2 == 0, chip // 2, chips - 1 - chip // 2)

    def device(place):
        place = (place + 2 * chips) % chips
        return jnp.where(place < depth, place * 4, (chips - 1 - place) * 4 + 2) + core

    partner = me + 1 - 2 * core
    ways = (device(spot + 1), device(spot - 1))
    barrier = pltpu.get_barrier_semaphore()
    for peer in (*ways, partner):
        pl.semaphore_signal(barrier, inc=1, device_id={"tok": peer}, device_id_type=mesh_id)
    if share:
        pl.semaphore_signal(barrier, inc=1, device_id={"tp": 1 - tp}, device_id_type=mesh_id)
    pl.semaphore_wait(barrier, 4 if share else 3)

    def block(way, origin):
        return out_ref.at[way, pl.ds(pl.multiple_of(origin * rows, rows), rows), :]

    pending = []

    def step_copies(step, way):
        origin = device(spot - step if way == 0 else spot + step)
        source = x_ref.at[way] if step == 0 else block(way, origin)
        ring = None
        if step < chips - 1:
            ring = pltpu.make_async_remote_copy(
                src_ref=source, dst_ref=block(way, origin), send_sem=send.at[way, step],
                recv_sem=recv.at[way, step], device_id={"tok": ways[way]}, device_id_type=mesh_id,
            )
            ring.start()
        beside = pltpu.make_async_remote_copy(
            src_ref=source, dst_ref=block(way, origin), send_sem=psend.at[way, step],
            recv_sem=precv.at[way, step], device_id={"tok": partner}, device_id_type=mesh_id,
        )
        beside.start()
        pending.append((ring, beside))
        return ring

    rings = [step_copies(0, way) for way in range(2)]
    own = [pltpu.make_async_copy(x_ref.at[way], block(way, me), local.at[way]) for way in range(2)]
    for copy in own:
        copy.start()
    if share:
        width = side_ref.shape[1]
        half = x_ref.shape[2]
        owner = me // (count // 2)
        my_way = me * width % (2 * half) // half
        features = pl.ds(pl.multiple_of(me * width % half, width), width)

    def side_copy(step, way, kind):
        origin = device(spot - step if way == 0 else spot + step)
        origin = origin + kind * (1 - 2 * core)
        source = x_ref.at[way, :, features]
        if step > 0 or kind > 0:
            source = out_ref.at[way, pl.ds(pl.multiple_of(origin * rows, rows), rows), features]
        return pltpu.make_async_remote_copy(
            src_ref=source,
            dst_ref=side_ref.at[pl.ds(pl.multiple_of(origin * rows, rows), rows), :],
            send_sem=ssend.at[kind, step], recv_sem=srecv.at[kind, step],
            device_id={"tp": 1 - tp}, device_id_type=mesh_id,
        )

    def each_side(act, step, way, kind, holder):
        if share:
            @pl.when((my_way == way) & ((owner == tp) == holder))
            def _():
                act(side_copy(step, way, kind))

    def start(copy):
        copy.start()

    for way in range(2):
        each_side(start, 0, way, 0, True)
    for step in range(1, chips):
        for way in range(2):
            rings[way].wait_recv()
            rings[way] = step_copies(step, way)
            each_side(start, step, way, 0, True)
            pending[2 * (step - 1) + way][1].wait_recv()
            each_side(start, step - 1, way, 1, True)
    for way in range(2):
        pending[2 * (chips - 1) + way][1].wait_recv()
        each_side(start, chips - 1, way, 1, True)
    for ring, beside in pending:
        if ring is not None:
            ring.wait_send()
        beside.wait_send()
    for copy in own:
        copy.wait()
    for step in range(chips):
        for way in range(2):
            for kind in range(2):
                each_side(lambda copy: copy.wait_send(), step, way, kind, True)
                each_side(lambda copy: copy.wait_recv(), step, way, kind, False)


def ring_gather(halves, share, call_id):
    _, rows, width = halves.shape
    count = lax.axis_size("tok")
    chips = count // 2
    out_shape = [jax.ShapeDtypeStruct((2, rows * count, width), halves.dtype)]
    dma = pltpu.SemaphoreType.DMA
    scratch = [dma((2, chips))] * 4 + [dma((2,))]
    if share:
        out_shape.append(jax.ShapeDtypeStruct((rows * count, 4 * width // count), halves.dtype))
        scratch += [dma((2, chips))] * 2
    return pl.pallas_call(
        functools.partial(ring_kernel, chips, share),
        out_shape=out_shape,
        in_specs=[pl.BlockSpec(memory_space=pltpu.VMEM)],
        out_specs=[pl.BlockSpec(memory_space=pl.ANY)] * len(out_shape),
        scratch_shapes=scratch,
        compiler_params=pltpu.CompilerParams(
            collective_id=call_id, has_side_effects=True, vmem_limit_bytes=VMEM_LIMIT
        ),
        cost_estimate=pl.CostEstimate(
            flops=40_000_000_000, bytes_accessed=2 * halves.size * count * 2, transcendentals=0
        ),
        name="ring_share" if share else "ring",
    )(halves)


def row_features(columns, arrived):
    _, all_rows, half = columns.shape
    row_width = 2 * half * lax.axis_size("tp") // lax.axis_size("tok")
    first = lax.axis_index("tok") * row_width
    offset, owner = first % (2 * half), first // (2 * half)
    mine = lax.dynamic_slice(columns, (offset // half, 0, offset % half), (1, all_rows, row_width))[0]
    owned = lax.axis_index("tp") == owner
    if arrived is None:
        return lax.psum(jnp.where(owned, mine, jnp.zeros_like(mine)), "tp")
    return jnp.where(owned, mine, arrived)


SUBS = 2
SIDE_STEPS = 6
COV_SUBS = 2
MESH = pl.DeviceIdType.MESH


def ring_place(chips):
    me, tp = lax.axis_index("tok"), lax.axis_index("tp")
    core, chip = me % 2, me // 2
    spot = jnp.where(chip % 2 == 0, chip // 2, chips - 1 - chip // 2)

    def chip_at(place):
        place = (place + 2 * chips) % chips
        return jnp.where(place < chips // 2, place * 2, (chips - 1 - place) * 2 + 1)

    ahead = 1 - 2 * core
    return me, tp, core, spot, chip_at, ahead, chips


class Ring:
    def __init__(self, place, big, own, subs, sems, far=None, side=None, side_sems=None):
        self.me, self.tp, self.core, self.spot, self.chip_at, self.ahead, self.chips = place
        self.big, self.own, self.subs = big, own, subs
        self.rows = big.shape[0] // (2 * self.chips)
        self.part = self.rows // subs
        self.send, self.recv, self.psend, self.precv = sems
        self.far, self.side = far, side
        self.partner = self.me + 1 - 2 * self.core
        self.onward = self.chip_at(self.spot + self.ahead) * 2 + self.core
        self.back = self.chip_at(self.spot - self.ahead) * 2 + self.core
        if far is not None:
            self.ssend, self.srecv, self.tsend, self.trecv = side_sems
            width = big.shape[1]
            self.owner = self.me * side // width == self.tp
            self.feature = pl.multiple_of(self.me * side % width, side)
            self.partner_feature = pl.multiple_of(self.partner * side % width, side)

    def block(self, step, mine):
        turn = self.ahead if mine else -self.ahead
        return self.chip_at(self.spot - turn * step) * 2 + (self.core if mine else 1 - self.core)

    def block_row(self, step, mine):
        return pl.multiple_of(self.block(step, mine) * self.rows, self.rows)

    def span(self, step, sub):
        return pl.ds(pl.multiple_of(self.block_row(step, True) + sub * self.part, self.part), self.part)

    def source(self, step, sub):
        if self.own is not None and isinstance(step, int) and step == 0:
            return self.own.at[pl.ds(sub * self.part, self.part)]
        return self.big.at[self.span(step, sub)]

    def ring_copy(self, step, sub):
        return pltpu.make_async_remote_copy(
            src_ref=self.source(step, sub), dst_ref=self.big.at[self.span(step, sub)],
            send_sem=self.send.at[step, sub], recv_sem=self.recv.at[step, sub],
            device_id={"tok": self.onward}, device_id_type=MESH,
        )

    def beside_copy(self, step, sub):
        return pltpu.make_async_remote_copy(
            src_ref=self.source(step, sub), dst_ref=self.big.at[self.span(step, sub)],
            send_sem=self.psend.at[step, sub], recv_sem=self.precv.at[step, sub],
            device_id={"tok": self.partner}, device_id_type=MESH,
        )

    def side_copy(self, step, sub, same):
        wanted, target = (self.feature, self.me) if same else (self.partner_feature, self.partner)
        out_sem, in_sem = (self.ssend, self.srecv) if same else (self.tsend, self.trecv)
        return pltpu.make_async_remote_copy(
            src_ref=self.source(step, sub).at[:, pl.ds(wanted, self.side)],
            dst_ref=self.far.at[self.span(step, sub), :],
            send_sem=out_sem.at[step, sub], recv_sem=in_sem.at[step, sub],
            device_id={"tok": target, "tp": 1 - self.tp}, device_id_type=MESH,
        )

    def launch(self, step, sub):
        if isinstance(step, int):
            if step < self.chips - 1:
                self.ring_copy(step, sub).start()
        else:
            @pl.when(step < self.chips - 1)
            def _():
                self.ring_copy(step, sub).start()
        self.beside_copy(step, sub).start()

    def launch_side(self, step, sub):
        @pl.when(self.owner)
        def _():
            for same in (True, False):
                self.side_copy(step, sub, same).start()

    def event(self, step, sub):
        self.ring_copy(step - 1, sub).wait_recv()
        self.launch(step, sub)

    def beside_arrived(self, step):
        for sub in range(self.subs):
            self.beside_copy(step, sub).wait_recv()

    def side_arrived(self, step, mine):
        @pl.when(jnp.logical_not(self.owner))
        def _():
            for sub in range(self.subs):
                self.side_copy(step, sub, mine).wait_recv()

    def drain(self, side_steps=0):
        for step in range(self.chips):
            for sub in range(self.subs):
                if step < self.chips - 1:
                    self.ring_copy(step, sub).wait_send()
                self.beside_copy(step, sub).wait_send()
                if step < side_steps:
                    @pl.when(self.owner)
                    def _():
                        for same in (True, False):
                            self.side_copy(step, sub, same).wait_send()


def greet(ring):
    barrier = pltpu.get_barrier_semaphore()
    for peer in (ring.onward, ring.back, ring.partner):
        pl.semaphore_signal(barrier, inc=1, device_id={"tok": peer}, device_id_type=MESH)
    for peer in (ring.me, ring.partner):
        pl.semaphore_signal(
            barrier, inc=1, device_id={"tok": peer, "tp": 1 - ring.tp}, device_id_type=MESH
        )
    pl.semaphore_wait(barrier, 5)


def cov_kernel(chips, x_ref, cin_ref, rin_ref, *refs):
    acc_ref, rsum_ref, big, far, lt, cbuf, rbuf, late = refs[:8]
    sems, side_sems = refs[8:12], refs[12:16]
    own_sem, cin_sem, rin_sem, lsend, lrecv, ones_r = refs[16:]
    ring = Ring(ring_place(chips), big, x_ref, COV_SUBS, sems, far, rin_ref.shape[1], side_sems)
    rows, width = x_ref.shape
    side = ring.side
    owner = ring.owner
    greet(ring)
    for sub in range(COV_SUBS):
        ring.launch(0, sub)
        ring.launch_side(0, sub)
    own = pltpu.make_async_copy(x_ref, big.at[pl.ds(pl.multiple_of(ring.me * rows, rows), rows)], own_sem.at[0])
    own.start()

    def slot_of(step, mine):
        return step % 2 * 2 + (0 if mine else 1)

    def fetch_cols(step, mine):
        slot = slot_of(step, mine)
        place = pl.ds(ring.block_row(step, mine), rows)
        return pltpu.make_async_copy(cin_ref.at[place, :], cbuf.at[slot], cin_sem.at[slot])

    def fetch_strip(step, mine):
        slot = slot_of(step, mine)
        place = pl.ds(ring.block_row(step, mine), rows)
        return pltpu.make_async_copy(rin_ref.at[place, :], rbuf.at[slot], rin_sem.at[slot])

    def late_copy(step, same):
        wanted, target = (ring.feature, ring.me) if same else (ring.partner_feature, ring.partner)
        slot = (step - SIDE_STEPS) * 2 + (0 if same else 1)
        return pltpu.make_async_remote_copy(
            src_ref=cin_ref.at[pl.ds(ring.block_row(step, True), rows), pl.ds(wanted, side)],
            dst_ref=late.at[slot], send_sem=lsend.at[slot], recv_sem=lrecv.at[slot],
            device_id={"tok": target, "tp": 1 - ring.tp}, device_id_type=MESH,
        )

    def start_fetch(step, mine):
        fetch_cols(step, mine).start()
        if step < SIDE_STEPS:
            @pl.when(jnp.logical_not(owner))
            def _():
                fetch_strip(step, mine).start()

    for step in range(2):
        for mine in (True, False):
            start_fetch(step, mine)

    ones_r[...] = jnp.ones_like(ones_r)
    lt[2 * side:, :] = jnp.ones((lt.shape[0] - 2 * side, rows), lt.dtype)
    acc_ref[...] = jnp.zeros_like(acc_ref)
    rsum_ref[...] = jnp.zeros_like(rsum_ref)
    own.wait()
    tile = min(512, width)

    def work(step, mine):
        if not mine:
            ring.beside_arrived(step)
        ring.side_arrived(step, mine)
        slot = slot_of(step, mine)
        place = pl.ds(ring.block_row(step, mine), rows)
        fetch_cols(step, mine).wait()

        @pl.when(owner)
        def _():
            lt[0:side, :] = cbuf[slot, :, pl.ds(ring.feature, side)].T
            lt[side:2 * side, :] = big[place, pl.ds(ring.feature, side)].T

        @pl.when(jnp.logical_not(owner))
        def _():
            if step < SIDE_STEPS:
                fetch_strip(step, mine).wait()
                lt[0:side, :] = rbuf[slot].T
            else:
                late_copy(step, mine).wait_recv()
                lt[0:side, :] = late[(step - SIDE_STEPS) * 2 + (0 if mine else 1)].T
            lt[side:2 * side, :] = far[place, :].T

        rsum_ref[...] += jnp.dot(lt[0:2 * side, :], ones_r[...], preferred_element_type=jnp.float32)

        @pl.loop(0, width // tile)
        def _(i):
            here = pl.ds(pl.multiple_of(i * tile, tile), tile)
            acc_ref[:, here] += jnp.dot(
                lt[...], cbuf[slot, :, here], preferred_element_type=jnp.float32
            )
            there = pl.ds(pl.multiple_of(width + i * tile, tile), tile)
            acc_ref[:, there] += jnp.dot(
                lt[...], big[place, here], preferred_element_type=jnp.float32
            )

        if step + 2 < chips:
            start_fetch(step + 2, mine)

    for step in range(1, chips):
        for sub in range(COV_SUBS):
            ring.event(step, sub)
            ring.launch_side(step, sub)
            if sub == 0 and 1 <= step <= chips - SIDE_STEPS:
                @pl.when(owner)
                def _():
                    for same in (True, False):
                        late_copy(SIDE_STEPS + step - 1, same).start()
            if sub == COV_SUBS // 2 - 1:
                work(step - 1, True)
            if sub == (COV_SUBS // 2 if step == chips - 1 else COV_SUBS) - 1:
                work(step - 1, False)
    work(chips - 1, True)
    work(chips - 1, False)
    ring.drain(chips)

    @pl.when(owner)
    def _():
        for step in range(SIDE_STEPS, chips):
            for same in (True, False):
                late_copy(step, same).wait_send()


def finish_kernel(all_rows, strips, acc_ref, rsum_ref, x_ref, out_ref, y_ref):
    width = acc_ref.shape[1] // 2
    side = rsum_ref.shape[0] // 2
    tall = side // strips
    groups = 2 * width // 128
    part_of = 1.0 / all_rows
    y_ref[...] = x_ref[...]
    for row_source in range(2):
        place = pl.ds(pl.multiple_of(row_source * side + pl.program_id(0) * tall, tall), tall)
        mean_row = rsum_ref[place, :] * part_of
        for source in range(2):
            for j in range(width // 128):
                part = slice(source * width + j * 128, source * width + (j + 1) * 128)
                mean_col = acc_ref[2 * side:2 * side + 1, part] * part_of
                out_ref[row_source, pl.ds(2 * j + source, tall, stride=groups), :] = (
                    acc_ref[place, part] * part_of - mean_row * mean_col
                )


def joint_cov(hidden_out, rows_in, cols_in, call_id):
    rows, width = hidden_out.shape
    all_rows, side = cols_in.shape[0], rows_in.shape[1]
    chips = all_rows // rows // 2
    dma = pltpu.SemaphoreType.DMA
    tall = 2 * side + 16
    acc, rsum = pl.pallas_call(
        functools.partial(cov_kernel, chips),
        out_shape=[
            jax.ShapeDtypeStruct((tall, 2 * width), jnp.float32),
            jax.ShapeDtypeStruct((2 * side, 128), jnp.float32),
        ],
        in_specs=[pl.BlockSpec(memory_space=pltpu.VMEM)]
        + [pl.BlockSpec(memory_space=pl.ANY)] * 2,
        out_specs=[pl.BlockSpec(memory_space=pltpu.VMEM)] * 2,
        scratch_shapes=[
            pltpu.VMEM((all_rows, width), jnp.bfloat16),
            pltpu.VMEM((all_rows, side), jnp.bfloat16),
            pltpu.VMEM((tall, rows), jnp.bfloat16),
            pltpu.VMEM((4, rows, width), jnp.bfloat16),
            pltpu.VMEM((4, rows, side), jnp.bfloat16),
            pltpu.VMEM((2 * (chips - SIDE_STEPS), rows, side), jnp.bfloat16),
        ]
        + [dma((chips, COV_SUBS))] * 8
        + [dma((1,)), dma((4,)), dma((4,))]
        + [dma((2 * (chips - SIDE_STEPS),))] * 2
        + [pltpu.VMEM((rows, 128), jnp.bfloat16)],
        compiler_params=pltpu.CompilerParams(
            collective_id=call_id, has_side_effects=True, vmem_limit_bytes=38 * 1024 * 1024
        ),
        cost_estimate=pl.CostEstimate(
            flops=8 * all_rows * side * width * 4,
            bytes_accessed=4 * all_rows * (side + width) + 16 * side * width,
            transcendentals=0,
        ),
        name="cov_ring",
    )(hidden_out, cols_in, rows_in)
    cov, settled = finish(acc, rsum, hidden_out, side)
    return settled, cov


def finish(acc, rsum, hidden_out, side):
    rows, width = hidden_out.shape
    all_rows = rows * lax.axis_size("tok")
    strips = 8
    tall = side // strips
    groups = 2 * width // 128
    cov, settled = pl.pallas_call(
        functools.partial(finish_kernel, all_rows, strips),
        out_shape=[
            jax.ShapeDtypeStruct((2, side * groups, 128), jnp.float32),
            jax.ShapeDtypeStruct(hidden_out.shape, hidden_out.dtype),
        ],
        grid=(strips,),
        in_specs=[
            pl.BlockSpec(memory_space=pltpu.VMEM),
            pl.BlockSpec(memory_space=pltpu.VMEM),
            pl.BlockSpec((rows // strips, width), lambda i: (i, 0)),
        ],
        out_specs=[
            pl.BlockSpec((2, tall * groups, 128), lambda i: (0, i, 0)),
            pl.BlockSpec((rows // strips, width), lambda i: (i, 0)),
        ],
        compiler_params=pltpu.CompilerParams(
            dimension_semantics=("arbitrary",), vmem_limit_bytes=8 * 1024 * 1024
        ),
        name="finish",
    )(acc, rsum, hidden_out)
    cov = cov.reshape(2, side, width // 128, 2, 128).transpose(0, 1, 3, 2, 4)
    return cov.reshape(2, side, 2, width), settled


NEG = -1e30


def front_kernel(
    chips, kv_heads, groups, x_ref, gain_ref, cos_ref, sin_ref, kdoc_ref,
    wq_ref, wk_ref, wv_ref, wo_ref, out_ref, cin, far, other, normed, wkv, wq, wo, kv, q_ref,
    m_ref, l_ref, acc_ref, att, mine_sum, sent, arrived, bias, qdoc_ref, *sems
):
    place = ring_place(chips)
    hid_sems, side_sems, kv_sems = sems[0:4], sems[4:8], sems[8:12]
    xsend, xrecv, osend, orecv, own_sem, wkv_sem, wq_sem, wo_sem = sems[12:]
    rows, width = x_ref.shape
    side = far.shape[1]
    hid = Ring(place, cin, x_ref, SUBS, hid_sems, far, side, side_sems)
    ring = Ring(place, kv, None, SUBS, kv_sems)
    me, tp = hid.me, hid.tp
    half = rows // SUBS
    kv_width = kv_heads * HS
    scale = HS ** (-0.5) * math.log2(math.e)
    head_pair = 2 * HS
    q_tiles = kv_heads * groups // 2
    out_tile = width // 4

    def swap(sub):
        part = pl.ds(sub * half, half)
        return pltpu.make_async_remote_copy(
            src_ref=x_ref.at[part], dst_ref=other.at[part], send_sem=xsend.at[sub],
            recv_sem=xrecv.at[sub], device_id={"tp": 1 - tp}, device_id_type=MESH,
        )

    def fetch_q(t):
        col = pl.ds(pl.multiple_of(t * head_pair, head_pair), head_pair)
        return pltpu.make_async_copy(wq_ref.at[:, col], wq.at[t % 4], wq_sem.at[t % 4])

    def fetch_out(side_tp, i):
        col = pl.ds(pl.multiple_of(side_tp * width + i * out_tile, out_tile), out_tile)
        return pltpu.make_async_copy(wo_ref.at[:, col], wo.at[i], wo_sem.at[i])

    def out_part(i):
        return pl.ds(pl.multiple_of(i * out_tile, out_tile), out_tile)

    def give(i):
        return pltpu.make_async_remote_copy(
            src_ref=sent.at[:, out_part(i)], dst_ref=arrived.at[:, out_part(i)],
            send_sem=osend.at[i], recv_sem=orecv.at[i],
            device_id={"tp": 1 - tp}, device_id_type=MESH,
        )

    keys = [
        pltpu.make_async_copy(ref, wkv.at[:, pl.ds(i * kv_width, kv_width)], wkv_sem.at[i])
        for i, ref in enumerate((wk_ref, wv_ref))
    ]
    for copy in keys:
        copy.start()
    greet(hid)
    for sub in range(SUBS):
        swap(sub).start()
        hid.launch(0, sub)
    own = pltpu.make_async_copy(x_ref, cin.at[pl.ds(pl.multiple_of(me * rows, rows), rows)], own_sem.at[0])
    own.start()
    for t in range(4):
        fetch_q(t).start()
    for i in range(4):
        fetch_out(1 - tp, i).start()

    @pl.loop(0, kv_heads)
    def _(g):
        m_ref[g] = jnp.full(m_ref.shape[1:], NEG, jnp.float32)
        l_ref[g] = jnp.zeros(l_ref.shape[1:], jnp.float32)
        acc_ref[g] = jnp.zeros(acc_ref.shape[1:], jnp.float32)

    my_doc = kdoc_ref[:, pl.ds(pl.multiple_of(me * rows, rows), rows)]
    qdoc_ref[...] = jnp.broadcast_to(my_doc, (128, rows)).T
    my_cols = pl.ds(pl.multiple_of(tp * width, width), width)
    other_cols = pl.ds(pl.multiple_of((1 - tp) * width, width), width)

    def normalise(sub):
        @pl.loop(0, half // 32)
        def _(r):
            part = pl.ds(pl.multiple_of(sub * half + r * 32, 32), 32)
            near = x_ref[part, :].astype(jnp.float32)
            away = other[part, :].astype(jnp.float32)
            total = jnp.sum(near * near, axis=1, keepdims=True) + jnp.sum(away * away, axis=1, keepdims=True)
            factor = lax.rsqrt(total / (2 * width) + epsilon)
            normed[part, my_cols] = (near * factor * gain_ref[:, my_cols]).astype(jnp.bfloat16)
            normed[part, other_cols] = (away * factor * gain_ref[:, other_cols]).astype(jnp.bfloat16)

    def turned(vectors):
        return vectors * cos_ref[...] + pltpu.roll(vectors, HS // 2, 1) * sin_ref[...]

    hid.event(1, 0)
    hid.event(1, 1)
    swap(0).wait_recv()
    normalise(0)
    hid.event(2, 0)
    hid.event(2, 1)
    swap(1).wait_recv()
    normalise(1)
    for copy in keys:
        copy.wait()
    my_base = pl.multiple_of(me * 2 * kv_width, 2 * kv_width)

    @pl.loop(0, kv_width // head_pair)
    def _(t):
        col = pl.multiple_of(t * head_pair, head_pair)
        found = jnp.dot(normed[...], wkv[:, pl.ds(col, head_pair)], preferred_element_type=jnp.float32)
        for j in range(2):
            piece = turned(found[:, j * HS:(j + 1) * HS])
            kv[pl.ds(pl.multiple_of(my_base + col + j * HS, HS), HS), :] = piece.T.astype(jnp.bfloat16)


    @pl.loop(0, kv_width // head_pair)
    def _(t):
        col = pl.multiple_of(kv_width + t * head_pair, head_pair)
        found = jnp.dot(normed[...], wkv[:, pl.ds(col, head_pair)], preferred_element_type=jnp.float32)
        kv[pl.ds(pl.multiple_of(my_base + col, head_pair), rows), :] = found.astype(jnp.bfloat16)

        @pl.when(t == 0)
        def _():
            ring.launch(0, 0)

    ring.launch(0, 1)
    for step in range(3):
        for sub in range(SUBS):
            hid.launch_side(step, sub)

    @pl.loop(0, q_tiles)
    def _(t):
        fetch_q(t).wait()
        found = jnp.dot(normed[...], wq[t % 4], preferred_element_type=jnp.float32)
        for j in range(2):
            head = t * 2 + j
            row = pl.multiple_of(head % groups * rows, rows)
            q_ref[head // groups, pl.ds(row, rows), :] = turned(found[:, j * HS:(j + 1) * HS]).astype(jnp.bfloat16)

        @pl.when(t + 4 < q_tiles)
        def _():
            fetch_q(t + 4).start()

        @pl.when(t == q_tiles // 2)
        def _():
            ring.event(1, 0)

    ring.event(1, 1)

    def make_bias(blocks):
        for i, block in enumerate(blocks):
            row = pl.multiple_of(block * rows, rows)
            key_pos = row + lax.broadcasted_iota(jnp.int32, (rows, rows), 1)
            query_pos = me * rows + lax.broadcasted_iota(jnp.int32, (rows, rows), 0)
            allowed = (kdoc_ref[:, pl.ds(row, rows)] == qdoc_ref[:, :1]) & (key_pos <= query_pos)
            bias[:, i * rows:(i + 1) * rows] = jnp.where(allowed, 0.0, NEG)

    def pair_attention(blocks, heads):
        @pl.loop(*heads)
        def _(g):
            k_row, v_row = g * HS, kv_width + g // 2 * rows
            v_col = pl.ds(pl.multiple_of(g % 2 * HS, HS), HS)
            k = jnp.concatenate(
                [kv[pl.ds(pl.multiple_of(b * 2 * kv_width + k_row, HS), HS), :] for b in blocks], axis=1
            )
            v = jnp.concatenate(
                [kv[pl.ds(pl.multiple_of(b * 2 * kv_width + v_row, rows), rows), v_col] for b in blocks],
                axis=0,
            )
            for head in range(groups):
                part = pl.ds(head * rows, rows)
                s = jnp.dot(q_ref[g, part, :], k, preferred_element_type=jnp.float32) * scale + bias[...]
                old = m_ref[g, part, :]
                pieces = [s[:, i:i + 128] for i in range(0, 2 * rows, 128)]
                peak = functools.reduce(jnp.maximum, pieces)
                top = jnp.maximum(old, jnp.max(peak, axis=-1, keepdims=True))
                fade = jnp.exp2(old - top)
                weights = [jnp.exp2(piece - top) for piece in pieces]
                l_ref[g, part, :] = l_ref[g, part, :] * fade + functools.reduce(jnp.add, weights)
                m_ref[g, part, :] = top
                acc_ref[g, part, :] = acc_ref[g, part, :] * fade + jnp.dot(
                    jnp.concatenate(weights, axis=1).astype(jnp.bfloat16), v,
                    preferred_element_type=jnp.float32,
                )

    @pl.loop(0, chips * SUBS)
    def _(turn):
        step, sub = turn // SUBS, turn % SUBS

        @pl.when(step + 2 < chips)
        def _():
            ring.event(step + 2, sub)


        @pl.when((step + 2 == chips - 2) & (sub == 1))
        def _():
            for part in range(SUBS):
                hid.event(3, part)
                hid.launch_side(3, part)

        @pl.when(step + 2 == chips + 1)
        def _():
            hid.event(4, sub)
            hid.launch_side(4, sub)

        blocks = (ring.block(step, True), ring.block(step, False))
        needed = (blocks[0] <= me) | (blocks[1] <= me)

        @pl.when(sub == 0)
        def _():
            ring.beside_arrived(step)

        @pl.when((sub == 0) & needed)
        def _():
            make_bias(blocks)

        @pl.when(needed)
        def _():
            pair_attention(blocks, (sub * (kv_heads // SUBS), (sub + 1) * (kv_heads // SUBS)))

    @pl.loop(0, kv_heads)
    def _(g):
        for head in range(groups):
            part = pl.ds(head * rows, rows)
            weight_sum = jnp.sum(l_ref[g, part, :], axis=-1, keepdims=True)
            col = pl.ds(pl.multiple_of((g * groups + head) * HS, HS), HS)
            att[:, col] = (acc_ref[g, part, :] / weight_sum).astype(jnp.bfloat16)

    @pl.loop(0, 4)
    def _(i):
        fetch_out(1 - tp, i).wait()
        found = jnp.dot(att[...], wo[i], preferred_element_type=jnp.float32)
        sent[:, out_part(i)] = found.astype(jnp.bfloat16)

        @pl.when(i > 0)
        def _():
            give(i - 1).start()

        fetch_out(tp, i).start()

    give(3).start()
    for i in range(2):
        hid.event(5, i)
        hid.launch_side(5, i)
    hid.event(6, 0)

    @pl.loop(0, 4)
    def _(i):
        fetch_out(tp, i).wait()
        mine_sum[:, out_part(i)] = jnp.dot(att[...], wo[i], preferred_element_type=jnp.float32)

    hid.event(6, 1)

    def settle(i):
        give(i).wait_recv()
        summed = mine_sum[:, out_part(i)] + arrived[:, out_part(i)].astype(jnp.float32)
        out_ref[:, out_part(i)] = (x_ref[:, out_part(i)].astype(jnp.float32) + summed).astype(jnp.bfloat16)

    pl.loop(0, 4)(settle)
    for sub in range(SUBS):
        hid.event(7, sub)
    own.wait()
    for step in range(chips):
        hid.beside_arrived(step)
        if step < SIDE_STEPS:
            for mine in (True, False):
                hid.side_arrived(step, mine)
    hid.drain(SIDE_STEPS)
    ring.drain()
    for sub in range(SUBS):
        swap(sub).wait_send()
    for i in range(4):
        give(i).wait_send()


def front(hidden_in, norm_gain, cosine, sine, doc_ids, w_query, w_key, w_value, w_out, call_id):
    rows, width = hidden_in.shape
    all_rows = doc_ids.shape[1]
    chips = all_rows // rows // 2
    side = width * 2 // (2 * chips)
    kv_heads = w_key.shape[1] // HS
    groups = w_query.shape[1] // w_key.shape[1]
    dma = pltpu.SemaphoreType.DMA
    bf16, f32 = jnp.bfloat16, jnp.float32
    stacked = (kv_heads, groups * rows, HS)
    return pl.pallas_call(
        functools.partial(front_kernel, chips, kv_heads, groups),
        out_shape=[
            jax.ShapeDtypeStruct((rows, width), bf16),
            jax.ShapeDtypeStruct((all_rows, width), bf16),
            jax.ShapeDtypeStruct((8 * all_rows, side), bf16),
        ],
        in_specs=[pl.BlockSpec(memory_space=pltpu.VMEM)] * 5 + [pl.BlockSpec(memory_space=pl.ANY)] * 4,
        out_specs=[pl.BlockSpec(memory_space=pltpu.VMEM)] + [pl.BlockSpec(memory_space=pl.ANY)] * 2,
        scratch_shapes=[
            pltpu.VMEM((rows, width), bf16),
            pltpu.VMEM((rows, 2 * width), bf16),
            pltpu.VMEM((2 * width, 2 * w_key.shape[1]), bf16),
            pltpu.VMEM((4, 2 * width, 2 * HS), bf16),
            pltpu.VMEM((4, w_out.shape[0], width // 4), bf16),
            pltpu.VMEM((all_rows // rows * 2 * w_key.shape[1], rows), bf16),
            pltpu.VMEM(stacked, bf16),
            pltpu.VMEM(stacked, f32),
            pltpu.VMEM(stacked, f32),
            pltpu.VMEM(stacked, f32),
            pltpu.VMEM((rows, w_out.shape[0]), bf16),
            pltpu.VMEM((rows, width), f32),
            pltpu.VMEM((rows, width), bf16),
            pltpu.VMEM((rows, width), bf16),
            pltpu.VMEM((rows, 2 * rows), f32),
            pltpu.VMEM((rows, 128), jnp.int32),
        ]
        + [dma((chips, SUBS))] * 12
        + [dma((SUBS,))] * 2
        + [dma((4,))] * 2
        + [dma((1,)), dma((2,)), dma((4,)), dma((4,))],
        compiler_params=pltpu.CompilerParams(
            collective_id=call_id, has_side_effects=True, vmem_limit_bytes=52 * 1024 * 1024
        ),
        name="front",
    )(hidden_in, norm_gain, cosine, sine, doc_ids, w_query, w_key, w_value, w_out)


def on_pairs(hidden_in, norm_gain, w_query, w_key, w_value, w_out, doc_ids):
    rows = hidden_in.shape[0]
    first_row = lax.axis_index("tok") * rows
    positions = (first_row + jnp.arange(rows, dtype=jnp.int32)) % doc_ids.shape[0]
    lane = jnp.arange(HS, dtype=jnp.int32)
    pair = (lane % (HS // 2)).astype(jnp.float32)
    inv_freq = rope_base ** (-(pair * 2.0) / HS)
    angles = positions.astype(jnp.float32)[:, None] * inv_freq[None, :]
    sine = jnp.sin(angles) * jnp.where(lane < HS // 2, -1.0, 1.0)[None, :]
    hidden_out, cols_in, rows_in = front(
        hidden_in, norm_gain[None, :], jnp.cos(angles), sine, doc_ids[None, :],
        w_query, w_key, w_value, w_out, 0,
    )
    return joint_cov(hidden_out, rows_in, cols_in, 1)


def on_device(hidden_in, norm_gain, w_query, w_key, w_value, w_out, doc_ids):
    tok_rows, col_width = hidden_in.shape
    tok_count = lax.axis_size("tok")
    tp_count = lax.axis_size("tp")
    if tp_count == 2 and tok_rows == 2 * HS and w_key.shape[1] % (2 * HS) == 0:
        return on_pairs(hidden_in, norm_gain, w_query, w_key, w_value, w_out, doc_ids)
    tok_index = lax.axis_index("tok")
    all_rows = tok_rows * tok_count
    full_in = both_sides(hidden_in)
    widened = full_in.astype(jnp.float32)
    factor = lax.rsqrt(jnp.mean(widened * widened, axis=1, keepdims=True) + epsilon)
    normed = (widened * factor * norm_gain[None, :]).astype(jnp.bfloat16)
    kv_heads = w_key.shape[1] // HS
    groups = w_query.shape[1] // w_key.shape[1]
    first_row = tok_index * tok_rows
    positions = first_row + jnp.arange(tok_rows, dtype=jnp.int32)
    key_local = rotate(
        jnp.dot(normed, w_key, preferred_element_type=jnp.float32).reshape(tok_rows, kv_heads, HS),
        positions % all_rows,
    )
    key_local = key_local.astype(jnp.bfloat16).reshape(tok_rows, kv_heads * HS)
    value_local = jnp.dot(normed, w_value, preferred_element_type=jnp.float32).astype(jnp.bfloat16)
    (kv_rows,) = ring_gather(jnp.stack([key_local, value_local]), False, 0)
    early, late = hidden_in[:, : col_width // 2], hidden_in[:, col_width // 2 :]
    late, kv_rows = lax.optimization_barrier((late, kv_rows))
    cols_in = [lax.all_gather(part, "tok", axis=0, tiled=True) for part in (early, late)]
    rows_in = lax.all_to_all(full_in, "tok", 1, 0, tiled=True)
    queries = rotate(
        jnp.dot(normed, w_query, preferred_element_type=jnp.float32).reshape(
            tok_rows, kv_heads * groups, HS
        ),
        positions % all_rows,
    )
    queries = queries.astype(jnp.bfloat16).reshape(tok_rows, kv_heads * groups * HS)
    query_doc = lax.dynamic_slice_in_dim(doc_ids, first_row, tok_rows, 0)
    lo = jnp.sum((doc_ids[None, :] < query_doc[:, None]).astype(jnp.int32), axis=1)
    bounds = jnp.stack([first_row.astype(jnp.int32), lo[0]])
    attended = attend(queries, kv_rows, jnp.broadcast_to(lo[:, None], (tok_rows, 128)), bounds, kv_heads)
    partial_out = jnp.dot(attended, w_out, preferred_element_type=jnp.float32)
    summed = lax.psum_scatter(partial_out, "tp", scatter_dimension=1, tiled=True)
    hidden_out = (hidden_in.astype(jnp.float32) + summed).astype(jnp.bfloat16)
    halves = jnp.stack([hidden_out[:, : col_width // 2], hidden_out[:, col_width // 2 :]])
    (cols_out,) = ring_gather(halves, False, 1)
    rows_out = row_features(cols_out, None)
    return (hidden_out, joint_gram(rows_in, rows_out, cols_in, cols_out))


def solution(mesh):
    return jax.shard_map(
        on_device,
        mesh=mesh,
        in_specs=(
            P("tok", "tp"),
            P(),
            P(None, "tp"),
            P(None, "tp"),
            P(None, "tp"),
            P("tp", None),
            P(),
        ),
        out_specs=(P("tok", "tp"), P(None, "tok", None, "tp")),
        check_vma=False,
    )
```

```python
import functools
import math

import jax
import jax.numpy as jnp
from jax import lax
from jax.experimental import pallas as pl
from jax.experimental.pallas import tpu as pltpu
from jax.sharding import PartitionSpec as P

HS = 128
epsilon = 1e-05
rope_base = 500000.0
VMEM_LIMIT = 60 * 1024 * 1024


def rotate(vectors, positions):
    half_dim = vectors.shape[-1] // 2
    inv_freq = rope_base ** (-(jnp.arange(half_dim, dtype=jnp.float32) * 2.0) / vectors.shape[-1])
    angles = positions.astype(jnp.float32)[:, None] * inv_freq[None, :]
    cosine = jnp.cos(angles)[:, None, :]
    sine_part = jnp.sin(angles)[:, None, :]
    first_half = vectors[..., :half_dim]
    second_half = vectors[..., half_dim:]
    return jnp.concatenate(
        [
            first_half * cosine - second_half * sine_part,
            second_half * cosine + first_half * sine_part,
        ],
        axis=-1,
    )


def attend_kernel(groups, block, bounds, q_ref, k_ref, v_ref, lo_ref, out_ref, s_ref, m_ref, l_ref, acc_ref):
    rows = q_ref.shape[0]
    first_row = bounds[0]
    scale = HS ** (-0.5) * math.log2(math.e)
    start = bounds[1] // block
    stop = (first_row + rows + block - 1) // block
    lanes = 128
    m_ref[...] = jnp.full_like(m_ref, -jnp.inf)
    l_ref[...] = jnp.zeros_like(l_ref)
    acc_ref[...] = jnp.zeros_like(acc_ref)

    @pl.loop(start, stop)
    def _(step):
        first_key = pl.multiple_of(step * block, block)
        keys = k_ref[pl.ds(first_key, block), :]
        key_pos = first_key + lax.broadcasted_iota(jnp.int32, (rows, block), 1)
        query_pos = first_row + lax.broadcasted_iota(jnp.int32, (rows, block), 0)
        allowed = (key_pos >= lo_ref[:, :1]) & (key_pos <= query_pos)
        for head in range(groups):
            part = pl.ds(head * rows, rows)
            s = lax.dot_general(
                q_ref[:, head * HS:(head + 1) * HS], keys,
                (((1,), (1,)), ((), ())), preferred_element_type=jnp.float32,
            ) * scale
            s = jnp.where(allowed, s, -jnp.inf)
            s_ref[step, part, :] = s
            top = m_ref[part, :]
            for piece in range(block // lanes):
                top = jnp.maximum(top, s[:, piece * lanes:(piece + 1) * lanes])
            m_ref[part, :] = top

    m_ref[...] = jnp.broadcast_to(jnp.max(m_ref[...], axis=-1, keepdims=True), m_ref.shape)

    @pl.loop(start, stop)
    def _(step):
        first_key = pl.multiple_of(step * block, block)
        values = v_ref[pl.ds(first_key, block), :]
        for head in range(groups):
            part = pl.ds(head * rows, rows)
            weights = jnp.exp2(s_ref[step, part, :] - m_ref[part, :1])
            total = l_ref[part, :]
            for piece in range(block // lanes):
                total = total + weights[:, piece * lanes:(piece + 1) * lanes]
            l_ref[part, :] = total
            acc_ref[part, :] += jnp.dot(
                weights.astype(jnp.bfloat16), values, preferred_element_type=jnp.float32
            )

    for head in range(groups):
        part = pl.ds(head * rows, rows)
        weight_sum = jnp.sum(l_ref[part, :], axis=-1, keepdims=True)
        out_ref[:, head * HS:(head + 1) * HS] = (acc_ref[part, :] / weight_sum).astype(out_ref.dtype)


def attend(queries, kv_rows, lo, bounds, kv_heads):
    rows, width = queries.shape
    all_rows = kv_rows.shape[1]
    groups = width // (kv_heads * HS)
    block = min(512, all_rows)
    wide = groups * HS
    return pl.pallas_call(
        functools.partial(attend_kernel, groups, block),
        out_shape=jax.ShapeDtypeStruct((rows, width), jnp.bfloat16),
        grid_spec=pltpu.PrefetchScalarGridSpec(
            num_scalar_prefetch=1,
            grid=(kv_heads,),
            in_specs=[
                pl.BlockSpec((rows, wide), lambda g, b: (0, g)),
                pl.BlockSpec((None, all_rows, HS), lambda g, b: (0, 0, g)),
                pl.BlockSpec((None, all_rows, HS), lambda g, b: (1, 0, g)),
                pl.BlockSpec((rows, 128), lambda g, b: (0, 0)),
            ],
            out_specs=pl.BlockSpec((rows, wide), lambda g, b: (0, g)),
            scratch_shapes=[
                pltpu.VMEM((all_rows // block, groups * rows, block), jnp.float32),
                pltpu.VMEM((groups * rows, 128), jnp.float32),
                pltpu.VMEM((groups * rows, 128), jnp.float32),
                pltpu.VMEM((groups * rows, HS), jnp.float32),
            ],
        ),
        compiler_params=pltpu.CompilerParams(
            dimension_semantics=("arbitrary",), vmem_limit_bytes=VMEM_LIMIT
        ),
        cost_estimate=pl.CostEstimate(
            flops=4 * rows * all_rows * width,
            bytes_accessed=2 * all_rows * kv_heads * HS * 2 + 4 * rows * width,
            transcendentals=rows * all_rows * width // HS,
        ),
        name="attend",
    )(bounds, queries, kv_rows, kv_rows, lo)


def gram_kernel(strips, rin_ref, rout_ref, low_ref, high_ref, cout_ref, out_ref, rt_ref, mean_ref):
    all_rows, row_width = rin_ref.shape

    @pl.when(pl.program_id(0) == 0)
    def _():
        ones = jnp.ones((all_rows, 128), jnp.bfloat16)
        for source, ref in enumerate((rin_ref, rout_ref)):
            part = pl.ds(source * row_width, row_width)
            rt_ref[part, :] = ref[...].T
            mean_ref[part, :] = (
                jnp.dot(rt_ref[part, :], ones, preferred_element_type=jnp.float32) / all_rows
            )

    ones = jnp.ones((8, all_rows), jnp.bfloat16)

    def block(source, ref):
        cols = ref[...]
        col_mean = jnp.dot(ones, cols, preferred_element_type=jnp.float32)[:1] / all_rows
        gram = jnp.dot(rt_ref[...], cols, preferred_element_type=jnp.float32)
        cov = gram / all_rows - mean_ref[:, :1] * col_mean
        for row_source in range(2):
            out_ref[row_source, :, source, :] = cov[row_source * row_width:(row_source + 1) * row_width]

    @pl.when(pl.program_id(0) < strips)
    def _():
        block(0, low_ref)

    @pl.when(pl.program_id(0) >= strips)
    def _():
        block(0, high_ref)

    block(1, cout_ref)


def joint_gram(rin, rout, cin, cout):
    all_rows, row_width = rin.shape
    half = cout.shape[2]
    col_width = 2 * half
    tile = min(256, half)
    strips = half // tile
    whole = pl.BlockSpec((all_rows, row_width), lambda j: (0, 0), pipeline_mode=pl.Buffered(1))
    strip = pl.BlockSpec((None, all_rows, tile), lambda j: (j // strips, 0, j % strips))
    low = pl.BlockSpec((all_rows, tile), lambda j: (0, jnp.minimum(j, strips - 1)))
    high = pl.BlockSpec((all_rows, tile), lambda j: (0, jnp.maximum(j - strips, 0)))
    return pl.pallas_call(
        functools.partial(gram_kernel, strips),
        out_shape=jax.ShapeDtypeStruct((2, row_width, 2, col_width), jnp.float32),
        grid=(col_width // tile,),
        in_specs=[whole, whole, low, high, strip],
        out_specs=pl.BlockSpec((2, row_width, 2, tile), lambda j: (0, 0, 0, j)),
        scratch_shapes=[
            pltpu.VMEM((2 * row_width, all_rows), jnp.bfloat16),
            pltpu.VMEM((2 * row_width, 128), jnp.float32),
        ],
        compiler_params=pltpu.CompilerParams(
            dimension_semantics=("arbitrary",), vmem_limit_bytes=VMEM_LIMIT
        ),
        cost_estimate=pl.CostEstimate(
            flops=8 * all_rows * row_width * col_width,
            bytes_accessed=4 * all_rows * (row_width + col_width) + 16 * row_width * col_width,
            transcendentals=0,
        ),
        name="joint_gram",
    )(rin, rout, *cin, cout)


def both_sides(block):
    if lax.axis_size("tp") != 2:
        return lax.all_gather(block, "tp", axis=1, tiled=True)
    other = lax.ppermute(block, "tp", ((0, 1), (1, 0)))
    first = lax.axis_index("tp") == 0
    return jnp.concatenate([jnp.where(first, block, other), jnp.where(first, other, block)], axis=1)


def ring_kernel(chips, share, x_ref, *refs):
    if share:
        out_ref, side_ref, send, recv, psend, precv, local, ssend, srecv = refs
    else:
        out_ref, send, recv, psend, precv, local = refs
    mesh_id = pl.DeviceIdType.MESH
    rows = x_ref.shape[1]
    me, tp = lax.axis_index("tok"), lax.axis_index("tp")
    count = 2 * chips
    core, chip = me % 2, me // 2
    depth = chips // 2
    spot = jnp.where(chip % 2 == 0, chip // 2, chips - 1 - chip // 2)

    def device(place):
        place = (place + 2 * chips) % chips
        return jnp.where(place < depth, place * 4, (chips - 1 - place) * 4 + 2) + core

    partner = me + 1 - 2 * core
    ways = (device(spot + 1), device(spot - 1))
    barrier = pltpu.get_barrier_semaphore()
    for peer in (*ways, partner):
        pl.semaphore_signal(barrier, inc=1, device_id={"tok": peer}, device_id_type=mesh_id)
    if share:
        pl.semaphore_signal(barrier, inc=1, device_id={"tp": 1 - tp}, device_id_type=mesh_id)
    pl.semaphore_wait(barrier, 4 if share else 3)

    def block(way, origin):
        return out_ref.at[way, pl.ds(pl.multiple_of(origin * rows, rows), rows), :]

    pending = []

    def step_copies(step, way):
        origin = device(spot - step if way == 0 else spot + step)
        source = x_ref.at[way] if step == 0 else block(way, origin)
        ring = None
        if step < chips - 1:
            ring = pltpu.make_async_remote_copy(
                src_ref=source, dst_ref=block(way, origin), send_sem=send.at[way, step],
                recv_sem=recv.at[way, step], device_id={"tok": ways[way]}, device_id_type=mesh_id,
            )
            ring.start()
        beside = pltpu.make_async_remote_copy(
            src_ref=source, dst_ref=block(way, origin), send_sem=psend.at[way, step],
            recv_sem=precv.at[way, step], device_id={"tok": partner}, device_id_type=mesh_id,
        )
        beside.start()
        pending.append((ring, beside))
        return ring

    rings = [step_copies(0, way) for way in range(2)]
    own = [pltpu.make_async_copy(x_ref.at[way], block(way, me), local.at[way]) for way in range(2)]
    for copy in own:
        copy.start()
    if share:
        width = side_ref.shape[1]
        half = x_ref.shape[2]
        owner = me // (count // 2)
        my_way = me * width % (2 * half) // half
        features = pl.ds(pl.multiple_of(me * width % half, width), width)

    def side_copy(step, way, kind):
        origin = device(spot - step if way == 0 else spot + step)
        origin = origin + kind * (1 - 2 * core)
        source = x_ref.at[way, :, features]
        if step > 0 or kind > 0:
            source = out_ref.at[way, pl.ds(pl.multiple_of(origin * rows, rows), rows), features]
        return pltpu.make_async_remote_copy(
            src_ref=source,
            dst_ref=side_ref.at[pl.ds(pl.multiple_of(origin * rows, rows), rows), :],
            send_sem=ssend.at[kind, step], recv_sem=srecv.at[kind, step],
            device_id={"tp": 1 - tp}, device_id_type=mesh_id,
        )

    def each_side(act, step, way, kind, holder):
        if share:
            @pl.when((my_way == way) & ((owner == tp) == holder))
            def _():
                act(side_copy(step, way, kind))

    def start(copy):
        copy.start()

    for way in range(2):
        each_side(start, 0, way, 0, True)
    for step in range(1, chips):
        for way in range(2):
            rings[way].wait_recv()
            rings[way] = step_copies(step, way)
            each_side(start, step, way, 0, True)
            pending[2 * (step - 1) + way][1].wait_recv()
            each_side(start, step - 1, way, 1, True)
    for way in range(2):
        pending[2 * (chips - 1) + way][1].wait_recv()
        each_side(start, chips - 1, way, 1, True)
    for ring, beside in pending:
        if ring is not None:
            ring.wait_send()
        beside.wait_send()
    for copy in own:
        copy.wait()
    for step in range(chips):
        for way in range(2):
            for kind in range(2):
                each_side(lambda copy: copy.wait_send(), step, way, kind, True)
                each_side(lambda copy: copy.wait_recv(), step, way, kind, False)


def ring_gather(halves, share, call_id):
    _, rows, width = halves.shape
    count = lax.axis_size("tok")
    chips = count // 2
    out_shape = [jax.ShapeDtypeStruct((2, rows * count, width), halves.dtype)]
    dma = pltpu.SemaphoreType.DMA
    scratch = [dma((2, chips))] * 4 + [dma((2,))]
    if share:
        out_shape.append(jax.ShapeDtypeStruct((rows * count, 4 * width // count), halves.dtype))
        scratch += [dma((2, chips))] * 2
    return pl.pallas_call(
        functools.partial(ring_kernel, chips, share),
        out_shape=out_shape,
        in_specs=[pl.BlockSpec(memory_space=pltpu.VMEM)],
        out_specs=[pl.BlockSpec(memory_space=pl.ANY)] * len(out_shape),
        scratch_shapes=scratch,
        compiler_params=pltpu.CompilerParams(
            collective_id=call_id, has_side_effects=True, vmem_limit_bytes=VMEM_LIMIT
        ),
        cost_estimate=pl.CostEstimate(
            flops=40_000_000_000, bytes_accessed=2 * halves.size * count * 2, transcendentals=0
        ),
        name="ring_share" if share else "ring",
    )(halves)


def row_features(columns, arrived):
    _, all_rows, half = columns.shape
    row_width = 2 * half * lax.axis_size("tp") // lax.axis_size("tok")
    first = lax.axis_index("tok") * row_width
    offset, owner = first % (2 * half), first // (2 * half)
    mine = lax.dynamic_slice(columns, (offset // half, 0, offset % half), (1, all_rows, row_width))[0]
    owned = lax.axis_index("tp") == owner
    if arrived is None:
        return lax.psum(jnp.where(owned, mine, jnp.zeros_like(mine)), "tp")
    return jnp.where(owned, mine, arrived)


SUBS = 2
SIDE_STEPS = 6
COV_SUBS = 2
MESH = pl.DeviceIdType.MESH


def ring_place(chips):
    me, tp = lax.axis_index("tok"), lax.axis_index("tp")
    core, chip = me % 2, me // 2
    spot = jnp.where(chip % 2 == 0, chip // 2, chips - 1 - chip // 2)

    def chip_at(place):
        place = (place + 2 * chips) % chips
        return jnp.where(place < chips // 2, place * 2, (chips - 1 - place) * 2 + 1)

    ahead = 1 - 2 * core
    return me, tp, core, spot, chip_at, ahead, chips


class Ring:
    def __init__(self, place, big, own, subs, sems, far=None, side=None, side_sems=None):
        self.me, self.tp, self.core, self.spot, self.chip_at, self.ahead, self.chips = place
        self.big, self.own, self.subs = big, own, subs
        self.rows = big.shape[0] // (2 * self.chips)
        self.part = self.rows // subs
        self.send, self.recv, self.psend, self.precv = sems
        self.far, self.side = far, side
        self.partner = self.me + 1 - 2 * self.core
        self.onward = self.chip_at(self.spot + self.ahead) * 2 + self.core
        self.back = self.chip_at(self.spot - self.ahead) * 2 + self.core
        if far is not None:
            self.ssend, self.srecv, self.tsend, self.trecv = side_sems
            width = big.shape[1]
            self.owner = self.me * side // width == self.tp
            self.feature = pl.multiple_of(self.me * side % width, side)
            self.partner_feature = pl.multiple_of(self.partner * side % width, side)

    def block(self, step, mine):
        turn = self.ahead if mine else -self.ahead
        return self.chip_at(self.spot - turn * step) * 2 + (self.core if mine else 1 - self.core)

    def block_row(self, step, mine):
        return pl.multiple_of(self.block(step, mine) * self.rows, self.rows)

    def span(self, step, sub):
        return pl.ds(pl.multiple_of(self.block_row(step, True) + sub * self.part, self.part), self.part)

    def source(self, step, sub):
        if self.own is not None and isinstance(step, int) and step == 0:
            return self.own.at[pl.ds(sub * self.part, self.part)]
        return self.big.at[self.span(step, sub)]

    def ring_copy(self, step, sub):
        return pltpu.make_async_remote_copy(
            src_ref=self.source(step, sub), dst_ref=self.big.at[self.span(step, sub)],
            send_sem=self.send.at[step, sub], recv_sem=self.recv.at[step, sub],
            device_id={"tok": self.onward}, device_id_type=MESH,
        )

    def beside_copy(self, step, sub):
        return pltpu.make_async_remote_copy(
            src_ref=self.source(step, sub), dst_ref=self.big.at[self.span(step, sub)],
            send_sem=self.psend.at[step, sub], recv_sem=self.precv.at[step, sub],
            device_id={"tok": self.partner}, device_id_type=MESH,
        )

    def side_copy(self, step, sub, same):
        wanted, target = (self.feature, self.me) if same else (self.partner_feature, self.partner)
        out_sem, in_sem = (self.ssend, self.srecv) if same else (self.tsend, self.trecv)
        return pltpu.make_async_remote_copy(
            src_ref=self.source(step, sub).at[:, pl.ds(wanted, self.side)],
            dst_ref=self.far.at[self.span(step, sub), :],
            send_sem=out_sem.at[step, sub], recv_sem=in_sem.at[step, sub],
            device_id={"tok": target, "tp": 1 - self.tp}, device_id_type=MESH,
        )

    def launch(self, step, sub):
        if isinstance(step, int):
            if step < self.chips - 1:
                self.ring_copy(step, sub).start()
        else:
            @pl.when(step < self.chips - 1)
            def _():
                self.ring_copy(step, sub).start()
        self.beside_copy(step, sub).start()

    def launch_side(self, step, sub):
        @pl.when(self.owner)
        def _():
            for same in (True, False):
                self.side_copy(step, sub, same).start()

    def event(self, step, sub):
        self.ring_copy(step - 1, sub).wait_recv()
        self.launch(step, sub)

    def beside_arrived(self, step):
        for sub in range(self.subs):
            self.beside_copy(step, sub).wait_recv()

    def side_arrived(self, step, mine):
        @pl.when(jnp.logical_not(self.owner))
        def _():
            for sub in range(self.subs):
                self.side_copy(step, sub, mine).wait_recv()

    def drain(self, side_steps=0):
        for step in range(self.chips):
            for sub in range(self.subs):
                if step < self.chips - 1:
                    self.ring_copy(step, sub).wait_send()
                self.beside_copy(step, sub).wait_send()
                if step < side_steps:
                    @pl.when(self.owner)
                    def _():
                        for same in (True, False):
                            self.side_copy(step, sub, same).wait_send()


def greet(ring):
    barrier = pltpu.get_barrier_semaphore()
    for peer in (ring.onward, ring.back, ring.partner):
        pl.semaphore_signal(barrier, inc=1, device_id={"tok": peer}, device_id_type=MESH)
    for peer in (ring.me, ring.partner):
        pl.semaphore_signal(
            barrier, inc=1, device_id={"tok": peer, "tp": 1 - ring.tp}, device_id_type=MESH
        )
    pl.semaphore_wait(barrier, 5)


def cov_kernel(chips, x_ref, cin_ref, rin_ref, *refs):
    acc_ref, rsum_ref, big, far, lt, cbuf, rbuf, late = refs[:8]
    sems, side_sems = refs[8:12], refs[12:16]
    own_sem, cin_sem, rin_sem, lsend, lrecv, ones_r = refs[16:]
    ring = Ring(ring_place(chips), big, x_ref, COV_SUBS, sems, far, rin_ref.shape[1], side_sems)
    rows, width = x_ref.shape
    side = ring.side
    owner = ring.owner
    greet(ring)
    for sub in range(COV_SUBS):
        ring.launch(0, sub)
        ring.launch_side(0, sub)
    own = pltpu.make_async_copy(x_ref, big.at[pl.ds(pl.multiple_of(ring.me * rows, rows), rows)], own_sem.at[0])
    own.start()

    def slot_of(step, mine):
        return step % 2 * 2 + (0 if mine else 1)

    def fetch_cols(step, mine):
        slot = slot_of(step, mine)
        place = pl.ds(ring.block_row(step, mine), rows)
        return pltpu.make_async_copy(cin_ref.at[place, :], cbuf.at[slot], cin_sem.at[slot])

    def fetch_strip(step, mine):
        slot = slot_of(step, mine)
        place = pl.ds(ring.block_row(step, mine), rows)
        return pltpu.make_async_copy(rin_ref.at[place, :], rbuf.at[slot], rin_sem.at[slot])

    def late_copy(step, same):
        wanted, target = (ring.feature, ring.me) if same else (ring.partner_feature, ring.partner)
        slot = (step - SIDE_STEPS) * 2 + (0 if same else 1)
        return pltpu.make_async_remote_copy(
            src_ref=cin_ref.at[pl.ds(ring.block_row(step, True), rows), pl.ds(wanted, side)],
            dst_ref=late.at[slot], send_sem=lsend.at[slot], recv_sem=lrecv.at[slot],
            device_id={"tok": target, "tp": 1 - ring.tp}, device_id_type=MESH,
        )

    def start_fetch(step, mine):
        fetch_cols(step, mine).start()
        if step < SIDE_STEPS:
            @pl.when(jnp.logical_not(owner))
            def _():
                fetch_strip(step, mine).start()

    for step in range(2):
        for mine in (True, False):
            start_fetch(step, mine)

    ones_r[...] = jnp.ones_like(ones_r)
    lt[2 * side:, :] = jnp.ones((lt.shape[0] - 2 * side, rows), lt.dtype)
    acc_ref[...] = jnp.zeros_like(acc_ref)
    rsum_ref[...] = jnp.zeros_like(rsum_ref)
    own.wait()
    tile = min(512, width)

    def work(step, mine):
        if not mine:
            ring.beside_arrived(step)
        ring.side_arrived(step, mine)
        slot = slot_of(step, mine)
        place = pl.ds(ring.block_row(step, mine), rows)
        fetch_cols(step, mine).wait()

        @pl.when(owner)
        def _():
            lt[0:side, :] = cbuf[slot, :, pl.ds(ring.feature, side)].T
            lt[side:2 * side, :] = big[place, pl.ds(ring.feature, side)].T

        @pl.when(jnp.logical_not(owner))
        def _():
            if step < SIDE_STEPS:
                fetch_strip(step, mine).wait()
                lt[0:side, :] = rbuf[slot].T
            else:
                late_copy(step, mine).wait_recv()
                lt[0:side, :] = late[(step - SIDE_STEPS) * 2 + (0 if mine else 1)].T
            lt[side:2 * side, :] = far[place, :].T

        rsum_ref[...] += jnp.dot(lt[0:2 * side, :], ones_r[...], preferred_element_type=jnp.float32)

        @pl.loop(0, width // tile)
        def _(i):
            here = pl.ds(pl.multiple_of(i * tile, tile), tile)
            acc_ref[:, here] += jnp.dot(
                lt[...], cbuf[slot, :, here], preferred_element_type=jnp.float32
            )
            there = pl.ds(pl.multiple_of(width + i * tile, tile), tile)
            acc_ref[:, there] += jnp.dot(
                lt[...], big[place, here], preferred_element_type=jnp.float32
            )

        if step + 2 < chips:
            start_fetch(step + 2, mine)

    for step in range(1, chips):
        for sub in range(COV_SUBS):
            ring.event(step, sub)
            ring.launch_side(step, sub)
            if sub == 0 and 1 <= step <= chips - SIDE_STEPS:
                @pl.when(owner)
                def _():
                    for same in (True, False):
                        late_copy(SIDE_STEPS + step - 1, same).start()
            if sub == COV_SUBS // 2 - 1:
                work(step - 1, True)
            if sub == (COV_SUBS // 2 if step == chips - 1 else COV_SUBS) - 1:
                work(step - 1, False)
    work(chips - 1, True)
    work(chips - 1, False)
    ring.drain(chips)

    @pl.when(owner)
    def _():
        for step in range(SIDE_STEPS, chips):
            for same in (True, False):
                late_copy(step, same).wait_send()


def finish_kernel(all_rows, strips, acc_ref, rsum_ref, x_ref, out_ref, y_ref):
    width = acc_ref.shape[1] // 2
    side = rsum_ref.shape[0] // 2
    tall = side // strips
    groups = 2 * width // 128
    part_of = 1.0 / all_rows
    y_ref[...] = x_ref[...]
    for row_source in range(2):
        for first in range(0, tall, 8):
            row = row_source * side + pl.program_id(0) * tall + first
            place = pl.ds(pl.multiple_of(row, 8), 8)
            mean_row = rsum_ref[place, :] * part_of
            pieces = []
            for j in range(width // 128):
                for source in range(2):
                    part = slice(source * width + j * 128, source * width + (j + 1) * 128)
                    mean_col = acc_ref[2 * side:2 * side + 1, part] * part_of
                    pieces.append(acc_ref[place, part] * part_of - mean_row * mean_col)
            turned = jnp.swapaxes(jnp.stack(pieces, axis=0), 0, 1)
            out_ref[row_source, first * groups:(first + 8) * groups, :] = turned.reshape(8 * groups, 128)


def joint_cov(hidden_out, rows_in, cols_in, call_id):
    rows, width = hidden_out.shape
    all_rows, side = cols_in.shape[0], rows_in.shape[1]
    chips = all_rows // rows // 2
    dma = pltpu.SemaphoreType.DMA
    tall = 2 * side + 16
    acc, rsum = pl.pallas_call(
        functools.partial(cov_kernel, chips),
        out_shape=[
            jax.ShapeDtypeStruct((tall, 2 * width), jnp.float32),
            jax.ShapeDtypeStruct((2 * side, 128), jnp.float32),
        ],
        in_specs=[pl.BlockSpec(memory_space=pltpu.VMEM)]
        + [pl.BlockSpec(memory_space=pl.ANY)] * 2,
        out_specs=[pl.BlockSpec(memory_space=pltpu.VMEM)] * 2,
        scratch_shapes=[
            pltpu.VMEM((all_rows, width), jnp.bfloat16),
            pltpu.VMEM((all_rows, side), jnp.bfloat16),
            pltpu.VMEM((tall, rows), jnp.bfloat16),
            pltpu.VMEM((4, rows, width), jnp.bfloat16),
            pltpu.VMEM((4, rows, side), jnp.bfloat16),
            pltpu.VMEM((2 * (chips - SIDE_STEPS), rows, side), jnp.bfloat16),
        ]
        + [dma((chips, COV_SUBS))] * 8
        + [dma((1,)), dma((4,)), dma((4,))]
        + [dma((2 * (chips - SIDE_STEPS),))] * 2
        + [pltpu.VMEM((rows, 128), jnp.bfloat16)],
        compiler_params=pltpu.CompilerParams(
            collective_id=call_id, has_side_effects=True, vmem_limit_bytes=38 * 1024 * 1024
        ),
        cost_estimate=pl.CostEstimate(
            flops=8 * all_rows * side * width * 4,
            bytes_accessed=4 * all_rows * (side + width) + 16 * side * width,
            transcendentals=0,
        ),
        name="cov_ring",
    )(hidden_out, cols_in, rows_in)
    cov, settled = finish(acc, rsum, hidden_out, side)
    return settled, cov


def finish(acc, rsum, hidden_out, side):
    rows, width = hidden_out.shape
    all_rows = rows * lax.axis_size("tok")
    strips = 8
    tall = side // strips
    groups = 2 * width // 128
    cov, settled = pl.pallas_call(
        functools.partial(finish_kernel, all_rows, strips),
        out_shape=[
            jax.ShapeDtypeStruct((2, side * groups, 128), jnp.float32),
            jax.ShapeDtypeStruct(hidden_out.shape, hidden_out.dtype),
        ],
        grid=(strips,),
        in_specs=[
            pl.BlockSpec(memory_space=pltpu.VMEM),
            pl.BlockSpec(memory_space=pltpu.VMEM),
            pl.BlockSpec((rows // strips, width), lambda i: (i, 0)),
        ],
        out_specs=[
            pl.BlockSpec((2, tall * groups, 128), lambda i: (0, i, 0)),
            pl.BlockSpec((rows // strips, width), lambda i: (i, 0)),
        ],
        compiler_params=pltpu.CompilerParams(
            dimension_semantics=("arbitrary",), vmem_limit_bytes=8 * 1024 * 1024
        ),
        name="finish",
    )(acc, rsum, hidden_out)
    cov = cov.reshape(2, side, width // 128, 2, 128).transpose(0, 1, 3, 2, 4)
    return cov.reshape(2, side, 2, width), settled


NEG = -1e30


def front_kernel(
    chips, kv_heads, groups, x_ref, gain_ref, cos_ref, sin_ref, kdoc_ref,
    wq_ref, wk_ref, wv_ref, wo_ref, out_ref, cin, far, other, normed, wkv, wq, wo, kv, q_ref,
    m_ref, l_ref, acc_ref, att, mine_sum, sent, arrived, bias, qdoc_ref, *sems
):
    place = ring_place(chips)
    hid_sems, side_sems, kv_sems = sems[0:4], sems[4:8], sems[8:12]
    xsend, xrecv, osend, orecv, own_sem, wkv_sem, wq_sem, wo_sem = sems[12:]
    rows, width = x_ref.shape
    side = far.shape[1]
    hid = Ring(place, cin, x_ref, SUBS, hid_sems, far, side, side_sems)
    ring = Ring(place, kv, None, SUBS, kv_sems)
    me, tp = hid.me, hid.tp
    half = rows // SUBS
    kv_width = kv_heads * HS
    scale = HS ** (-0.5) * math.log2(math.e)
    head_pair = 2 * HS
    q_tiles = kv_heads * groups // 2
    out_tile = width // 4

    def swap(sub):
        part = pl.ds(sub * half, half)
        return pltpu.make_async_remote_copy(
            src_ref=x_ref.at[part], dst_ref=other.at[part], send_sem=xsend.at[sub],
            recv_sem=xrecv.at[sub], device_id={"tp": 1 - tp}, device_id_type=MESH,
        )

    def fetch_q(t):
        col = pl.ds(pl.multiple_of(t * head_pair, head_pair), head_pair)
        return pltpu.make_async_copy(wq_ref.at[:, col], wq.at[t % 4], wq_sem.at[t % 4])

    def fetch_out(side_tp, i):
        col = pl.ds(pl.multiple_of(side_tp * width + i * out_tile, out_tile), out_tile)
        return pltpu.make_async_copy(wo_ref.at[:, col], wo.at[i], wo_sem.at[i])

    def out_part(i):
        return pl.ds(pl.multiple_of(i * out_tile, out_tile), out_tile)

    def give(i):
        return pltpu.make_async_remote_copy(
            src_ref=sent.at[:, out_part(i)], dst_ref=arrived.at[:, out_part(i)],
            send_sem=osend.at[i], recv_sem=orecv.at[i],
            device_id={"tp": 1 - tp}, device_id_type=MESH,
        )

    keys = [
        pltpu.make_async_copy(ref, wkv.at[:, pl.ds(i * kv_width, kv_width)], wkv_sem.at[i])
        for i, ref in enumerate((wk_ref, wv_ref))
    ]
    for copy in keys:
        copy.start()
    greet(hid)
    for sub in range(SUBS):
        swap(sub).start()
        hid.launch(0, sub)
    own = pltpu.make_async_copy(x_ref, cin.at[pl.ds(pl.multiple_of(me * rows, rows), rows)], own_sem.at[0])
    own.start()
    for t in range(4):
        fetch_q(t).start()
    for i in range(4):
        fetch_out(1 - tp, i).start()

    @pl.loop(0, kv_heads)
    def _(g):
        m_ref[g] = jnp.full(m_ref.shape[1:], NEG, jnp.float32)
        l_ref[g] = jnp.zeros(l_ref.shape[1:], jnp.float32)
        acc_ref[g] = jnp.zeros(acc_ref.shape[1:], jnp.float32)

    my_doc = kdoc_ref[:, pl.ds(pl.multiple_of(me * rows, rows), rows)]
    qdoc_ref[...] = jnp.broadcast_to(my_doc, (128, rows)).T
    my_cols = pl.ds(pl.multiple_of(tp * width, width), width)
    other_cols = pl.ds(pl.multiple_of((1 - tp) * width, width), width)

    def normalise(sub):
        @pl.loop(0, half // 32)
        def _(r):
            part = pl.ds(pl.multiple_of(sub * half + r * 32, 32), 32)
            near = x_ref[part, :].astype(jnp.float32)
            away = other[part, :].astype(jnp.float32)
            total = jnp.sum(near * near, axis=1, keepdims=True) + jnp.sum(away * away, axis=1, keepdims=True)
            factor = lax.rsqrt(total / (2 * width) + epsilon)
            normed[part, my_cols] = (near * factor * gain_ref[:, my_cols]).astype(jnp.bfloat16)
            normed[part, other_cols] = (away * factor * gain_ref[:, other_cols]).astype(jnp.bfloat16)

    def turned(vectors):
        return vectors * cos_ref[...] + pltpu.roll(vectors, HS // 2, 1) * sin_ref[...]

    hid.event(1, 0)
    hid.event(1, 1)
    swap(0).wait_recv()
    normalise(0)
    hid.event(2, 0)
    hid.event(2, 1)
    swap(1).wait_recv()
    normalise(1)
    for copy in keys:
        copy.wait()
    my_base = pl.multiple_of(me * 2 * kv_width, 2 * kv_width)

    @pl.loop(0, kv_width // head_pair)
    def _(t):
        col = pl.multiple_of(t * head_pair, head_pair)
        found = jnp.dot(normed[...], wkv[:, pl.ds(col, head_pair)], preferred_element_type=jnp.float32)
        for j in range(2):
            piece = turned(found[:, j * HS:(j + 1) * HS])
            kv[pl.ds(pl.multiple_of(my_base + col + j * HS, HS), HS), :] = piece.T.astype(jnp.bfloat16)


    @pl.loop(0, kv_width // head_pair)
    def _(t):
        col = pl.multiple_of(kv_width + t * head_pair, head_pair)
        found = jnp.dot(normed[...], wkv[:, pl.ds(col, head_pair)], preferred_element_type=jnp.float32)
        kv[pl.ds(pl.multiple_of(my_base + col, head_pair), rows), :] = found.astype(jnp.bfloat16)

        @pl.when(t == 0)
        def _():
            ring.launch(0, 0)

    ring.launch(0, 1)
    for step in range(3):
        for sub in range(SUBS):
            hid.launch_side(step, sub)

    @pl.loop(0, q_tiles)
    def _(t):
        fetch_q(t).wait()
        found = jnp.dot(normed[...], wq[t % 4], preferred_element_type=jnp.float32)
        for j in range(2):
            head = t * 2 + j
            row = pl.multiple_of(head % groups * rows, rows)
            q_ref[head // groups, pl.ds(row, rows), :] = turned(found[:, j * HS:(j + 1) * HS]).astype(jnp.bfloat16)

        @pl.when(t + 4 < q_tiles)
        def _():
            fetch_q(t + 4).start()

        @pl.when(t == q_tiles // 2)
        def _():
            ring.event(1, 0)

    ring.event(1, 1)

    def make_bias(blocks):
        for i, block in enumerate(blocks):
            row = pl.multiple_of(block * rows, rows)
            key_pos = row + lax.broadcasted_iota(jnp.int32, (rows, rows), 1)
            query_pos = me * rows + lax.broadcasted_iota(jnp.int32, (rows, rows), 0)
            allowed = (kdoc_ref[:, pl.ds(row, rows)] == qdoc_ref[:, :1]) & (key_pos <= query_pos)
            bias[:, i * rows:(i + 1) * rows] = jnp.where(allowed, 0.0, NEG)

    def pair_attention(blocks, heads):
        @pl.loop(*heads)
        def _(g):
            k_row, v_row = g * HS, kv_width + g // 2 * rows
            v_col = pl.ds(pl.multiple_of(g % 2 * HS, HS), HS)
            k = jnp.concatenate(
                [kv[pl.ds(pl.multiple_of(b * 2 * kv_width + k_row, HS), HS), :] for b in blocks], axis=1
            )
            v = jnp.concatenate(
                [kv[pl.ds(pl.multiple_of(b * 2 * kv_width + v_row, rows), rows), v_col] for b in blocks],
                axis=0,
            )
            for head in range(groups):
                part = pl.ds(head * rows, rows)
                s = jnp.dot(q_ref[g, part, :], k, preferred_element_type=jnp.float32) * scale + bias[...]
                old = m_ref[g, part, :]
                pieces = [s[:, i:i + 128] for i in range(0, 2 * rows, 128)]
                peak = functools.reduce(jnp.maximum, pieces)
                top = jnp.maximum(old, jnp.max(peak, axis=-1, keepdims=True))
                fade = jnp.exp2(old - top)
                weights = [jnp.exp2(piece - top) for piece in pieces]
                l_ref[g, part, :] = l_ref[g, part, :] * fade + functools.reduce(jnp.add, weights)
                m_ref[g, part, :] = top
                acc_ref[g, part, :] = acc_ref[g, part, :] * fade + jnp.dot(
                    jnp.concatenate(weights, axis=1).astype(jnp.bfloat16), v,
                    preferred_element_type=jnp.float32,
                )

    @pl.loop(0, chips * SUBS)
    def _(turn):
        step, sub = turn // SUBS, turn % SUBS

        @pl.when(step + 2 < chips)
        def _():
            ring.event(step + 2, sub)


        @pl.when((step + 2 == chips - 2) & (sub == 1))
        def _():
            for part in range(SUBS):
                hid.event(3, part)
                hid.launch_side(3, part)

        @pl.when(step + 2 == chips + 1)
        def _():
            hid.event(4, sub)
            hid.launch_side(4, sub)

        blocks = (ring.block(step, True), ring.block(step, False))
        needed = (blocks[0] <= me) | (blocks[1] <= me)

        @pl.when(sub == 0)
        def _():
            ring.beside_arrived(step)

        @pl.when((sub == 0) & needed)
        def _():
            make_bias(blocks)

        @pl.when(needed)
        def _():
            pair_attention(blocks, (sub * (kv_heads // SUBS), (sub + 1) * (kv_heads // SUBS)))

    @pl.loop(0, kv_heads)
    def _(g):
        for head in range(groups):
            part = pl.ds(head * rows, rows)
            weight_sum = jnp.sum(l_ref[g, part, :], axis=-1, keepdims=True)
            col = pl.ds(pl.multiple_of((g * groups + head) * HS, HS), HS)
            att[:, col] = (acc_ref[g, part, :] / weight_sum).astype(jnp.bfloat16)

    @pl.loop(0, 4)
    def _(i):
        fetch_out(1 - tp, i).wait()
        found = jnp.dot(att[...], wo[i], preferred_element_type=jnp.float32)
        sent[:, out_part(i)] = found.astype(jnp.bfloat16)

        @pl.when(i > 0)
        def _():
            give(i - 1).start()

        fetch_out(tp, i).start()

    give(3).start()
    for i in range(2):
        hid.event(5, i)
        hid.launch_side(5, i)
    hid.event(6, 0)

    @pl.loop(0, 4)
    def _(i):
        fetch_out(tp, i).wait()
        mine_sum[:, out_part(i)] = jnp.dot(att[...], wo[i], preferred_element_type=jnp.float32)

    hid.event(6, 1)

    def settle(i):
        give(i).wait_recv()
        summed = mine_sum[:, out_part(i)] + arrived[:, out_part(i)].astype(jnp.float32)
        out_ref[:, out_part(i)] = (x_ref[:, out_part(i)].astype(jnp.float32) + summed).astype(jnp.bfloat16)

    pl.loop(0, 4)(settle)
    for sub in range(SUBS):
        hid.event(7, sub)
    own.wait()
    for step in range(chips):
        hid.beside_arrived(step)
        if step < SIDE_STEPS:
            for mine in (True, False):
                hid.side_arrived(step, mine)
    hid.drain(SIDE_STEPS)
    ring.drain()
    for sub in range(SUBS):
        swap(sub).wait_send()
    for i in range(4):
        give(i).wait_send()


def front(hidden_in, norm_gain, cosine, sine, doc_ids, w_query, w_key, w_value, w_out, call_id):
    rows, width = hidden_in.shape
    all_rows = doc_ids.shape[1]
    chips = all_rows // rows // 2
    side = width * 2 // (2 * chips)
    kv_heads = w_key.shape[1] // HS
    groups = w_query.shape[1] // w_key.shape[1]
    dma = pltpu.SemaphoreType.DMA
    bf16, f32 = jnp.bfloat16, jnp.float32
    stacked = (kv_heads, groups * rows, HS)
    return pl.pallas_call(
        functools.partial(front_kernel, chips, kv_heads, groups),
        out_shape=[
            jax.ShapeDtypeStruct((rows, width), bf16),
            jax.ShapeDtypeStruct((all_rows, width), bf16),
            jax.ShapeDtypeStruct((8 * all_rows, side), bf16),
        ],
        in_specs=[pl.BlockSpec(memory_space=pltpu.VMEM)] * 5 + [pl.BlockSpec(memory_space=pl.ANY)] * 4,
        out_specs=[pl.BlockSpec(memory_space=pltpu.VMEM)] + [pl.BlockSpec(memory_space=pl.ANY)] * 2,
        scratch_shapes=[
            pltpu.VMEM((rows, width), bf16),
            pltpu.VMEM((rows, 2 * width), bf16),
            pltpu.VMEM((2 * width, 2 * w_key.shape[1]), bf16),
            pltpu.VMEM((4, 2 * width, 2 * HS), bf16),
            pltpu.VMEM((4, w_out.shape[0], width // 4), bf16),
            pltpu.VMEM((all_rows // rows * 2 * w_key.shape[1], rows), bf16),
            pltpu.VMEM(stacked, bf16),
            pltpu.VMEM(stacked, f32),
            pltpu.VMEM(stacked, f32),
            pltpu.VMEM(stacked, f32),
            pltpu.VMEM((rows, w_out.shape[0]), bf16),
            pltpu.VMEM((rows, width), f32),
            pltpu.VMEM((rows, width), bf16),
            pltpu.VMEM((rows, width), bf16),
            pltpu.VMEM((rows, 2 * rows), f32),
            pltpu.VMEM((rows, 128), jnp.int32),
        ]
        + [dma((chips, SUBS))] * 12
        + [dma((SUBS,))] * 2
        + [dma((4,))] * 2
        + [dma((1,)), dma((2,)), dma((4,)), dma((4,))],
        compiler_params=pltpu.CompilerParams(
            collective_id=call_id, has_side_effects=True, vmem_limit_bytes=52 * 1024 * 1024
        ),
        name="front",
    )(hidden_in, norm_gain, cosine, sine, doc_ids, w_query, w_key, w_value, w_out)


def on_pairs(hidden_in, norm_gain, w_query, w_key, w_value, w_out, doc_ids):
    rows = hidden_in.shape[0]
    first_row = lax.axis_index("tok") * rows
    positions = (first_row + jnp.arange(rows, dtype=jnp.int32)) % doc_ids.shape[0]
    lane = jnp.arange(HS, dtype=jnp.int32)
    pair = (lane % (HS // 2)).astype(jnp.float32)
    inv_freq = rope_base ** (-(pair * 2.0) / HS)
    angles = positions.astype(jnp.float32)[:, None] * inv_freq[None, :]
    sine = jnp.sin(angles) * jnp.where(lane < HS // 2, -1.0, 1.0)[None, :]
    hidden_out, cols_in, rows_in = front(
        hidden_in, norm_gain[None, :], jnp.cos(angles), sine, doc_ids[None, :],
        w_query, w_key, w_value, w_out, 0,
    )
    return joint_cov(hidden_out, rows_in, cols_in, 1)


def on_device(hidden_in, norm_gain, w_query, w_key, w_value, w_out, doc_ids):
    tok_rows, col_width = hidden_in.shape
    tok_count = lax.axis_size("tok")
    tp_count = lax.axis_size("tp")
    if tp_count == 2 and tok_rows == 2 * HS and w_key.shape[1] % (2 * HS) == 0:
        return on_pairs(hidden_in, norm_gain, w_query, w_key, w_value, w_out, doc_ids)
    tok_index = lax.axis_index("tok")
    all_rows = tok_rows * tok_count
    full_in = both_sides(hidden_in)
    widened = full_in.astype(jnp.float32)
    factor = lax.rsqrt(jnp.mean(widened * widened, axis=1, keepdims=True) + epsilon)
    normed = (widened * factor * norm_gain[None, :]).astype(jnp.bfloat16)
    kv_heads = w_key.shape[1] // HS
    groups = w_query.shape[1] // w_key.shape[1]
    first_row = tok_index * tok_rows
    positions = first_row + jnp.arange(tok_rows, dtype=jnp.int32)
    key_local = rotate(
        jnp.dot(normed, w_key, preferred_element_type=jnp.float32).reshape(tok_rows, kv_heads, HS),
        positions % all_rows,
    )
    key_local = key_local.astype(jnp.bfloat16).reshape(tok_rows, kv_heads * HS)
    value_local = jnp.dot(normed, w_value, preferred_element_type=jnp.float32).astype(jnp.bfloat16)
    (kv_rows,) = ring_gather(jnp.stack([key_local, value_local]), False, 0)
    early, late = hidden_in[:, : col_width // 2], hidden_in[:, col_width // 2 :]
    late, kv_rows = lax.optimization_barrier((late, kv_rows))
    cols_in = [lax.all_gather(part, "tok", axis=0, tiled=True) for part in (early, late)]
    rows_in = lax.all_to_all(full_in, "tok", 1, 0, tiled=True)
    queries = rotate(
        jnp.dot(normed, w_query, preferred_element_type=jnp.float32).reshape(
            tok_rows, kv_heads * groups, HS
        ),
        positions % all_rows,
    )
    queries = queries.astype(jnp.bfloat16).reshape(tok_rows, kv_heads * groups * HS)
    query_doc = lax.dynamic_slice_in_dim(doc_ids, first_row, tok_rows, 0)
    lo = jnp.sum((doc_ids[None, :] < query_doc[:, None]).astype(jnp.int32), axis=1)
    bounds = jnp.stack([first_row.astype(jnp.int32), lo[0]])
    attended = attend(queries, kv_rows, jnp.broadcast_to(lo[:, None], (tok_rows, 128)), bounds, kv_heads)
    partial_out = jnp.dot(attended, w_out, preferred_element_type=jnp.float32)
    summed = lax.psum_scatter(partial_out, "tp", scatter_dimension=1, tiled=True)
    hidden_out = (hidden_in.astype(jnp.float32) + summed).astype(jnp.bfloat16)
    halves = jnp.stack([hidden_out[:, : col_width // 2], hidden_out[:, col_width // 2 :]])
    (cols_out,) = ring_gather(halves, False, 1)
    rows_out = row_features(cols_out, None)
    return (hidden_out, joint_gram(rows_in, rows_out, cols_in, cols_out))


def solution(mesh):
    return jax.shard_map(
        on_device,
        mesh=mesh,
        in_specs=(
            P("tok", "tp"),
            P(),
            P(None, "tp"),
            P(None, "tp"),
            P(None, "tp"),
            P("tp", None),
            P(),
        ),
        out_specs=(P("tok", "tp"), P(None, "tok", None, "tp")),
        check_vma=False,
    )
```

```python
import functools
import math

import jax
import jax.numpy as jnp
from jax import lax
from jax.experimental import pallas as pl
from jax.experimental.pallas import tpu as pltpu
from jax.sharding import PartitionSpec as P

HS = 128
epsilon = 1e-05
rope_base = 500000.0
VMEM_LIMIT = 60 * 1024 * 1024


def rotate(vectors, positions):
    half_dim = vectors.shape[-1] // 2
    inv_freq = rope_base ** (-(jnp.arange(half_dim, dtype=jnp.float32) * 2.0) / vectors.shape[-1])
    angles = positions.astype(jnp.float32)[:, None] * inv_freq[None, :]
    cosine = jnp.cos(angles)[:, None, :]
    sine_part = jnp.sin(angles)[:, None, :]
    first_half = vectors[..., :half_dim]
    second_half = vectors[..., half_dim:]
    return jnp.concatenate(
        [
            first_half * cosine - second_half * sine_part,
            second_half * cosine + first_half * sine_part,
        ],
        axis=-1,
    )


def attend_kernel(groups, block, bounds, q_ref, k_ref, v_ref, lo_ref, out_ref, s_ref, m_ref, l_ref, acc_ref):
    rows = q_ref.shape[0]
    first_row = bounds[0]
    scale = HS ** (-0.5) * math.log2(math.e)
    start = bounds[1] // block
    stop = (first_row + rows + block - 1) // block
    lanes = 128
    m_ref[...] = jnp.full_like(m_ref, -jnp.inf)
    l_ref[...] = jnp.zeros_like(l_ref)
    acc_ref[...] = jnp.zeros_like(acc_ref)

    @pl.loop(start, stop)
    def _(step):
        first_key = pl.multiple_of(step * block, block)
        keys = k_ref[pl.ds(first_key, block), :]
        key_pos = first_key + lax.broadcasted_iota(jnp.int32, (rows, block), 1)
        query_pos = first_row + lax.broadcasted_iota(jnp.int32, (rows, block), 0)
        allowed = (key_pos >= lo_ref[:, :1]) & (key_pos <= query_pos)
        for head in range(groups):
            part = pl.ds(head * rows, rows)
            s = lax.dot_general(
                q_ref[:, head * HS:(head + 1) * HS], keys,
                (((1,), (1,)), ((), ())), preferred_element_type=jnp.float32,
            ) * scale
            s = jnp.where(allowed, s, -jnp.inf)
            s_ref[step, part, :] = s
            top = m_ref[part, :]
            for piece in range(block // lanes):
                top = jnp.maximum(top, s[:, piece * lanes:(piece + 1) * lanes])
            m_ref[part, :] = top

    m_ref[...] = jnp.broadcast_to(jnp.max(m_ref[...], axis=-1, keepdims=True), m_ref.shape)

    @pl.loop(start, stop)
    def _(step):
        first_key = pl.multiple_of(step * block, block)
        values = v_ref[pl.ds(first_key, block), :]
        for head in range(groups):
            part = pl.ds(head * rows, rows)
            weights = jnp.exp2(s_ref[step, part, :] - m_ref[part, :1])
            total = l_ref[part, :]
            for piece in range(block // lanes):
                total = total + weights[:, piece * lanes:(piece + 1) * lanes]
            l_ref[part, :] = total
            acc_ref[part, :] += jnp.dot(
                weights.astype(jnp.bfloat16), values, preferred_element_type=jnp.float32
            )

    for head in range(groups):
        part = pl.ds(head * rows, rows)
        weight_sum = jnp.sum(l_ref[part, :], axis=-1, keepdims=True)
        out_ref[:, head * HS:(head + 1) * HS] = (acc_ref[part, :] / weight_sum).astype(out_ref.dtype)


def attend(queries, kv_rows, lo, bounds, kv_heads):
    rows, width = queries.shape
    all_rows = kv_rows.shape[1]
    groups = width // (kv_heads * HS)
    block = min(512, all_rows)
    wide = groups * HS
    return pl.pallas_call(
        functools.partial(attend_kernel, groups, block),
        out_shape=jax.ShapeDtypeStruct((rows, width), jnp.bfloat16),
        grid_spec=pltpu.PrefetchScalarGridSpec(
            num_scalar_prefetch=1,
            grid=(kv_heads,),
            in_specs=[
                pl.BlockSpec((rows, wide), lambda g, b: (0, g)),
                pl.BlockSpec((None, all_rows, HS), lambda g, b: (0, 0, g)),
                pl.BlockSpec((None, all_rows, HS), lambda g, b: (1, 0, g)),
                pl.BlockSpec((rows, 128), lambda g, b: (0, 0)),
            ],
            out_specs=pl.BlockSpec((rows, wide), lambda g, b: (0, g)),
            scratch_shapes=[
                pltpu.VMEM((all_rows // block, groups * rows, block), jnp.float32),
                pltpu.VMEM((groups * rows, 128), jnp.float32),
                pltpu.VMEM((groups * rows, 128), jnp.float32),
                pltpu.VMEM((groups * rows, HS), jnp.float32),
            ],
        ),
        compiler_params=pltpu.CompilerParams(
            dimension_semantics=("arbitrary",), vmem_limit_bytes=VMEM_LIMIT
        ),
        cost_estimate=pl.CostEstimate(
            flops=4 * rows * all_rows * width,
            bytes_accessed=2 * all_rows * kv_heads * HS * 2 + 4 * rows * width,
            transcendentals=rows * all_rows * width // HS,
        ),
        name="attend",
    )(bounds, queries, kv_rows, kv_rows, lo)


def gram_kernel(strips, rin_ref, rout_ref, low_ref, high_ref, cout_ref, out_ref, rt_ref, mean_ref):
    all_rows, row_width = rin_ref.shape

    @pl.when(pl.program_id(0) == 0)
    def _():
        ones = jnp.ones((all_rows, 128), jnp.bfloat16)
        for source, ref in enumerate((rin_ref, rout_ref)):
            part = pl.ds(source * row_width, row_width)
            rt_ref[part, :] = ref[...].T
            mean_ref[part, :] = (
                jnp.dot(rt_ref[part, :], ones, preferred_element_type=jnp.float32) / all_rows
            )

    ones = jnp.ones((8, all_rows), jnp.bfloat16)

    def block(source, ref):
        cols = ref[...]
        col_mean = jnp.dot(ones, cols, preferred_element_type=jnp.float32)[:1] / all_rows
        gram = jnp.dot(rt_ref[...], cols, preferred_element_type=jnp.float32)
        cov = gram / all_rows - mean_ref[:, :1] * col_mean
        for row_source in range(2):
            out_ref[row_source, :, source, :] = cov[row_source * row_width:(row_source + 1) * row_width]

    @pl.when(pl.program_id(0) < strips)
    def _():
        block(0, low_ref)

    @pl.when(pl.program_id(0) >= strips)
    def _():
        block(0, high_ref)

    block(1, cout_ref)


def joint_gram(rin, rout, cin, cout):
    all_rows, row_width = rin.shape
    half = cout.shape[2]
    col_width = 2 * half
    tile = min(256, half)
    strips = half // tile
    whole = pl.BlockSpec((all_rows, row_width), lambda j: (0, 0), pipeline_mode=pl.Buffered(1))
    strip = pl.BlockSpec((None, all_rows, tile), lambda j: (j // strips, 0, j % strips))
    low = pl.BlockSpec((all_rows, tile), lambda j: (0, jnp.minimum(j, strips - 1)))
    high = pl.BlockSpec((all_rows, tile), lambda j: (0, jnp.maximum(j - strips, 0)))
    return pl.pallas_call(
        functools.partial(gram_kernel, strips),
        out_shape=jax.ShapeDtypeStruct((2, row_width, 2, col_width), jnp.float32),
        grid=(col_width // tile,),
        in_specs=[whole, whole, low, high, strip],
        out_specs=pl.BlockSpec((2, row_width, 2, tile), lambda j: (0, 0, 0, j)),
        scratch_shapes=[
            pltpu.VMEM((2 * row_width, all_rows), jnp.bfloat16),
            pltpu.VMEM((2 * row_width, 128), jnp.float32),
        ],
        compiler_params=pltpu.CompilerParams(
            dimension_semantics=("arbitrary",), vmem_limit_bytes=VMEM_LIMIT
        ),
        cost_estimate=pl.CostEstimate(
            flops=8 * all_rows * row_width * col_width,
            bytes_accessed=4 * all_rows * (row_width + col_width) + 16 * row_width * col_width,
            transcendentals=0,
        ),
        name="joint_gram",
    )(rin, rout, *cin, cout)


def both_sides(block):
    if lax.axis_size("tp") != 2:
        return lax.all_gather(block, "tp", axis=1, tiled=True)
    other = lax.ppermute(block, "tp", ((0, 1), (1, 0)))
    first = lax.axis_index("tp") == 0
    return jnp.concatenate([jnp.where(first, block, other), jnp.where(first, other, block)], axis=1)


def ring_kernel(chips, share, x_ref, *refs):
    if share:
        out_ref, side_ref, send, recv, psend, precv, local, ssend, srecv = refs
    else:
        out_ref, send, recv, psend, precv, local = refs
    mesh_id = pl.DeviceIdType.MESH
    rows = x_ref.shape[1]
    me, tp = lax.axis_index("tok"), lax.axis_index("tp")
    count = 2 * chips
    core, chip = me % 2, me // 2
    depth = chips // 2
    spot = jnp.where(chip % 2 == 0, chip // 2, chips - 1 - chip // 2)

    def device(place):
        place = (place + 2 * chips) % chips
        return jnp.where(place < depth, place * 4, (chips - 1 - place) * 4 + 2) + core

    partner = me + 1 - 2 * core
    ways = (device(spot + 1), device(spot - 1))
    barrier = pltpu.get_barrier_semaphore()
    for peer in (*ways, partner):
        pl.semaphore_signal(barrier, inc=1, device_id={"tok": peer}, device_id_type=mesh_id)
    if share:
        pl.semaphore_signal(barrier, inc=1, device_id={"tp": 1 - tp}, device_id_type=mesh_id)
    pl.semaphore_wait(barrier, 4 if share else 3)

    def block(way, origin):
        return out_ref.at[way, pl.ds(pl.multiple_of(origin * rows, rows), rows), :]

    pending = []

    def step_copies(step, way):
        origin = device(spot - step if way == 0 else spot + step)
        source = x_ref.at[way] if step == 0 else block(way, origin)
        ring = None
        if step < chips - 1:
            ring = pltpu.make_async_remote_copy(
                src_ref=source, dst_ref=block(way, origin), send_sem=send.at[way, step],
                recv_sem=recv.at[way, step], device_id={"tok": ways[way]}, device_id_type=mesh_id,
            )
            ring.start()
        beside = pltpu.make_async_remote_copy(
            src_ref=source, dst_ref=block(way, origin), send_sem=psend.at[way, step],
            recv_sem=precv.at[way, step], device_id={"tok": partner}, device_id_type=mesh_id,
        )
        beside.start()
        pending.append((ring, beside))
        return ring

    rings = [step_copies(0, way) for way in range(2)]
    own = [pltpu.make_async_copy(x_ref.at[way], block(way, me), local.at[way]) for way in range(2)]
    for copy in own:
        copy.start()
    if share:
        width = side_ref.shape[1]
        half = x_ref.shape[2]
        owner = me // (count // 2)
        my_way = me * width % (2 * half) // half
        features = pl.ds(pl.multiple_of(me * width % half, width), width)

    def side_copy(step, way, kind):
        origin = device(spot - step if way == 0 else spot + step)
        origin = origin + kind * (1 - 2 * core)
        source = x_ref.at[way, :, features]
        if step > 0 or kind > 0:
            source = out_ref.at[way, pl.ds(pl.multiple_of(origin * rows, rows), rows), features]
        return pltpu.make_async_remote_copy(
            src_ref=source,
            dst_ref=side_ref.at[pl.ds(pl.multiple_of(origin * rows, rows), rows), :],
            send_sem=ssend.at[kind, step], recv_sem=srecv.at[kind, step],
            device_id={"tp": 1 - tp}, device_id_type=mesh_id,
        )

    def each_side(act, step, way, kind, holder):
        if share:
            @pl.when((my_way == way) & ((owner == tp) == holder))
            def _():
                act(side_copy(step, way, kind))

    def start(copy):
        copy.start()

    for way in range(2):
        each_side(start, 0, way, 0, True)
    for step in range(1, chips):
        for way in range(2):
            rings[way].wait_recv()
            rings[way] = step_copies(step, way)
            each_side(start, step, way, 0, True)
            pending[2 * (step - 1) + way][1].wait_recv()
            each_side(start, step - 1, way, 1, True)
    for way in range(2):
        pending[2 * (chips - 1) + way][1].wait_recv()
        each_side(start, chips - 1, way, 1, True)
    for ring, beside in pending:
        if ring is not None:
            ring.wait_send()
        beside.wait_send()
    for copy in own:
        copy.wait()
    for step in range(chips):
        for way in range(2):
            for kind in range(2):
                each_side(lambda copy: copy.wait_send(), step, way, kind, True)
                each_side(lambda copy: copy.wait_recv(), step, way, kind, False)


def ring_gather(halves, share, call_id):
    _, rows, width = halves.shape
    count = lax.axis_size("tok")
    chips = count // 2
    out_shape = [jax.ShapeDtypeStruct((2, rows * count, width), halves.dtype)]
    dma = pltpu.SemaphoreType.DMA
    scratch = [dma((2, chips))] * 4 + [dma((2,))]
    if share:
        out_shape.append(jax.ShapeDtypeStruct((rows * count, 4 * width // count), halves.dtype))
        scratch += [dma((2, chips))] * 2
    return pl.pallas_call(
        functools.partial(ring_kernel, chips, share),
        out_shape=out_shape,
        in_specs=[pl.BlockSpec(memory_space=pltpu.VMEM)],
        out_specs=[pl.BlockSpec(memory_space=pl.ANY)] * len(out_shape),
        scratch_shapes=scratch,
        compiler_params=pltpu.CompilerParams(
            collective_id=call_id, has_side_effects=True, vmem_limit_bytes=VMEM_LIMIT
        ),
        cost_estimate=pl.CostEstimate(
            flops=40_000_000_000, bytes_accessed=2 * halves.size * count * 2, transcendentals=0
        ),
        name="ring_share" if share else "ring",
    )(halves)


def row_features(columns, arrived):
    _, all_rows, half = columns.shape
    row_width = 2 * half * lax.axis_size("tp") // lax.axis_size("tok")
    first = lax.axis_index("tok") * row_width
    offset, owner = first % (2 * half), first // (2 * half)
    mine = lax.dynamic_slice(columns, (offset // half, 0, offset % half), (1, all_rows, row_width))[0]
    owned = lax.axis_index("tp") == owner
    if arrived is None:
        return lax.psum(jnp.where(owned, mine, jnp.zeros_like(mine)), "tp")
    return jnp.where(owned, mine, arrived)


SUBS = 2
SIDE_STEPS = 6
COV_SUBS = 2
MESH = pl.DeviceIdType.MESH


def ring_place(chips):
    me, tp = lax.axis_index("tok"), lax.axis_index("tp")
    core, chip = me % 2, me // 2
    spot = jnp.where(chip % 2 == 0, chip // 2, chips - 1 - chip // 2)

    def chip_at(place):
        place = (place + 2 * chips) % chips
        return jnp.where(place < chips // 2, place * 2, (chips - 1 - place) * 2 + 1)

    ahead = 1 - 2 * core
    return me, tp, core, spot, chip_at, ahead, chips


class Ring:
    def __init__(self, place, big, own, subs, sems, far=None, side=None, side_sems=None):
        self.me, self.tp, self.core, self.spot, self.chip_at, self.ahead, self.chips = place
        self.big, self.own, self.subs = big, own, subs
        self.rows = big.shape[0] // (2 * self.chips)
        self.part = self.rows // subs
        self.send, self.recv, self.psend, self.precv = sems
        self.far, self.side = far, side
        self.partner = self.me + 1 - 2 * self.core
        self.onward = self.chip_at(self.spot + self.ahead) * 2 + self.core
        self.back = self.chip_at(self.spot - self.ahead) * 2 + self.core
        if far is not None:
            self.ssend, self.srecv, self.tsend, self.trecv = side_sems
            width = big.shape[1]
            self.owner = self.me * side // width == self.tp
            self.feature = pl.multiple_of(self.me * side % width, side)
            self.partner_feature = pl.multiple_of(self.partner * side % width, side)

    def block(self, step, mine):
        turn = self.ahead if mine else -self.ahead
        return self.chip_at(self.spot - turn * step) * 2 + (self.core if mine else 1 - self.core)

    def block_row(self, step, mine):
        return pl.multiple_of(self.block(step, mine) * self.rows, self.rows)

    def span(self, step, sub):
        return pl.ds(pl.multiple_of(self.block_row(step, True) + sub * self.part, self.part), self.part)

    def source(self, step, sub):
        if self.own is not None and isinstance(step, int) and step == 0:
            return self.own.at[pl.ds(sub * self.part, self.part)]
        return self.big.at[self.span(step, sub)]

    def ring_copy(self, step, sub):
        return pltpu.make_async_remote_copy(
            src_ref=self.source(step, sub), dst_ref=self.big.at[self.span(step, sub)],
            send_sem=self.send.at[step, sub], recv_sem=self.recv.at[step, sub],
            device_id={"tok": self.onward}, device_id_type=MESH,
        )

    def beside_copy(self, step, sub):
        return pltpu.make_async_remote_copy(
            src_ref=self.source(step, sub), dst_ref=self.big.at[self.span(step, sub)],
            send_sem=self.psend.at[step, sub], recv_sem=self.precv.at[step, sub],
            device_id={"tok": self.partner}, device_id_type=MESH,
        )

    def side_copy(self, step, sub, same):
        wanted, target = (self.feature, self.me) if same else (self.partner_feature, self.partner)
        out_sem, in_sem = (self.ssend, self.srecv) if same else (self.tsend, self.trecv)
        return pltpu.make_async_remote_copy(
            src_ref=self.source(step, sub).at[:, pl.ds(wanted, self.side)],
            dst_ref=self.far.at[self.span(step, sub), :],
            send_sem=out_sem.at[step, sub], recv_sem=in_sem.at[step, sub],
            device_id={"tok": target, "tp": 1 - self.tp}, device_id_type=MESH,
        )

    def launch(self, step, sub):
        if isinstance(step, int):
            if step < self.chips - 1:
                self.ring_copy(step, sub).start()
        else:
            @pl.when(step < self.chips - 1)
            def _():
                self.ring_copy(step, sub).start()
        self.beside_copy(step, sub).start()

    def launch_side(self, step, sub):
        @pl.when(self.owner)
        def _():
            for same in (True, False):
                self.side_copy(step, sub, same).start()

    def event(self, step, sub):
        self.ring_copy(step - 1, sub).wait_recv()
        self.launch(step, sub)

    def beside_arrived(self, step):
        for sub in range(self.subs):
            self.beside_copy(step, sub).wait_recv()

    def side_arrived(self, step, mine):
        @pl.when(jnp.logical_not(self.owner))
        def _():
            for sub in range(self.subs):
                self.side_copy(step, sub, mine).wait_recv()

    def drain(self, side_steps=0):
        for step in range(self.chips):
            for sub in range(self.subs):
                if step < self.chips - 1:
                    self.ring_copy(step, sub).wait_send()
                self.beside_copy(step, sub).wait_send()
                if step < side_steps:
                    @pl.when(self.owner)
                    def _():
                        for same in (True, False):
                            self.side_copy(step, sub, same).wait_send()


def greet(ring):
    barrier = pltpu.get_barrier_semaphore()
    for peer in (ring.onward, ring.back, ring.partner):
        pl.semaphore_signal(barrier, inc=1, device_id={"tok": peer}, device_id_type=MESH)
    for peer in (ring.me, ring.partner):
        pl.semaphore_signal(
            barrier, inc=1, device_id={"tok": peer, "tp": 1 - ring.tp}, device_id_type=MESH
        )
    pl.semaphore_wait(barrier, 5)


def cov_kernel(chips, x_ref, cin_ref, rin_ref, *refs):
    acc_ref, rsum_ref, big, far, lt, cbuf, rbuf, late = refs[:8]
    sems, side_sems = refs[8:12], refs[12:16]
    own_sem, cin_sem, rin_sem, lsend, lrecv, ones_r = refs[16:]
    ring = Ring(ring_place(chips), big, x_ref, COV_SUBS, sems, far, rin_ref.shape[1], side_sems)
    rows, width = x_ref.shape
    side = ring.side
    owner = ring.owner
    greet(ring)
    for sub in range(COV_SUBS):
        ring.launch(0, sub)
        ring.launch_side(0, sub)
    own = pltpu.make_async_copy(x_ref, big.at[pl.ds(pl.multiple_of(ring.me * rows, rows), rows)], own_sem.at[0])
    own.start()

    def slot_of(step, mine):
        return step % 2 * 2 + (0 if mine else 1)

    def fetch_cols(step, mine):
        slot = slot_of(step, mine)
        place = pl.ds(ring.block_row(step, mine), rows)
        return pltpu.make_async_copy(cin_ref.at[place, :], cbuf.at[slot], cin_sem.at[slot])

    def fetch_strip(step, mine):
        slot = slot_of(step, mine)
        place = pl.ds(ring.block_row(step, mine), rows)
        return pltpu.make_async_copy(rin_ref.at[place, :], rbuf.at[slot], rin_sem.at[slot])

    def late_copy(step, same):
        wanted, target = (ring.feature, ring.me) if same else (ring.partner_feature, ring.partner)
        slot = (step - SIDE_STEPS) * 2 + (0 if same else 1)
        return pltpu.make_async_remote_copy(
            src_ref=cin_ref.at[pl.ds(ring.block_row(step, True), rows), pl.ds(wanted, side)],
            dst_ref=late.at[slot], send_sem=lsend.at[slot], recv_sem=lrecv.at[slot],
            device_id={"tok": target, "tp": 1 - ring.tp}, device_id_type=MESH,
        )

    def start_fetch(step, mine):
        fetch_cols(step, mine).start()
        if step < SIDE_STEPS:
            @pl.when(jnp.logical_not(owner))
            def _():
                fetch_strip(step, mine).start()

    for step in range(2):
        for mine in (True, False):
            start_fetch(step, mine)

    ones_r[...] = jnp.ones_like(ones_r)
    lt[2 * side:, :] = jnp.ones((lt.shape[0] - 2 * side, rows), lt.dtype)
    acc_ref[...] = jnp.zeros_like(acc_ref)
    rsum_ref[...] = jnp.zeros_like(rsum_ref)
    own.wait()
    tile = min(1024, width)

    def work(step, mine):
        if not mine:
            ring.beside_arrived(step)
        ring.side_arrived(step, mine)
        slot = slot_of(step, mine)
        place = pl.ds(ring.block_row(step, mine), rows)
        fetch_cols(step, mine).wait()

        @pl.when(owner)
        def _():
            lt[0:side, :] = cbuf[slot, :, pl.ds(ring.feature, side)].T
            lt[side:2 * side, :] = big[place, pl.ds(ring.feature, side)].T

        @pl.when(jnp.logical_not(owner))
        def _():
            if step < SIDE_STEPS:
                fetch_strip(step, mine).wait()
                lt[0:side, :] = rbuf[slot].T
            else:
                late_copy(step, mine).wait_recv()
                lt[0:side, :] = late[(step - SIDE_STEPS) * 2 + (0 if mine else 1)].T
            lt[side:2 * side, :] = far[place, :].T

        rsum_ref[...] += jnp.dot(lt[0:2 * side, :], ones_r[...], preferred_element_type=jnp.float32)

        @pl.loop(0, width // tile)
        def _(i):
            here = pl.ds(pl.multiple_of(i * tile, tile), tile)
            acc_ref[:, here] += jnp.dot(
                lt[...], cbuf[slot, :, here], preferred_element_type=jnp.float32
            )
            there = pl.ds(pl.multiple_of(width + i * tile, tile), tile)
            acc_ref[:, there] += jnp.dot(
                lt[...], big[place, here], preferred_element_type=jnp.float32
            )

        if step + 2 < chips:
            start_fetch(step + 2, mine)

    for step in range(1, chips):
        for sub in range(COV_SUBS):
            ring.event(step, sub)
            ring.launch_side(step, sub)
            if sub == 0 and 1 <= step <= chips - SIDE_STEPS:
                @pl.when(owner)
                def _():
                    for same in (True, False):
                        late_copy(SIDE_STEPS + step - 1, same).start()
            if sub == COV_SUBS // 2 - 1:
                work(step - 1, True)
            if sub == (COV_SUBS // 2 if step == chips - 1 else COV_SUBS) - 1:
                work(step - 1, False)
    work(chips - 1, True)
    work(chips - 1, False)
    ring.drain(chips)

    @pl.when(owner)
    def _():
        for step in range(SIDE_STEPS, chips):
            for same in (True, False):
                late_copy(step, same).wait_send()


def finish_kernel(all_rows, strips, acc_ref, rsum_ref, x_ref, out_ref, y_ref):
    width = acc_ref.shape[1] // 2
    side = rsum_ref.shape[0] // 2
    tall = side // strips
    groups = 2 * width // 128
    part_of = 1.0 / all_rows
    y_ref[...] = x_ref[...]
    for row_source in range(2):
        for first in range(0, tall, 8):
            row = row_source * side + pl.program_id(0) * tall + first
            place = pl.ds(pl.multiple_of(row, 8), 8)
            mean_row = rsum_ref[place, :] * part_of
            pieces = []
            for j in range(width // 128):
                for source in range(2):
                    part = slice(source * width + j * 128, source * width + (j + 1) * 128)
                    mean_col = acc_ref[2 * side:2 * side + 1, part] * part_of
                    pieces.append(acc_ref[place, part] * part_of - mean_row * mean_col)
            turned = jnp.swapaxes(jnp.stack(pieces, axis=0), 0, 1)
            out_ref[row_source, first * groups:(first + 8) * groups, :] = turned.reshape(8 * groups, 128)


def joint_cov(hidden_out, rows_in, cols_in, call_id):
    rows, width = hidden_out.shape
    all_rows, side = cols_in.shape[0], rows_in.shape[1]
    chips = all_rows // rows // 2
    dma = pltpu.SemaphoreType.DMA
    tall = 2 * side + 16
    acc, rsum = pl.pallas_call(
        functools.partial(cov_kernel, chips),
        out_shape=[
            jax.ShapeDtypeStruct((tall, 2 * width), jnp.float32),
            jax.ShapeDtypeStruct((2 * side, 128), jnp.float32),
        ],
        in_specs=[pl.BlockSpec(memory_space=pltpu.VMEM)]
        + [pl.BlockSpec(memory_space=pl.ANY)] * 2,
        out_specs=[pl.BlockSpec(memory_space=pltpu.VMEM)] * 2,
        scratch_shapes=[
            pltpu.VMEM((all_rows, width), jnp.bfloat16),
            pltpu.VMEM((all_rows, side), jnp.bfloat16),
            pltpu.VMEM((tall, rows), jnp.bfloat16),
            pltpu.VMEM((4, rows, width), jnp.bfloat16),
            pltpu.VMEM((4, rows, side), jnp.bfloat16),
            pltpu.VMEM((2 * (chips - SIDE_STEPS), rows, side), jnp.bfloat16),
        ]
        + [dma((chips, COV_SUBS))] * 8
        + [dma((1,)), dma((4,)), dma((4,))]
        + [dma((2 * (chips - SIDE_STEPS),))] * 2
        + [pltpu.VMEM((rows, 128), jnp.bfloat16)],
        compiler_params=pltpu.CompilerParams(
            collective_id=call_id, has_side_effects=True, vmem_limit_bytes=38 * 1024 * 1024
        ),
        cost_estimate=pl.CostEstimate(
            flops=8 * all_rows * side * width * 4,
            bytes_accessed=4 * all_rows * (side + width) + 16 * side * width,
            transcendentals=0,
        ),
        name="cov_ring",
    )(hidden_out, cols_in, rows_in)
    cov, settled = finish(acc, rsum, hidden_out, side)
    return settled, cov


def finish(acc, rsum, hidden_out, side):
    rows, width = hidden_out.shape
    all_rows = rows * lax.axis_size("tok")
    strips = 8
    tall = side // strips
    groups = 2 * width // 128
    cov, settled = pl.pallas_call(
        functools.partial(finish_kernel, all_rows, strips),
        out_shape=[
            jax.ShapeDtypeStruct((2, side * groups, 128), jnp.float32),
            jax.ShapeDtypeStruct(hidden_out.shape, hidden_out.dtype),
        ],
        grid=(strips,),
        in_specs=[
            pl.BlockSpec(memory_space=pltpu.VMEM),
            pl.BlockSpec(memory_space=pltpu.VMEM),
            pl.BlockSpec((rows // strips, width), lambda i: (i, 0)),
        ],
        out_specs=[
            pl.BlockSpec((2, tall * groups, 128), lambda i: (0, i, 0)),
            pl.BlockSpec((rows // strips, width), lambda i: (i, 0)),
        ],
        compiler_params=pltpu.CompilerParams(
            dimension_semantics=("arbitrary",), vmem_limit_bytes=8 * 1024 * 1024
        ),
        name="finish",
    )(acc, rsum, hidden_out)
    cov = cov.reshape(2, side, width // 128, 2, 128).transpose(0, 1, 3, 2, 4)
    return cov.reshape(2, side, 2, width), settled


NEG = -1e30


def front_kernel(
    chips, kv_heads, groups, x_ref, gain_ref, cos_ref, sin_ref, kdoc_ref,
    wq_ref, wk_ref, wv_ref, wo_ref, out_ref, cin, far, other, normed, wkv, wq, wo, kv, q_ref,
    m_ref, l_ref, acc_ref, att, mine_sum, sent, arrived, bias, qdoc_ref, *sems
):
    place = ring_place(chips)
    hid_sems, side_sems, kv_sems = sems[0:4], sems[4:8], sems[8:12]
    xsend, xrecv, osend, orecv, own_sem, wkv_sem, wq_sem, wo_sem = sems[12:]
    rows, width = x_ref.shape
    side = far.shape[1]
    hid = Ring(place, cin, x_ref, SUBS, hid_sems, far, side, side_sems)
    ring = Ring(place, kv, None, SUBS, kv_sems)
    me, tp = hid.me, hid.tp
    half = rows // SUBS
    kv_width = kv_heads * HS
    scale = HS ** (-0.5) * math.log2(math.e)
    head_pair = 2 * HS
    q_tiles = kv_heads * groups // 2
    out_tile = width // 4

    def swap(sub):
        part = pl.ds(sub * half, half)
        return pltpu.make_async_remote_copy(
            src_ref=x_ref.at[part], dst_ref=other.at[part], send_sem=xsend.at[sub],
            recv_sem=xrecv.at[sub], device_id={"tp": 1 - tp}, device_id_type=MESH,
        )

    def fetch_q(t):
        col = pl.ds(pl.multiple_of(t * head_pair, head_pair), head_pair)
        return pltpu.make_async_copy(wq_ref.at[:, col], wq.at[t % 4], wq_sem.at[t % 4])

    def fetch_out(side_tp, i):
        col = pl.ds(pl.multiple_of(side_tp * width + i * out_tile, out_tile), out_tile)
        return pltpu.make_async_copy(wo_ref.at[:, col], wo.at[i], wo_sem.at[i])

    def out_part(i):
        return pl.ds(pl.multiple_of(i * out_tile, out_tile), out_tile)

    def give(i):
        return pltpu.make_async_remote_copy(
            src_ref=sent.at[:, out_part(i)], dst_ref=arrived.at[:, out_part(i)],
            send_sem=osend.at[i], recv_sem=orecv.at[i],
            device_id={"tp": 1 - tp}, device_id_type=MESH,
        )

    keys = [
        pltpu.make_async_copy(ref, wkv.at[:, pl.ds(i * kv_width, kv_width)], wkv_sem.at[i])
        for i, ref in enumerate((wk_ref, wv_ref))
    ]
    for copy in keys:
        copy.start()
    greet(hid)
    for sub in range(SUBS):
        swap(sub).start()
        hid.launch(0, sub)
    own = pltpu.make_async_copy(x_ref, cin.at[pl.ds(pl.multiple_of(me * rows, rows), rows)], own_sem.at[0])
    own.start()
    for t in range(4):
        fetch_q(t).start()
    for i in range(4):
        fetch_out(1 - tp, i).start()

    @pl.loop(0, kv_heads)
    def _(g):
        m_ref[g] = jnp.full(m_ref.shape[1:], NEG, jnp.float32)
        l_ref[g] = jnp.zeros(l_ref.shape[1:], jnp.float32)
        acc_ref[g] = jnp.zeros(acc_ref.shape[1:], jnp.float32)

    my_doc = kdoc_ref[:, pl.ds(pl.multiple_of(me * rows, rows), rows)]
    qdoc_ref[...] = jnp.broadcast_to(my_doc, (128, rows)).T
    my_cols = pl.ds(pl.multiple_of(tp * width, width), width)
    other_cols = pl.ds(pl.multiple_of((1 - tp) * width, width), width)

    def normalise(sub):
        @pl.loop(0, half // 32)
        def _(r):
            part = pl.ds(pl.multiple_of(sub * half + r * 32, 32), 32)
            near = x_ref[part, :].astype(jnp.float32)
            away = other[part, :].astype(jnp.float32)
            total = jnp.sum(near * near, axis=1, keepdims=True) + jnp.sum(away * away, axis=1, keepdims=True)
            factor = lax.rsqrt(total / (2 * width) + epsilon)
            normed[part, my_cols] = (near * factor * gain_ref[:, my_cols]).astype(jnp.bfloat16)
            normed[part, other_cols] = (away * factor * gain_ref[:, other_cols]).astype(jnp.bfloat16)

    def turned(vectors):
        return vectors * cos_ref[...] + pltpu.roll(vectors, HS // 2, 1) * sin_ref[...]

    hid.event(1, 0)
    hid.event(1, 1)
    swap(0).wait_recv()
    normalise(0)
    hid.event(2, 0)
    hid.event(2, 1)
    swap(1).wait_recv()
    normalise(1)
    for copy in keys:
        copy.wait()
    my_base = pl.multiple_of(me * 2 * kv_width, 2 * kv_width)

    @pl.loop(0, kv_width // head_pair)
    def _(t):
        col = pl.multiple_of(t * head_pair, head_pair)
        found = jnp.dot(normed[...], wkv[:, pl.ds(col, head_pair)], preferred_element_type=jnp.float32)
        for j in range(2):
            piece = turned(found[:, j * HS:(j + 1) * HS])
            kv[pl.ds(pl.multiple_of(my_base + col + j * HS, HS), HS), :] = piece.T.astype(jnp.bfloat16)


    @pl.loop(0, kv_width // head_pair)
    def _(t):
        col = pl.multiple_of(kv_width + t * head_pair, head_pair)
        found = jnp.dot(normed[...], wkv[:, pl.ds(col, head_pair)], preferred_element_type=jnp.float32)
        kv[pl.ds(pl.multiple_of(my_base + col, head_pair), rows), :] = found.astype(jnp.bfloat16)

        @pl.when(t == 0)
        def _():
            ring.launch(0, 0)

    ring.launch(0, 1)
    for step in range(3):
        for sub in range(SUBS):
            hid.launch_side(step, sub)

    @pl.loop(0, q_tiles)
    def _(t):
        fetch_q(t).wait()
        found = jnp.dot(normed[...], wq[t % 4], preferred_element_type=jnp.float32)
        for j in range(2):
            head = t * 2 + j
            row = pl.multiple_of(head % groups * rows, rows)
            q_ref[head // groups, pl.ds(row, rows), :] = turned(found[:, j * HS:(j + 1) * HS]).astype(jnp.bfloat16)

        @pl.when(t + 4 < q_tiles)
        def _():
            fetch_q(t + 4).start()

        @pl.when(t == q_tiles // 2)
        def _():
            ring.event(1, 0)

    ring.event(1, 1)

    def make_bias(blocks):
        for i, block in enumerate(blocks):
            row = pl.multiple_of(block * rows, rows)
            key_pos = row + lax.broadcasted_iota(jnp.int32, (rows, rows), 1)
            query_pos = me * rows + lax.broadcasted_iota(jnp.int32, (rows, rows), 0)
            allowed = (kdoc_ref[:, pl.ds(row, rows)] == qdoc_ref[:, :1]) & (key_pos <= query_pos)
            bias[:, i * rows:(i + 1) * rows] = jnp.where(allowed, 0.0, NEG)

    def pair_attention(blocks, heads):
        @pl.loop(*heads)
        def _(g):
            k_row, v_row = g * HS, kv_width + g // 2 * rows
            v_col = pl.ds(pl.multiple_of(g % 2 * HS, HS), HS)
            k = jnp.concatenate(
                [kv[pl.ds(pl.multiple_of(b * 2 * kv_width + k_row, HS), HS), :] for b in blocks], axis=1
            )
            v = jnp.concatenate(
                [kv[pl.ds(pl.multiple_of(b * 2 * kv_width + v_row, rows), rows), v_col] for b in blocks],
                axis=0,
            )
            for head in range(groups):
                part = pl.ds(head * rows, rows)
                s = jnp.dot(q_ref[g, part, :], k, preferred_element_type=jnp.float32) * scale + bias[...]
                old = m_ref[g, part, :]
                pieces = [s[:, i:i + 128] for i in range(0, 2 * rows, 128)]
                peak = functools.reduce(jnp.maximum, pieces)
                top = jnp.maximum(old, jnp.max(peak, axis=-1, keepdims=True))
                fade = jnp.exp2(old - top)
                weights = [jnp.exp2(piece - top) for piece in pieces]
                l_ref[g, part, :] = l_ref[g, part, :] * fade + functools.reduce(jnp.add, weights)
                m_ref[g, part, :] = top
                acc_ref[g, part, :] = acc_ref[g, part, :] * fade + jnp.dot(
                    jnp.concatenate(weights, axis=1).astype(jnp.bfloat16), v,
                    preferred_element_type=jnp.float32,
                )

    @pl.loop(0, chips * SUBS)
    def _(turn):
        step, sub = turn // SUBS, turn % SUBS

        @pl.when(step + 2 < chips)
        def _():
            ring.event(step + 2, sub)


        @pl.when((step + 2 == chips - 2) & (sub == 1))
        def _():
            for part in range(SUBS):
                hid.event(3, part)
                hid.launch_side(3, part)

        @pl.when(step + 2 == chips + 1)
        def _():
            hid.event(4, sub)
            hid.launch_side(4, sub)

        blocks = (ring.block(step, True), ring.block(step, False))
        needed = (blocks[0] <= me) | (blocks[1] <= me)

        @pl.when(sub == 0)
        def _():
            ring.beside_arrived(step)

        @pl.when((sub == 0) & needed)
        def _():
            make_bias(blocks)

        @pl.when(needed)
        def _():
            pair_attention(blocks, (sub * (kv_heads // SUBS), (sub + 1) * (kv_heads // SUBS)))

    @pl.loop(0, kv_heads)
    def _(g):
        for head in range(groups):
            part = pl.ds(head * rows, rows)
            weight_sum = jnp.sum(l_ref[g, part, :], axis=-1, keepdims=True)
            col = pl.ds(pl.multiple_of((g * groups + head) * HS, HS), HS)
            att[:, col] = (acc_ref[g, part, :] / weight_sum).astype(jnp.bfloat16)

    @pl.loop(0, 4)
    def _(i):
        fetch_out(1 - tp, i).wait()
        found = jnp.dot(att[...], wo[i], preferred_element_type=jnp.float32)
        sent[:, out_part(i)] = found.astype(jnp.bfloat16)

        @pl.when(i > 0)
        def _():
            give(i - 1).start()

        fetch_out(tp, i).start()

    give(3).start()
    for i in range(2):
        hid.event(5, i)
        hid.launch_side(5, i)
    hid.event(6, 0)

    @pl.loop(0, 4)
    def _(i):
        fetch_out(tp, i).wait()
        mine_sum[:, out_part(i)] = jnp.dot(att[...], wo[i], preferred_element_type=jnp.float32)

    hid.event(6, 1)

    def settle(i):
        give(i).wait_recv()
        summed = mine_sum[:, out_part(i)] + arrived[:, out_part(i)].astype(jnp.float32)
        out_ref[:, out_part(i)] = (x_ref[:, out_part(i)].astype(jnp.float32) + summed).astype(jnp.bfloat16)

    pl.loop(0, 4)(settle)
    for sub in range(SUBS):
        hid.event(7, sub)
    own.wait()
    for step in range(chips):
        hid.beside_arrived(step)
        if step < SIDE_STEPS:
            for mine in (True, False):
                hid.side_arrived(step, mine)
    hid.drain(SIDE_STEPS)
    ring.drain()
    for sub in range(SUBS):
        swap(sub).wait_send()
    for i in range(4):
        give(i).wait_send()


def front(hidden_in, norm_gain, cosine, sine, doc_ids, w_query, w_key, w_value, w_out, call_id):
    rows, width = hidden_in.shape
    all_rows = doc_ids.shape[1]
    chips = all_rows // rows // 2
    side = width * 2 // (2 * chips)
    kv_heads = w_key.shape[1] // HS
    groups = w_query.shape[1] // w_key.shape[1]
    dma = pltpu.SemaphoreType.DMA
    bf16, f32 = jnp.bfloat16, jnp.float32
    stacked = (kv_heads, groups * rows, HS)
    return pl.pallas_call(
        functools.partial(front_kernel, chips, kv_heads, groups),
        out_shape=[
            jax.ShapeDtypeStruct((rows, width), bf16),
            jax.ShapeDtypeStruct((all_rows, width), bf16),
            jax.ShapeDtypeStruct((8 * all_rows, side), bf16),
        ],
        in_specs=[pl.BlockSpec(memory_space=pltpu.VMEM)] * 5 + [pl.BlockSpec(memory_space=pl.ANY)] * 4,
        out_specs=[pl.BlockSpec(memory_space=pltpu.VMEM)] + [pl.BlockSpec(memory_space=pl.ANY)] * 2,
        scratch_shapes=[
            pltpu.VMEM((rows, width), bf16),
            pltpu.VMEM((rows, 2 * width), bf16),
            pltpu.VMEM((2 * width, 2 * w_key.shape[1]), bf16),
            pltpu.VMEM((4, 2 * width, 2 * HS), bf16),
            pltpu.VMEM((4, w_out.shape[0], width // 4), bf16),
            pltpu.VMEM((all_rows // rows * 2 * w_key.shape[1], rows), bf16),
            pltpu.VMEM(stacked, bf16),
            pltpu.VMEM(stacked, f32),
            pltpu.VMEM(stacked, f32),
            pltpu.VMEM(stacked, f32),
            pltpu.VMEM((rows, w_out.shape[0]), bf16),
            pltpu.VMEM((rows, width), f32),
            pltpu.VMEM((rows, width), bf16),
            pltpu.VMEM((rows, width), bf16),
            pltpu.VMEM((rows, 2 * rows), f32),
            pltpu.VMEM((rows, 128), jnp.int32),
        ]
        + [dma((chips, SUBS))] * 12
        + [dma((SUBS,))] * 2
        + [dma((4,))] * 2
        + [dma((1,)), dma((2,)), dma((4,)), dma((4,))],
        compiler_params=pltpu.CompilerParams(
            collective_id=call_id, has_side_effects=True, vmem_limit_bytes=52 * 1024 * 1024
        ),
        name="front",
    )(hidden_in, norm_gain, cosine, sine, doc_ids, w_query, w_key, w_value, w_out)


def on_pairs(hidden_in, norm_gain, w_query, w_key, w_value, w_out, doc_ids):
    rows = hidden_in.shape[0]
    first_row = lax.axis_index("tok") * rows
    positions = (first_row + jnp.arange(rows, dtype=jnp.int32)) % doc_ids.shape[0]
    lane = jnp.arange(HS, dtype=jnp.int32)
    pair = (lane % (HS // 2)).astype(jnp.float32)
    inv_freq = rope_base ** (-(pair * 2.0) / HS)
    angles = positions.astype(jnp.float32)[:, None] * inv_freq[None, :]
    sine = jnp.sin(angles) * jnp.where(lane < HS // 2, -1.0, 1.0)[None, :]
    hidden_out, cols_in, rows_in = front(
        hidden_in, norm_gain[None, :], jnp.cos(angles), sine, doc_ids[None, :],
        w_query, w_key, w_value, w_out, 0,
    )
    return joint_cov(hidden_out, rows_in, cols_in, 1)


def on_device(hidden_in, norm_gain, w_query, w_key, w_value, w_out, doc_ids):
    tok_rows, col_width = hidden_in.shape
    tok_count = lax.axis_size("tok")
    tp_count = lax.axis_size("tp")
    if tp_count == 2 and tok_rows == 2 * HS and w_key.shape[1] % (2 * HS) == 0:
        return on_pairs(hidden_in, norm_gain, w_query, w_key, w_value, w_out, doc_ids)
    tok_index = lax.axis_index("tok")
    all_rows = tok_rows * tok_count
    full_in = both_sides(hidden_in)
    widened = full_in.astype(jnp.float32)
    factor = lax.rsqrt(jnp.mean(widened * widened, axis=1, keepdims=True) + epsilon)
    normed = (widened * factor * norm_gain[None, :]).astype(jnp.bfloat16)
    kv_heads = w_key.shape[1] // HS
    groups = w_query.shape[1] // w_key.shape[1]
    first_row = tok_index * tok_rows
    positions = first_row + jnp.arange(tok_rows, dtype=jnp.int32)
    key_local = rotate(
        jnp.dot(normed, w_key, preferred_element_type=jnp.float32).reshape(tok_rows, kv_heads, HS),
        positions % all_rows,
    )
    key_local = key_local.astype(jnp.bfloat16).reshape(tok_rows, kv_heads * HS)
    value_local = jnp.dot(normed, w_value, preferred_element_type=jnp.float32).astype(jnp.bfloat16)
    (kv_rows,) = ring_gather(jnp.stack([key_local, value_local]), False, 0)
    early, late = hidden_in[:, : col_width // 2], hidden_in[:, col_width // 2 :]
    late, kv_rows = lax.optimization_barrier((late, kv_rows))
    cols_in = [lax.all_gather(part, "tok", axis=0, tiled=True) for part in (early, late)]
    rows_in = lax.all_to_all(full_in, "tok", 1, 0, tiled=True)
    queries = rotate(
        jnp.dot(normed, w_query, preferred_element_type=jnp.float32).reshape(
            tok_rows, kv_heads * groups, HS
        ),
        positions % all_rows,
    )
    queries = queries.astype(jnp.bfloat16).reshape(tok_rows, kv_heads * groups * HS)
    query_doc = lax.dynamic_slice_in_dim(doc_ids, first_row, tok_rows, 0)
    lo = jnp.sum((doc_ids[None, :] < query_doc[:, None]).astype(jnp.int32), axis=1)
    bounds = jnp.stack([first_row.astype(jnp.int32), lo[0]])
    attended = attend(queries, kv_rows, jnp.broadcast_to(lo[:, None], (tok_rows, 128)), bounds, kv_heads)
    partial_out = jnp.dot(attended, w_out, preferred_element_type=jnp.float32)
    summed = lax.psum_scatter(partial_out, "tp", scatter_dimension=1, tiled=True)
    hidden_out = (hidden_in.astype(jnp.float32) + summed).astype(jnp.bfloat16)
    halves = jnp.stack([hidden_out[:, : col_width // 2], hidden_out[:, col_width // 2 :]])
    (cols_out,) = ring_gather(halves, False, 1)
    rows_out = row_features(cols_out, None)
    return (hidden_out, joint_gram(rows_in, rows_out, cols_in, cols_out))


def solution(mesh):
    return jax.shard_map(
        on_device,
        mesh=mesh,
        in_specs=(
            P("tok", "tp"),
            P(),
            P(None, "tp"),
            P(None, "tp"),
            P(None, "tp"),
            P("tp", None),
            P(),
        ),
        out_specs=(P("tok", "tp"), P(None, "tok", None, "tp")),
        check_vma=False,
    )
```
